128 devices in a mesh: grp: 4 (over y_hi, core), req: 32 (over x, z, y_lo).
Axes of the slice: x: 4, y: 4 (y_hi: 2, y_lo: 2; y = y_hi * 2 + y_lo), z: 4, core: 2. Of those that a mesh axis runs over, the one named last changes fastest.
Arguments:
- tokens: bfloat16 [16384, 1024], P(('grp', 'req')), may hold values from -6 to 6
- attn_gain: float32 [1024], replicated, may hold values from 0.1 to 1.9
- w_query: bfloat16 [1024, 1024], replicated, may hold values from -0.0234375 to 0.0234375
- w_key: bfloat16 [1024, 1024], replicated, may hold values from -0.1875 to 0.1875
- w_value: bfloat16 [1024, 1024], replicated, may hold values from -0.1875 to 0.1875
- w_attn_out: bfloat16 [1024, 1024], replicated, may hold values from -0.1875 to 0.1875
- rel_bias: float32 [32, 16], replicated, may hold values from -4 to 4
- prefix_cache: bfloat16 [8, 512, 2048], P('grp', 'req'), may hold values from -6 to 6
- lengths: int32 [4, 64], P('grp'), may hold values from 1 to 128, 4096 in all within a row
- prefix_map: int32 [4, 64], P('grp'), may hold values from 0 to 1
- mlp_gain: float32 [1024], replicated, may hold values from 0.1 to 1.9
- w_in: bfloat16 [4096, 1024], P('grp'), may hold values from -0.1875 to 0.1875
- w_out: bfloat16 [4096, 1024], P('grp'), may hold values from -0.09375 to 0.09375
Outputs:
- layer_out: bfloat16 [16384, 1024], P(('grp', 'req'))
The draws below stay inside these ranges and needn't reach their ends.
Inputs may be any that keep to these rules, and one draw needn't show every extreme that they name: In each group the lengths sum to 4096 and the longest is exactly 128.
All inputs are finite; a program needn't handle non-finite values.
Results may differ from the reference program's by a relative error of at most 0.017.
Values may be sent and summed in bfloat16 or wider, within the bound.
No kernel may reach another device: no remote copies, remote signals or barrier semaphores. Data moves between devices by JAX's collectives and lax.ppermute only.
A program may use at most 128 MiB of HBM per device.

```python
import math
import jax
import jax.numpy as jnp
import numpy as np
from jax import lax

D = 1024
H = 16
DK = 64
FF = 4096
BUCKETS = 32
PLEN = 512
PREF_GRP = 2
TOK_DEV = 128
TOK_GRP = 4096
TOKENS = 16384
REQ_GRP = 64
PREFIXES = 8
N_GRP = 4
N_REQ = 32


def shared_pattern(key):
    base = jax.random.fold_in(key, 7301)
    signs = (2 * jax.random.randint(jax.random.fold_in(base, 1), (D,), 0, 2) - 1).astype(jnp.float32)
    features = jax.random.permutation(jax.random.fold_in(base, 2), D)[:2].astype(jnp.int32)
    return (signs, features)


def draw_w_query(key, part):
    signs, features = shared_pattern(key)
    spread = 1.0 / math.sqrt(D * DK)
    limit = 6.0 * spread
    own = jax.random.fold_in(key, 11)
    drawn = jax.random.normal(own, (D, D), jnp.float32) * spread
    drawn = jnp.clip(drawn, -limit, limit)
    row_ids = jnp.arange(D, dtype=jnp.int32)
    marked = jnp.any(row_ids[:, None] == features[None, :], axis=1)
    return jnp.where(marked[:, None], limit * signs[None, :], drawn).astype(jnp.bfloat16)


def draw_tokens(key, part):
    signs, features = shared_pattern(key)
    own = jax.random.fold_in(key, 23)
    drawn = jnp.clip(jax.random.normal(own, (TOKENS, D), jnp.float32), -6.0, 6.0)
    quiet = jnp.clip(jax.random.normal(jax.random.fold_in(key, 31), (TOKENS, D), jnp.float32), -4.0, 4.0)
    columns = jnp.arange(D, dtype=jnp.int32)
    feature_col = (columns == features[0]) | (columns == features[1])
    drawn = jnp.where(feature_col[None, :], 0.1 * drawn, drawn)
    blocks = TOKENS // TOK_DEV
    spot = jax.random.randint(jax.random.fold_in(key, 29), (blocks,), 0, TOK_DEV)
    row_ids = jnp.arange(TOKENS, dtype=jnp.int32)
    block_of = row_ids // TOK_DEV
    is_spike = row_ids - block_of * TOK_DEV == spot[block_of]
    noise_level = jnp.array([0.05, 0.2, 0.35], jnp.float32)[block_of % 3]
    spike_rows = jnp.where(feature_col[None, :], 6.0, quiet * noise_level[:, None])
    return jnp.where(is_spike[:, None], spike_rows, drawn).astype(jnp.bfloat16)


def draw_prefix_cache(key, part):
    signs, features = shared_pattern(key)
    own = jax.random.fold_in(key, 41)
    drawn = jnp.clip(jax.random.normal(own, (PREFIXES, PLEN, 2 * D), jnp.float32), -6.0, 6.0)
    reach = max(PLEN - 128, PLEN // 2)
    first = jax.random.randint(jax.random.fold_in(key, 43), (PREFIXES,), 0, reach)
    second = (first + 1 + jax.random.randint(jax.random.fold_in(key, 47), (PREFIXES,), 0, reach - 1)) % reach
    positions = jnp.arange(PLEN, dtype=jnp.int32)
    columns = jnp.arange(2 * D, dtype=jnp.int32)
    key_col = columns < D
    dip = (columns % DK == 0) & key_col
    sign_full = jnp.concatenate([signs, jnp.zeros((D,), jnp.float32)])
    first_vals = 6.0 * sign_full
    second_vals = jnp.where(dip, 4.25, 6.0) * sign_full
    at_first = (positions[None, :] == first[:, None])[:, :, None] & key_col[None, None, :]
    at_second = (positions[None, :] == second[:, None])[:, :, None] & key_col[None, None, :]
    out = jnp.where(at_first, first_vals[None, None, :], drawn)
    return jnp.where(at_second, second_vals[None, None, :], out).astype(jnp.bfloat16)


def touch_ends(values, own_key, smallest, largest):
    dims = values.shape
    index_at = [jax.random.randint(jax.random.fold_in(own_key, axis), (), 0, dims[axis]) for axis in range(len(dims))]
    values = values.at[tuple(index_at)].set(smallest)
    longest = dims.index(max(dims))
    index_at[longest] = (index_at[longest] + 1) % dims[longest]
    return values.at[tuple(index_at)].set(largest)


def block_scale(rng, dims, split, low, high):
    level = 1.0
    for axis_at, blocks in split:
        draws = jax.random.uniform(jax.random.fold_in(jax.random.fold_in(rng, 6), axis_at), (blocks,), jnp.float32, low / len(split), high / len(split))
        level = level * jnp.repeat(jnp.exp(draws), dims[axis_at] // blocks).reshape((-1,) + (1,) * (len(dims) - 1 - axis_at))
    return level


def length_profile(number_of, total, bound, skew):
    weights = [(1 << 20) // math.isqrt(standing ** skew) + 1 for standing in range(2, number_of + 1)]
    spare, counts = total - bound - (number_of - 1), [1] * (number_of - 1)
    while spare > 0:
        movable = [i for i in range(number_of - 1) if counts[i] < bound]
        pool, remaining = sum([weights[i] for i in movable]), spare
        for i in movable:
            extra = min(bound - counts[i], max(1, remaining * weights[i] // pool), spare)
            counts[i] = counts[i] + extra
            spare = spare - extra
    return np.array([bound] + counts)


def uneven(stream_key, number_of, total, most, slope):
    if number_of == 2:
        one = jax.random.randint(stream_key, (), max(1, total - most), min(most, total - 1) + 1)
        return jnp.stack([one, total - one])
    sizes = jnp.asarray(length_profile(number_of, total, most, slope), jnp.int32)
    twos = (number_of - 1) // 2
    giver, taker = sizes[1:1 + 2 * twos:2], sizes[2:2 + 2 * twos:2]
    room = jnp.minimum(giver - 1, most - taker)
    shifted = jax.random.randint(jax.random.fold_in(stream_key, 1), (twos,), 0, 1 << 20) % (room + 1)
    sizes = sizes.at[1:1 + 2 * twos:2].set(giver - shifted).at[2:2 + 2 * twos:2].set(taker + shifted)
    return sizes[jax.random.permutation(jax.random.fold_in(stream_key, 2), number_of)]


def centred(key, shape, scale, most, shards=(), kind=jnp.bfloat16):
    entries = jax.random.normal(key, shape, jnp.float32) * scale
    if len(shards) > 0:
        entries = block_scale(key, shape, shards, -0.22, 0.18) * entries
    return jnp.clip(entries, min=-most, max=most).astype(kind)


def setup_inputs(seed: int = 0) -> dict:
    splits = jax.random.split(jax.random.key(seed), 14)
    return {
        "tokens": draw_tokens(jax.random.fold_in(splits[13], 71), 0),
        "attn_gain": jnp.clip(1.0 + 0.18 * jax.random.normal(splits[1], (D,), jnp.float32), 0.1, 1.9),
        "w_query": draw_w_query(jax.random.fold_in(splits[13], 71), 0),
        "w_key": centred(splits[3], (D, D), D ** -0.5, 0.1875),
        "w_value": centred(splits[4], (D, D), D ** -0.5, 0.1875),
        "w_attn_out": centred(splits[5], (D, D), D ** -0.5, 0.1875),
        "rel_bias": centred(splits[6], (BUCKETS, H), 1.0, 4.0, (), jnp.float32),
        "prefix_cache": draw_prefix_cache(jax.random.fold_in(splits[13], 71), 0),
        "lengths": jax.vmap(lambda own: uneven(own, REQ_GRP, TOK_GRP, TOK_DEV, 2))(jax.random.split(splits[8], N_GRP)).reshape((N_GRP, REQ_GRP)).astype(jnp.int32),
        "prefix_map": touch_ends(jax.random.randint(splits[9], (N_GRP, REQ_GRP), 0, PREF_GRP), jax.random.fold_in(splits[9], 1), 0, PREF_GRP - 1).astype(jnp.int32),
        "mlp_gain": jnp.clip(1.0 + 0.18 * jax.random.normal(splits[10], (D,), jnp.float32), 0.1, 1.9),
        "w_in": centred(splits[11], (FF, D), D ** -0.5, 0.1875, ((0, 4),)),
        "w_out": centred(splits[12], (FF, D), FF ** -0.5, 0.09375, ((0, 4),)),
    }


epsilon = 1e-06
far_marks = (12, 16, 23, 32, 46, 64, 91)
masked_score = -1e+30

def bucket_of(relative):
    distance = jnp.abs(relative)
    far_bucket = 8 + sum([(distance >= threshold).astype(jnp.int32) for threshold in far_marks])
    bucket = jnp.where(distance < 8, distance, far_bucket)
    return (bucket + jnp.where(relative > 0, 16, 0)).astype(jnp.int32)

def norm_rows(values_in, gain):
    widened = values_in.astype(jnp.float32)
    scale = lax.rsqrt(lax.optimization_barrier(jnp.mean(widened * widened, axis=-1, keepdims=True)) + epsilon)
    return (widened * scale * gain).astype(jnp.bfloat16)

def layout(lengths_row, prefix_row, row_ids):
    req_ends = jnp.cumsum(lengths_row).astype(jnp.int32)
    req_starts = (req_ends - lengths_row).astype(jnp.int32)
    member = ((row_ids[:, None] >= req_starts[None, :]) & (row_ids[:, None] < req_ends[None, :])).astype(jnp.int32)
    numbers = jnp.arange(lengths_row.shape[0], dtype=jnp.int32)
    req_index = (lax.optimization_barrier(jnp.sum(member * numbers[None, :], axis=1)) + lax.optimization_barrier(jnp.sum(member, axis=1)) - 1).astype(jnp.int32)
    offset = (row_ids - lax.optimization_barrier(jnp.sum(member * req_starts[None, :], axis=1))).astype(jnp.int32)
    chosen = lax.optimization_barrier(jnp.sum(member * prefix_row[None, :], axis=1)).astype(jnp.int32)
    return (req_index, offset, chosen)

def reference(tokens, attn_gain, w_query, w_key, w_value, w_attn_out, rel_bias, prefix_cache, lengths, prefix_map, mlp_gain, w_in, w_out):
    bias_table = rel_bias.T
    results = []
    for group_idx in range(N_GRP):
        group_rows = tokens[group_idx * TOK_GRP:(group_idx + 1) * TOK_GRP]
        normed = norm_rows(group_rows, attn_gain)
        query = jnp.dot(normed, w_query, preferred_element_type=jnp.float32).astype(jnp.bfloat16)
        key_proj = jnp.dot(normed, w_key, preferred_element_type=jnp.float32).astype(jnp.bfloat16)
        value_proj = jnp.dot(normed, w_value, preferred_element_type=jnp.float32).astype(jnp.bfloat16)
        pad_rows = jnp.zeros((TOK_DEV, D), jnp.bfloat16)
        key_padded = jnp.concatenate([pad_rows, key_proj, pad_rows], axis=0)
        value_padded = jnp.concatenate([pad_rows, value_proj, pad_rows], axis=0)
        cache = prefix_cache[group_idx * PREF_GRP:(group_idx + 1) * PREF_GRP].astype(jnp.float32)
        cache_keys = cache[:, :, :D].reshape(PREF_GRP * PLEN, H, DK)
        cache_values = cache[:, :, D:].reshape(PREF_GRP * PLEN, H, DK)
        group_lengths = lengths[group_idx]
        group_map = prefix_map[group_idx]

        def attend(block_idx):
            row_first = block_idx * TOK_DEV
            query_ids = row_first + jnp.arange(TOK_DEV, dtype=jnp.int32)
            window_ids = row_first - TOK_DEV + jnp.arange(3 * TOK_DEV, dtype=jnp.int32)
            query_req, query_offset, query_prefix = layout(group_lengths, group_map, query_ids)
            window_req = layout(group_lengths, group_map, window_ids)[0]
            query_block = lax.dynamic_slice_in_dim(query, row_first, TOK_DEV, 0).astype(jnp.float32).reshape(TOK_DEV, H, DK)
            key_window = lax.dynamic_slice_in_dim(key_padded, row_first, 3 * TOK_DEV, 0).astype(jnp.float32).reshape(3 * TOK_DEV, H, DK)
            value_window = lax.dynamic_slice_in_dim(value_padded, row_first, 3 * TOK_DEV, 0).astype(jnp.float32).reshape(3 * TOK_DEV, H, DK)
            positions = jnp.arange(PLEN, dtype=jnp.int32)
            prefix_terms = jnp.take(bias_table, bucket_of(positions[None, :] - PLEN - query_offset[:, None]), axis=1)
            prefix_terms = jnp.tile(prefix_terms, (1, 1, PREF_GRP))
            prefix_allowed = jnp.repeat(query_prefix[:, None] == jnp.arange(PREF_GRP, dtype=jnp.int32)[None, :], PLEN, axis=1)
            suffix_terms = jnp.take(bias_table, bucket_of(window_ids[None, :] - query_ids[:, None]), axis=1)
            suffix_allowed = window_req[None, :] == query_req[:, None]
            scores = jnp.concatenate([jnp.einsum('qhd,khd->hqk', query_block, cache_keys) + prefix_terms, jnp.einsum('qhd,khd->hqk', query_block, key_window) + suffix_terms], axis=2)
            allowed = jnp.concatenate([prefix_allowed, suffix_allowed], axis=1)
            scores = jnp.where(allowed[None], scores, masked_score)
            row_max = lax.optimization_barrier(jnp.max(scores, axis=2, keepdims=True))
            exp_terms = jnp.exp(scores - row_max)
            row_sum = lax.optimization_barrier(jnp.sum(exp_terms, axis=2))
            weights = lax.optimization_barrier(exp_terms.astype(jnp.bfloat16)).astype(jnp.float32)
            all_values = jnp.concatenate([cache_values, value_window], axis=0)
            weighted = jnp.einsum('hqk,khd->hqd', weights, all_values)
            attended = (weighted / row_sum[:, :, None]).transpose(1, 0, 2).reshape(TOK_DEV, D)
            return attended.astype(jnp.bfloat16)
        attended = lax.map(attend, jnp.arange(N_REQ, dtype=jnp.int32)).reshape(TOK_GRP, D)
        hidden_one = (group_rows.astype(jnp.float32) + jnp.dot(attended, w_attn_out, preferred_element_type=jnp.float32)).astype(jnp.bfloat16)
        normed_two = norm_rows(hidden_one, mlp_gain)
        units = jnp.maximum(jnp.dot(normed_two, w_in.T, preferred_element_type=jnp.float32), 0.0).astype(jnp.bfloat16)
        layer_out = (hidden_one.astype(jnp.float32) + jnp.dot(units, w_out, preferred_element_type=jnp.float32)).astype(jnp.bfloat16)
        results.append(layer_out)
    return jnp.concatenate(results, axis=0)
```

```python
import functools

import jax
import jax.numpy as jnp
from jax import lax
from jax.experimental import pallas as pl
from jax.experimental.pallas import tpu as pltpu
from jax.sharding import Mesh, PartitionSpec as P

D = 1024
H = 16
DK = 64
PLEN = 512
PREF_GRP = 2
ROWS = 128
PAIRS = 8
LANES = 128

epsilon = 1e-06
far_marks = (12, 16, 23, 32, 46, 64, 91)
masked_score = -1e30
VMEM_LIMIT = 56 * 1024 * 1024

AXES = ("yhi", "core", "x", "z", "ylo")
REQ = ("x", "z", "ylo")
PLANE = ("z", "ylo")
MIRROR = [(0, 3), (3, 0), (1, 2), (2, 1)]
SWAP = [(0, 1), (1, 0)]


def norm_rows(values_in, gain):
    widened = values_in.astype(jnp.float32)
    scale = lax.rsqrt(jnp.mean(widened * widened, axis=-1, keepdims=True) + epsilon)
    return (widened * scale * gain).astype(jnp.bfloat16)


def project_kernel(tok_ref, gain_ref, wq_ref, wk_ref, wv_ref, out_ref, normed_ref):
    @pl.when(pl.program_id(0) == 0)
    def _():
        normed_ref[...] = norm_rows(tok_ref[...], gain_ref[...])

    normed = normed_ref[...]
    for kind, w_ref in enumerate((wq_ref, wk_ref, wv_ref)):
        got = jnp.dot(normed, w_ref[...], preferred_element_type=jnp.float32)
        got = got.astype(jnp.bfloat16)
        for part in range(got.shape[1] // LANES):
            out_ref[part, kind] = got[:, part * LANES : (part + 1) * LANES]


def project(tokens, gain, w_query, w_key, w_value):
    width = 256
    per = width // LANES
    w_spec = pl.BlockSpec((D, width), lambda j: (0, j))
    return pl.pallas_call(
        project_kernel,
        grid=(D // width,),
        in_specs=[
            pl.BlockSpec((ROWS, D), lambda j: (0, 0)),
            pl.BlockSpec((1, D), lambda j: (0, 0)),
            w_spec,
            w_spec,
            w_spec,
        ],
        out_specs=pl.BlockSpec((per, 3, ROWS, LANES), lambda j: (j, 0, 0, 0)),
        out_shape=jax.ShapeDtypeStruct((PAIRS, 3, ROWS, LANES), jnp.bfloat16),
        scratch_shapes=[pltpu.VMEM((ROWS, D), jnp.bfloat16)],
        compiler_params=pltpu.CompilerParams(vmem_limit_bytes=VMEM_LIMIT),
        name="project",
    )(tokens, gain.reshape(1, D), w_query, w_key, w_value)


def bias_line(rel_ref, head, first_bucket):
    lane = lax.broadcasted_iota(jnp.int32, (ROWS, LANES), 1)
    line = jnp.full((ROWS, LANES), rel_ref[first_bucket, head], jnp.float32)
    for bucket in range(1, 16):
        mark = bucket if bucket <= 8 else far_marks[bucket - 9]
        line = jnp.where(lane >= mark, rel_ref[first_bucket + bucket, head], line)
    return line


def attend_kernel(
    pair_ref, rel_ref, qkv_ref, halo_ref, pref_ref, meta_ref, out_ref, kcat, vcat, kwin, vwin, near
):
    step = pl.program_id(0)
    pair = pair_ref[0]
    row = lax.broadcasted_iota(jnp.int32, (ROWS, LANES), 0)
    lane = lax.broadcasted_iota(jnp.int32, (ROWS, LANES), 1)

    @pl.when(step == 0)
    def _():
        for p in range(PREF_GRP):
            kcat[:, p * LANES : (p + 1) * LANES] = pref_ref[:, 0, p].reshape(PLEN, LANES)
            vcat[:, p * LANES : (p + 1) * LANES] = pref_ref[:, 1, p].reshape(PLEN, LANES)
        for dst, kind in ((kwin, 0), (vwin, 1)):
            dst[0:ROWS] = halo_ref[0, kind]
            for b in range(PAIRS):
                dst[(b + 1) * ROWS : (b + 2) * ROWS] = qkv_ref[b, kind + 1]
            dst[(PAIRS + 1) * ROWS : (PAIRS + 2) * ROWS] = halo_ref[1, kind]
        for h in range(2):
            before = bias_line(rel_ref, pair * 2 + h, 0)
            after = bias_line(rel_ref, pair * 2 + h, 16)

            def pick(line, distance):
                at = jnp.clip(distance, 0, LANES - 1)
                return jnp.take_along_axis(line, at, axis=1)

            rows = slice(h * ROWS, (h + 1) * ROWS)
            near[rows, 0:LANES] = pick(before, row + LANES - lane)
            near[rows, LANES : 2 * LANES] = jnp.where(
                lane > row, pick(after, lane - row), pick(before, row - lane)
            )
            near[rows, 2 * LANES : 3 * LANES] = pick(after, lane + LANES - row)

    query = qkv_ref[step, 0]
    own = jnp.transpose(meta_ref[step + 1])
    request, offset, chosen = own[:, 0:1], own[:, 1:2], own[:, 2:3]
    zero = jnp.zeros_like(query)
    low = lane < DK
    halves = [jnp.where(low, query, zero), jnp.where(low, zero, query)]
    stacked = jnp.concatenate(halves, axis=0)
    second = jnp.concatenate([chosen, chosen], axis=0) > 0.5
    zeros = jnp.zeros_like(stacked)
    split = jnp.concatenate(
        [jnp.where(second, zeros, stacked), jnp.where(second, stacked, zeros)], axis=1
    )
    contract = (((1,), (1,)), ((), ()))
    far_scores = lax.dot_general(split, kcat[...], contract, preferred_element_type=jnp.float32)
    begin = pl.multiple_of(step * ROWS, ROWS)
    near_scores = lax.dot_general(
        stacked, kwin[pl.ds(begin, 3 * ROWS)], contract, preferred_element_type=jnp.float32
    )
    tail_at = jnp.minimum(LANES - lane + offset.astype(jnp.int32), LANES - 1)
    tails, fulls = [], []
    for h in range(2):
        line = bias_line(rel_ref, pair * 2 + h, 0)
        tails.append(jnp.take_along_axis(line, tail_at, axis=1))
        fulls.append(jnp.full((ROWS, 1), rel_ref[15, pair * 2 + h], jnp.float32))
    far_head = far_scores[:, : PLEN - LANES] + jnp.concatenate(fulls, axis=0)
    far_tail = far_scores[:, PLEN - LANES :] + jnp.concatenate(tails, axis=0)
    same = []
    for b in range(3):
        mine = meta_ref[step + b, 0:1, :] == request
        same.append(jnp.concatenate([mine, mine], axis=0))
    near_scores = near_scores + near[...]
    near_parts = [
        jnp.where(same[b], near_scores[:, b * LANES : (b + 1) * LANES], masked_score)
        for b in range(3)
    ]
    parts = [far_head[:, b * LANES : (b + 1) * LANES] for b in range(3)] + [far_tail] + near_parts
    tallest = functools.reduce(jnp.maximum, parts)
    row_max = jnp.max(tallest, axis=1, keepdims=True)
    terms = [jnp.exp(part - row_max) for part in parts]
    row_sum = jnp.sum(functools.reduce(jnp.add, terms), axis=1, keepdims=True)
    weights = [t.astype(jnp.bfloat16) for t in terms]
    far_out = jnp.dot(
        jnp.concatenate(weights[:4], axis=1), vcat[...], preferred_element_type=jnp.float32
    )
    near_out = jnp.dot(
        jnp.concatenate(weights[4:], axis=1),
        vwin[pl.ds(begin, 3 * ROWS)],
        preferred_element_type=jnp.float32,
    )
    total = jnp.where(second, far_out[:, LANES:], far_out[:, :LANES]) + near_out
    total = total / row_sum
    out_ref[0] = jnp.where(low, total[:ROWS], total[ROWS:]).astype(jnp.bfloat16)


def attend(pair, rel_bias, qkv, halo, pref, meta):
    whole = lambda shape: pl.BlockSpec(shape, lambda i: (0,) * len(shape))
    smem = pl.BlockSpec(memory_space=pltpu.SMEM)
    window = (PAIRS + 2) * ROWS
    return pl.pallas_call(
        attend_kernel,
        grid=(PAIRS,),
        in_specs=[smem, smem, whole(qkv.shape), whole(halo.shape), whole(pref.shape), whole(meta.shape)],
        out_specs=pl.BlockSpec((1, ROWS, LANES), lambda i: (i, 0, 0)),
        out_shape=jax.ShapeDtypeStruct((PAIRS, ROWS, LANES), jnp.bfloat16),
        scratch_shapes=[
            pltpu.VMEM((PLEN, 2 * LANES), jnp.bfloat16),
            pltpu.VMEM((PLEN, 2 * LANES), jnp.bfloat16),
            pltpu.VMEM((window, LANES), jnp.bfloat16),
            pltpu.VMEM((window, LANES), jnp.bfloat16),
            pltpu.VMEM((2 * ROWS, 3 * LANES), jnp.float32),
        ],
        compiler_params=pltpu.CompilerParams(vmem_limit_bytes=VMEM_LIMIT),
        name="attend",
    )(pair, rel_bias, qkv, halo, pref, meta)


def token_table(lengths_row, prefix_row, first):
    count = (PAIRS + 2) * ROWS
    ends = jnp.cumsum(lengths_row)
    starts = ends - lengths_row
    ids = first + jnp.arange(count, dtype=jnp.int32)
    member = ((ids[None, :] >= starts[:, None]) & (ids[None, :] < ends[:, None])).astype(jnp.int32)
    numbers = jnp.arange(1, lengths_row.shape[0] + 1, dtype=jnp.int32)
    request = jnp.sum(member * numbers[:, None], axis=0) - 1
    offset = ids - jnp.sum(member * starts[:, None], axis=0)
    chosen = jnp.sum(member * prefix_row[:, None], axis=0)
    table = jnp.stack([request, offset, chosen] + [request] * 5, axis=0).astype(jnp.float32)
    return table.reshape(8, PAIRS + 2, ROWS).transpose(1, 0, 2)


def join_kernel(att_ref, w_ref, tok_ref, gain_ref, hidden_ref, normed_ref):
    attended = jnp.concatenate([att_ref[j] for j in range(PAIRS)], axis=1)
    got = jnp.dot(attended, w_ref[...], preferred_element_type=jnp.float32)
    hidden = (tok_ref[...].astype(jnp.float32) + got).astype(jnp.bfloat16)
    hidden_ref[...] = hidden
    normed_ref[...] = norm_rows(hidden, gain_ref[...])


def join(att, w_attn_out, tokens, gain):
    shape = jax.ShapeDtypeStruct((ROWS, D), jnp.bfloat16)
    return pl.pallas_call(
        join_kernel,
        out_shape=(shape, shape),
        compiler_params=pltpu.CompilerParams(vmem_limit_bytes=VMEM_LIMIT),
        name="join",
    )(att, w_attn_out, tokens, gain.reshape(1, D))


def feed_kernel(one_ref, two_ref, in_ref, out_ref, first_ref, second_ref):
    rows = jnp.concatenate([one_ref[...], two_ref[...]], axis=0)
    units = lax.dot_general(
        rows, in_ref[...], (((1,), (1,)), ((), ())), preferred_element_type=jnp.float32
    )
    units = jnp.maximum(units, 0.0).astype(jnp.bfloat16)
    got = jnp.dot(units, out_ref[...], preferred_element_type=jnp.float32).astype(jnp.bfloat16)
    first_ref[...] = got[:ROWS]
    second_ref[...] = got[ROWS:]


def feed(one, two, w_in, w_out):
    shape = jax.ShapeDtypeStruct((ROWS, D), jnp.bfloat16)
    return pl.pallas_call(
        feed_kernel,
        out_shape=(shape, shape),
        compiler_params=pltpu.CompilerParams(vmem_limit_bytes=VMEM_LIMIT),
        name="feed",
    )(one, two, w_in, w_out)


def body(
    tokens,
    attn_gain,
    w_query,
    w_key,
    w_value,
    w_attn_out,
    rel_bias,
    prefix_cache,
    lengths,
    prefix_map,
    mlp_gain,
    w_in,
    w_out,
):
    plane_x = lax.axis_index("x")
    count_x = lax.axis_size("x")
    pair = (lax.axis_index("z") * 2 + lax.axis_index("ylo")).astype(jnp.int32).reshape(1)

    held = prefix_cache.reshape(PREF_GRP, -1, 2, PAIRS, LANES).transpose(3, 2, 0, 1, 4)
    sent = jnp.broadcast_to(held[None], (count_x,) + held.shape).reshape((-1,) + held.shape[1:])
    pref = lax.all_to_all(sent, REQ, 0, 0, tiled=True)

    meta = token_table(lengths[0], prefix_map[0], plane_x * (PAIRS * ROWS) - ROWS)
    blocks = project(tokens, attn_gain, w_query, w_key, w_value)
    qkv = lax.all_to_all(blocks, PLANE, 0, 0, tiled=True)
    up = [(i, (i + 1) % count_x) for i in range(count_x)]
    down = [(j, i) for i, j in up]
    before = lax.ppermute(qkv[PAIRS - 1, 1:], "x", up)
    after = lax.ppermute(qkv[0, 1:], "x", down)
    mixed = attend(pair, rel_bias, qkv, jnp.stack([before, after]), pref, meta)
    att = lax.all_to_all(mixed, PLANE, 0, 0, tiled=True)
    hidden, normed = join(att, w_attn_out, tokens, mlp_gain)

    other = lax.ppermute(normed, "core", SWAP)
    far = lax.ppermute(normed, ("yhi", "ylo"), MIRROR)
    far_other = lax.ppermute(far, "core", SWAP)
    mine, theirs = feed(normed, other, w_in, w_out)
    far_mine, far_theirs = feed(far, far_other, w_in, w_out)
    far_sum = far_mine.astype(jnp.float32) + lax.ppermute(far_theirs, "core", SWAP).astype(jnp.float32)
    back = lax.ppermute(far_sum.astype(jnp.bfloat16), ("yhi", "ylo"), MIRROR)
    local = mine.astype(jnp.float32) + lax.ppermute(theirs, "core", SWAP).astype(jnp.float32)
    return (hidden.astype(jnp.float32) + (local + back.astype(jnp.float32))).astype(jnp.bfloat16)


def solution(mesh):
    split = Mesh(mesh.devices.reshape(2, 2, 4, 4, 2), AXES)
    grp, req = ("yhi", "core"), REQ
    return jax.shard_map(
        body,
        mesh=split,
        in_specs=(
            P(grp + req, None),
            P(),
            P(),
            P(),
            P(),
            P(),
            P(),
            P(grp, req, None),
            P(grp, None),
            P(grp, None),
            P(),
            P(grp, None),
            P(grp, None),
        ),
        out_specs=P(grp + req, None),
        check_vma=False,
    )
```

```python
import functools

import jax
import jax.numpy as jnp
from jax import lax
from jax.experimental import pallas as pl
from jax.experimental.pallas import tpu as pltpu
from jax.sharding import Mesh, PartitionSpec as P

D = 1024
H = 16
DK = 64
PLEN = 512
PREF_GRP = 2
ROWS = 128
PAIRS = 8
LANES = 128

epsilon = 1e-06
far_marks = (12, 16, 23, 32, 46, 64, 91)
masked_score = -1e30
VMEM_LIMIT = 16 * 1024 * 1024

AXES = ("yhi", "core", "x", "z", "ylo")
REQ = ("x", "z", "ylo")
PLANE = ("z", "ylo")
MIRROR = [(0, 3), (3, 0), (1, 2), (2, 1)]
SWAP = [(0, 1), (1, 0)]


def norm_rows(values_in, gain):
    widened = values_in.astype(jnp.float32)
    scale = lax.rsqrt(jnp.mean(widened * widened, axis=-1, keepdims=True) + epsilon)
    return (widened * scale * gain).astype(jnp.bfloat16)


def on_chip(*arrays):
    return tuple(pltpu.with_memory_space_constraint(a, pltpu.VMEM) for a in arrays)


VMEM_SPEC = pl.BlockSpec(memory_space=pltpu.VMEM)
SMEM_SPEC = pl.BlockSpec(memory_space=pltpu.SMEM)


def project_kernel(tok_ref, gain_ref, wq_ref, wk_ref, wv_ref, out_ref):
    normed = norm_rows(tok_ref[...], gain_ref[...])
    for kind, w_ref in enumerate((wq_ref, wk_ref, wv_ref)):
        got = jnp.dot(normed, w_ref[...], preferred_element_type=jnp.float32)
        got = got.astype(jnp.bfloat16)
        for part in range(PAIRS):
            out_ref[part, kind] = got[:, part * LANES : (part + 1) * LANES]


def project(tokens, gain, w_query, w_key, w_value):
    return pl.pallas_call(
        project_kernel,
        in_specs=[VMEM_SPEC] * 5,
        out_specs=VMEM_SPEC,
        out_shape=jax.ShapeDtypeStruct((PAIRS, 3, ROWS, LANES), jnp.bfloat16),
        compiler_params=pltpu.CompilerParams(vmem_limit_bytes=VMEM_LIMIT),
        name="project",
    )(*on_chip(tokens, gain.reshape(1, D), w_query, w_key, w_value))


def after(value, other):
    anywhere = pl.BlockSpec(memory_space=pl.ANY)
    return pl.pallas_call(
        lambda value_ref, other_ref, out_ref: None,
        in_specs=[anywhere, anywhere],
        out_specs=anywhere,
        out_shape=jax.ShapeDtypeStruct(value.shape, value.dtype),
        input_output_aliases={0: 0},
        name="after",
    )(value, other)


def bias_line(rel_ref, head, first_bucket):
    lane = lax.broadcasted_iota(jnp.int32, (ROWS, LANES), 1)
    line = jnp.full((ROWS, LANES), rel_ref[first_bucket, head], jnp.float32)
    for bucket in range(1, 16):
        mark = bucket if bucket <= 8 else far_marks[bucket - 9]
        line = jnp.where(lane >= mark, rel_ref[first_bucket + bucket, head], line)
    return line


def prepare_kernel(pair_ref, rel_ref, pref_ref, keys_ref, values_ref, near_ref, line_ref):
    row = lax.broadcasted_iota(jnp.int32, (ROWS, LANES), 0)
    lane = lax.broadcasted_iota(jnp.int32, (ROWS, LANES), 1)
    for p in range(PREF_GRP):
        keys_ref[p * LANES : (p + 1) * LANES, :] = jnp.transpose(pref_ref[:, 0, p].reshape(PLEN, LANES))
        values_ref[:, p * LANES : (p + 1) * LANES] = pref_ref[:, 1, p].reshape(PLEN, LANES)
    for h in range(2):
        head = pair_ref[0] * 2 + h
        before = bias_line(rel_ref, head, 0)
        after_it = bias_line(rel_ref, head, 16)

        def pick(line, distance):
            return jnp.take_along_axis(line, jnp.clip(distance, 0, LANES - 1), axis=1)

        rows = slice(h * ROWS, (h + 1) * ROWS)
        near_ref[rows, 0:LANES] = pick(before, row + LANES - lane)
        near_ref[rows, LANES : 2 * LANES] = jnp.where(
            lane > row, pick(after_it, lane - row), pick(before, row - lane)
        )
        near_ref[rows, 2 * LANES : 3 * LANES] = pick(after_it, lane + LANES - row)
        line_ref[rows, :] = before


def prepare(pair, rel_bias, pref):
    return pl.pallas_call(
        prepare_kernel,
        in_specs=[SMEM_SPEC, SMEM_SPEC, VMEM_SPEC],
        out_specs=(VMEM_SPEC,) * 4,
        out_shape=(
            pltpu.VMEM((PREF_GRP * LANES, PLEN), jnp.bfloat16),
            pltpu.VMEM((PLEN, PREF_GRP * LANES), jnp.bfloat16),
            pltpu.VMEM((2 * ROWS, 3 * LANES), jnp.float32),
            pltpu.VMEM((2 * ROWS, LANES), jnp.float32),
        ),
        compiler_params=pltpu.CompilerParams(vmem_limit_bytes=VMEM_LIMIT),
        name="prepare",
    )(pair, rel_bias, *on_chip(pref))


def attend_kernel(
    qkv_ref, prev_ref, next_ref, keys_ref, values_ref, near_ref, line_ref, meta_ref, out_ref, kwin, vwin
):
    lane = lax.broadcasted_iota(jnp.int32, (ROWS, LANES), 1)
    low = lane < DK
    for b in range(PAIRS + 2):
        for dst, kind in ((kwin, 0), (vwin, 1)):
            if b == 0:
                block = prev_ref[kind]
            elif b == PAIRS + 1:
                block = next_ref[kind]
            else:
                block = qkv_ref[b - 1, kind + 1]
            dst[b] = jnp.transpose(block) if kind == 0 else block

    def one(step, _):
        query = qkv_ref[step, 0]
        own = jnp.transpose(meta_ref[step + 1])
        request, offset, chosen = own[:, 0:1], own[:, 1:2], own[:, 2:3]
        zero = jnp.zeros_like(query)
        stacked = jnp.concatenate([jnp.where(low, query, zero), jnp.where(low, zero, query)], axis=0)
        second = jnp.concatenate([chosen, chosen], axis=0) > 0.5
        zeros = jnp.zeros_like(stacked)
        split = jnp.concatenate(
            [jnp.where(second, zeros, stacked), jnp.where(second, stacked, zeros)], axis=1
        )
        far_scores = jnp.dot(split, keys_ref[...], preferred_element_type=jnp.float32)
        near_keys = jnp.concatenate([kwin[step + b] for b in range(3)], axis=1)
        near_scores = jnp.dot(stacked, near_keys, preferred_element_type=jnp.float32)
        tail_at = jnp.minimum(LANES - lane + offset.astype(jnp.int32), LANES - 1)
        line = line_ref[...]
        tail = jnp.take_along_axis(line, jnp.concatenate([tail_at, tail_at], axis=0), axis=1)
        full = line[:, LANES - 1 :]
        parts = [far_scores[:, b * LANES : (b + 1) * LANES] + full for b in range(3)]
        parts.append(far_scores[:, 3 * LANES :] + tail)
        for b in range(3):
            mine = meta_ref[step + b, 0:1, :] == request
            mine = jnp.concatenate([mine, mine], axis=0)
            at = slice(b * LANES, (b + 1) * LANES)
            parts.append(jnp.where(mine, near_scores[:, at] + near_ref[:, at], masked_score))
        row_max = jnp.max(functools.reduce(jnp.maximum, parts), axis=1, keepdims=True)
        terms = [jnp.exp(part - row_max) for part in parts]
        row_sum = jnp.sum(functools.reduce(jnp.add, terms), axis=1, keepdims=True)
        weights = [t.astype(jnp.bfloat16) for t in terms]
        far_out = jnp.dot(
            jnp.concatenate(weights[:4], axis=1), values_ref[...], preferred_element_type=jnp.float32
        )
        near_values = jnp.concatenate([vwin[step + b] for b in range(3)], axis=0)
        near_out = jnp.dot(
            jnp.concatenate(weights[4:], axis=1), near_values, preferred_element_type=jnp.float32
        )
        total = jnp.where(second, far_out[:, LANES:], far_out[:, :LANES]) + near_out
        total = total / row_sum
        out_ref[step] = jnp.where(low, total[:ROWS], total[ROWS:]).astype(jnp.bfloat16)
        return 0

    lax.fori_loop(0, PAIRS, one, 0)


def attend(qkv, prev, after_it, prepared, meta):
    return pl.pallas_call(
        attend_kernel,
        in_specs=[VMEM_SPEC] * 8,
        out_specs=VMEM_SPEC,
        out_shape=pltpu.VMEM((PAIRS, ROWS, LANES), jnp.bfloat16),
        scratch_shapes=[
            pltpu.VMEM((PAIRS + 2, LANES, ROWS), jnp.bfloat16),
            pltpu.VMEM((PAIRS + 2, ROWS, LANES), jnp.bfloat16),
        ],
        compiler_params=pltpu.CompilerParams(vmem_limit_bytes=VMEM_LIMIT),
        name="attend",
    )(*on_chip(qkv, prev, after_it, *prepared, meta))


def token_table(lengths_row, prefix_row, first):
    count = (PAIRS + 2) * ROWS
    ends = jnp.cumsum(lengths_row)
    starts = ends - lengths_row
    ids = first + jnp.arange(count, dtype=jnp.int32)
    member = ((ids[None, :] >= starts[:, None]) & (ids[None, :] < ends[:, None])).astype(jnp.int32)
    numbers = jnp.arange(1, lengths_row.shape[0] + 1, dtype=jnp.int32)
    request = jnp.sum(member * numbers[:, None], axis=0) - 1
    offset = ids - jnp.sum(member * starts[:, None], axis=0)
    chosen = jnp.sum(member * prefix_row[:, None], axis=0)
    table = jnp.stack([request, offset, chosen] + [request] * 5, axis=0).astype(jnp.float32)
    return table.reshape(8, PAIRS + 2, ROWS).transpose(1, 0, 2)


def join_kernel(att_ref, w_ref, tok_ref, gain_ref, hidden_ref, normed_ref):
    attended = jnp.concatenate([att_ref[j] for j in range(PAIRS)], axis=1)
    got = jnp.dot(attended, w_ref[...], preferred_element_type=jnp.float32)
    hidden = (tok_ref[...].astype(jnp.float32) + got).astype(jnp.bfloat16)
    hidden_ref[...] = hidden
    normed_ref[...] = norm_rows(hidden, gain_ref[...])


def join(att, w_attn_out, tokens, gain):
    shape = pltpu.VMEM((ROWS, D), jnp.bfloat16)
    return pl.pallas_call(
        join_kernel,
        in_specs=[VMEM_SPEC] * 4,
        out_specs=(VMEM_SPEC,) * 2,
        out_shape=(shape, shape),
        compiler_params=pltpu.CompilerParams(vmem_limit_bytes=VMEM_LIMIT),
        name="join",
    )(*on_chip(att, w_attn_out, tokens, gain.reshape(1, D)))


def feed_kernel(one_ref, two_ref, in_ref, out_ref, first_ref, second_ref):
    two = two_ref[...] if len(two_ref.shape) == 2 else two_ref[0]
    rows = jnp.concatenate([one_ref[...], two], axis=0)
    units = lax.dot_general(
        rows, in_ref[...], (((1,), (1,)), ((), ())), preferred_element_type=jnp.float32
    )
    units = jnp.maximum(units, 0.0).astype(jnp.bfloat16)
    got = jnp.dot(units, out_ref[...], preferred_element_type=jnp.float32).astype(jnp.bfloat16)
    first_ref[...] = got[:ROWS]
    second_ref[...] = got[ROWS:]


def feed(one, two, w_in, w_out):
    shape = pltpu.VMEM((ROWS, D), jnp.bfloat16)
    return pl.pallas_call(
        feed_kernel,
        in_specs=[VMEM_SPEC] * 4,
        out_specs=(VMEM_SPEC,) * 2,
        out_shape=(shape, shape),
        compiler_params=pltpu.CompilerParams(vmem_limit_bytes=VMEM_LIMIT),
        name="feed",
    )(*on_chip(one, two, w_in, w_out))


def pack_kernel(one_ref, two_ref, out_ref):
    out_ref[0] = one_ref[...]
    out_ref[1] = two_ref[...]


def pack(one, two):
    return pl.pallas_call(
        pack_kernel,
        in_specs=[VMEM_SPEC] * 2,
        out_specs=VMEM_SPEC,
        out_shape=pltpu.VMEM((2,) + one.shape, one.dtype),
        compiler_params=pltpu.CompilerParams(vmem_limit_bytes=VMEM_LIMIT),
        name="pack",
    )(*on_chip(one, two))


def total_kernel(*refs):
    out_ref = refs[-1]
    values = [ref[...] if len(ref.shape) == 2 else ref[1] for ref in refs[:-1]]
    total = functools.reduce(jnp.add, [value.astype(jnp.float32) for value in values])
    out_ref[...] = total.astype(out_ref.dtype)


def total(dtype, *arrays, last=False):
    return pl.pallas_call(
        total_kernel,
        in_specs=[VMEM_SPEC] * len(arrays),
        out_specs=VMEM_SPEC,
        out_shape=(jax.ShapeDtypeStruct if last else pltpu.VMEM)(arrays[0].shape, dtype),
        compiler_params=pltpu.CompilerParams(vmem_limit_bytes=VMEM_LIMIT),
        name="total",
    )(*on_chip(*arrays))


def body(
    tokens,
    attn_gain,
    w_query,
    w_key,
    w_value,
    w_attn_out,
    rel_bias,
    prefix_cache,
    lengths,
    prefix_map,
    mlp_gain,
    w_in,
    w_out,
):
    plane_x = lax.axis_index("x")
    count_x = lax.axis_size("x")
    pair = (lax.axis_index("z") * 2 + lax.axis_index("ylo")).astype(jnp.int32).reshape(1)

    held = prefix_cache.reshape(PREF_GRP, -1, 2, PAIRS, LANES).transpose(3, 2, 0, 1, 4)
    sent = jnp.broadcast_to(held[None], (count_x,) + held.shape).reshape((-1,) + held.shape[1:])
    pref = lax.all_to_all(sent, REQ, 0, 0, tiled=True)

    meta = token_table(lengths[0], prefix_map[0], plane_x * (PAIRS * ROWS) - ROWS)
    blocks = after(project(tokens, attn_gain, w_query, w_key, w_value), pref[0, 0, 0])
    qkv = lax.all_to_all(blocks, PLANE, 0, 0, tiled=True)
    prepared = prepare(pair, rel_bias, pref)
    up = [(i, (i + 1) % count_x) for i in range(count_x)]
    down = [(j, i) for i, j in up]
    before = lax.ppermute(qkv[PAIRS - 1, 1:], "x", up)
    later = lax.ppermute(qkv[0, 1:], "x", down)
    mixed = attend(qkv, before, later, prepared, meta)
    att = lax.all_to_all(mixed, PLANE, 0, 0, tiled=True)
    hidden, normed = join(att, w_attn_out, tokens, mlp_gain)

    mirrored = ("yhi", "ylo")
    far = lax.ppermute(normed, mirrored, MIRROR)
    other = lax.ppermute(normed, "core", SWAP)
    mine, theirs = feed(normed, other, w_in, w_out)
    pair_swap = lax.ppermute(pack(far, theirs), "core", SWAP)
    far_mine, far_theirs = feed(far, pair_swap, w_in, w_out)
    far_sum = total(jnp.bfloat16, far_mine, lax.ppermute(far_theirs, "core", SWAP))
    back = lax.ppermute(far_sum, mirrored, MIRROR)
    local = total(jnp.float32, hidden, mine, pair_swap)
    return total(jnp.bfloat16, local, back, last=True)


def solution(mesh):
    split = Mesh(mesh.devices.reshape(2, 2, 4, 4, 2), AXES)
    grp, req = ("yhi", "core"), REQ
    return jax.shard_map(
        body,
        mesh=split,
        in_specs=(
            P(grp + req, None),
            P(),
            P(),
            P(),
            P(),
            P(),
            P(),
            P(grp, req, None),
            P(grp, None),
            P(grp, None),
            P(),
            P(grp, None),
            P(grp, None),
        ),
        out_specs=P(grp + req, None),
        check_vma=False,
    )
```

```python
import functools

import jax
import jax.numpy as jnp
from jax import lax
from jax.experimental import pallas as pl
from jax.experimental.pallas import tpu as pltpu
from jax.sharding import Mesh, PartitionSpec as P

D = 1024
H = 16
DK = 64
PLEN = 512
PREF_GRP = 2
ROWS = 128
PAIRS = 8
LANES = 128
CHUNK = 512
SHARE = 16
SENT = 3 * ROWS + 2 * PREF_GRP * SHARE
QUARTER = PAIRS * 2 * PREF_GRP * SHARE

epsilon = 1e-06
far_marks = (12, 16, 23, 32, 46, 64, 91)
masked_score = -1e30
VMEM_LIMIT = 16 * 1024 * 1024

AXES = ("yhi", "core", "x", "z", "ylo")
REQ = ("x", "z", "ylo")
PLANE = ("z", "ylo")
MIRROR = [(0, 3), (3, 0), (1, 2), (2, 1)]
SWAP = [(0, 1), (1, 0)]


def norm_rows(values_in, gain):
    widened = values_in.astype(jnp.float32)
    scale = lax.rsqrt(jnp.mean(widened * widened, axis=-1, keepdims=True) + epsilon)
    return (widened * scale * gain).astype(jnp.bfloat16)


def on_chip(*arrays):
    return tuple(pltpu.with_memory_space_constraint(a, pltpu.VMEM) for a in arrays)


VMEM_SPEC = pl.BlockSpec(memory_space=pltpu.VMEM)
SMEM_SPEC = pl.BlockSpec(memory_space=pltpu.SMEM)


def project_kernel(
    tok_ref, gain_ref, cache_ref, wq_ref, wk_ref, wv_ref, out_ref, held, arrived
):
    columns = [slice(c * CHUNK, (c + 1) * CHUNK) for c in range(D // CHUNK)]
    copies = [
        [
            pltpu.make_async_copy(w_ref.at[:, cut], held.at[kind, c], arrived.at[kind, c])
            for c, cut in enumerate(columns)
        ]
        for kind, w_ref in enumerate((wq_ref, wk_ref, wv_ref))
    ]
    for row in copies:
        for copy in row:
            copy.start()
    for part in range(PAIRS):
        for kind in range(2):
            for p in range(PREF_GRP):
                at = 3 * ROWS + (kind * PREF_GRP + p) * SHARE
                cut = slice(kind * D + part * LANES, kind * D + (part + 1) * LANES)
                out_ref[part, at : at + SHARE] = cache_ref[p, :, cut]
    normed = norm_rows(tok_ref[...], gain_ref[...])
    for kind, row in enumerate(copies):
        for c, copy in enumerate(row):
            copy.wait()
            got = jnp.dot(normed, held[kind, c], preferred_element_type=jnp.float32)
            got = got.astype(jnp.bfloat16)
            for part in range(CHUNK // LANES):
                to = c * (CHUNK // LANES) + part
                out_ref[to, kind * ROWS : (kind + 1) * ROWS] = got[:, part * LANES : (part + 1) * LANES]


def project(tokens, gain, w_query, w_key, w_value, prefix_cache):
    anywhere = pl.BlockSpec(memory_space=pl.ANY)
    return pl.pallas_call(
        project_kernel,
        in_specs=[VMEM_SPEC] * 3 + [anywhere] * 3,
        out_specs=VMEM_SPEC,
        out_shape=pltpu.VMEM((PAIRS, SENT, LANES), jnp.bfloat16),
        scratch_shapes=[
            pltpu.VMEM((3, D // CHUNK, D, CHUNK), jnp.bfloat16),
            pltpu.SemaphoreType.DMA((3, D // CHUNK)),
        ],
        compiler_params=pltpu.CompilerParams(vmem_limit_bytes=VMEM_LIMIT),
        name="project",
    )(*on_chip(tokens, gain.reshape(1, D), prefix_cache), w_query, w_key, w_value)


def spread_kernel(got_ref, up_ref, down_ref, far_ref):
    for source in range(PAIRS):
        rows = slice(source * 4 * SHARE, (source + 1) * 4 * SHARE)
        held = got_ref[source, 3 * ROWS :]
        up_ref[rows] = held
        down_ref[rows] = held
        far_ref[rows] = held
    up_ref[QUARTER:] = got_ref[PAIRS - 1, ROWS : 3 * ROWS]
    down_ref[QUARTER:] = got_ref[0, ROWS : 3 * ROWS]


def spread(got):
    shape = pltpu.VMEM((QUARTER + 2 * ROWS, LANES), jnp.bfloat16)
    return pl.pallas_call(
        spread_kernel,
        in_specs=[VMEM_SPEC],
        out_specs=(VMEM_SPEC,) * 3,
        out_shape=(shape, shape, pltpu.VMEM((QUARTER, LANES), jnp.bfloat16)),
        compiler_params=pltpu.CompilerParams(vmem_limit_bytes=VMEM_LIMIT),
        name="spread",
    )(*on_chip(got))


def bias_line(rel_ref, head, first_bucket):
    lane = lax.broadcasted_iota(jnp.int32, (ROWS, LANES), 1)
    line = jnp.full((ROWS, LANES), rel_ref[head, first_bucket], jnp.float32)
    for bucket in range(1, 16):
        mark = bucket if bucket <= 8 else far_marks[bucket - 9]
        line = jnp.where(lane >= mark, rel_ref[head, first_bucket + bucket], line)
    return line


def tables_kernel(place_ref, rel_ref, len_ref, map_ref, near_ref, line_ref, meta_ref):
    row = lax.broadcasted_iota(jnp.int32, (ROWS, LANES), 0)
    lane = lax.broadcasted_iota(jnp.int32, (ROWS, LANES), 1)
    for h in range(2):
        head = place_ref[1] * 2 + h
        before = bias_line(rel_ref, head, 0)
        after_it = bias_line(rel_ref, head, 16)

        def pick(line, distance):
            return jnp.take_along_axis(line, jnp.clip(distance, 0, LANES - 1), axis=1)

        rows = slice(h * ROWS, (h + 1) * ROWS)
        near_ref[rows, 0:LANES] = pick(before, row + LANES - lane)
        near_ref[rows, LANES : 2 * LANES] = jnp.where(
            lane > row, pick(after_it, lane - row), pick(before, row - lane)
        )
        near_ref[rows, 2 * LANES : 3 * LANES] = pick(after_it, lane + LANES - row)
        line_ref[rows, :] = before

    requests = len_ref.shape[1]
    down_it = lax.broadcasted_iota(jnp.int32, (requests, requests), 0)
    along = lax.broadcasted_iota(jnp.int32, (requests, requests), 1)
    length = jnp.broadcast_to(len_ref[...], (requests, requests)).astype(jnp.float32)
    prefix = jnp.broadcast_to(map_ref[...], (requests, requests)).astype(jnp.float32)

    def column(keep, values):
        return jnp.sum(jnp.where(keep, values, 0.0), axis=1, keepdims=True)

    starts = column(along < down_it, length)
    ends = column(along <= down_it, length)
    prefixes = column(along == down_it, prefix)
    number = lax.broadcasted_iota(jnp.int32, (requests, LANES), 0).astype(jnp.float32) + 1.0
    first = place_ref[0] * (PAIRS * ROWS) - ROWS
    for b in range(PAIRS + 2):
        ids = lax.broadcasted_iota(jnp.int32, (requests, LANES), 1) + (first + b * ROWS)
        ids = ids.astype(jnp.float32)
        member = (ids >= starts) & (ids < ends)
        request = jnp.sum(jnp.where(member, number, 0.0), axis=0, keepdims=True) - 1.0
        offset = ids[0:1] - jnp.sum(jnp.where(member, starts, 0.0), axis=0, keepdims=True)
        chosen = jnp.sum(jnp.where(member, prefixes, 0.0), axis=0, keepdims=True)
        meta_ref[b] = jnp.concatenate([request, offset, chosen] + [request] * 5, axis=0)


def tables(place, rel_bias, lengths, prefix_map):
    return pl.pallas_call(
        tables_kernel,
        in_specs=[SMEM_SPEC, SMEM_SPEC, VMEM_SPEC, VMEM_SPEC],
        out_specs=(VMEM_SPEC,) * 3,
        out_shape=(
            pltpu.VMEM((2 * ROWS, 3 * LANES), jnp.float32),
            pltpu.VMEM((2 * ROWS, LANES), jnp.float32),
            pltpu.VMEM((PAIRS + 2, 8, ROWS), jnp.float32),
        ),
        compiler_params=pltpu.CompilerParams(vmem_limit_bytes=VMEM_LIMIT),
        name="tables",
    )(place, rel_bias.T, *on_chip(lengths, prefix_map))


def attend_kernel(
    place_ref, got_ref, prev_ref, next_ref, far_ref, near_ref, line_ref, meta_ref, out_ref, keys, values, kwin, vwin
):
    lane = lax.broadcasted_iota(jnp.int32, (ROWS, LANES), 1)
    low = lane < DK
    for b in range(PAIRS + 2):
        if b == 0:
            key, value = prev_ref[QUARTER : QUARTER + ROWS], prev_ref[QUARTER + ROWS :]
        elif b == PAIRS + 1:
            key, value = next_ref[QUARTER : QUARTER + ROWS], next_ref[QUARTER + ROWS :]
        else:
            key, value = got_ref[b - 1, ROWS : 2 * ROWS], got_ref[b - 1, 2 * ROWS : 3 * ROWS]
        kwin[b] = jnp.transpose(key)
        vwin[b] = value
    for turn, ref in ((0, None), (3, prev_ref), (1, next_ref), (2, far_ref)):
        quarter = lax.rem(place_ref[0] + turn, 4)
        for p in range(PREF_GRP):
            pieces = [[], []]
            for source in range(PAIRS):
                for kind in range(2):
                    at = (kind * PREF_GRP + p) * SHARE
                    if ref is None:
                        piece = got_ref[source, 3 * ROWS + at : 3 * ROWS + at + SHARE]
                    else:
                        at = at + source * 4 * SHARE
                        piece = ref[at : at + SHARE]
                    pieces[kind].append(piece)
            keys[quarter, p * LANES : (p + 1) * LANES] = jnp.transpose(jnp.concatenate(pieces[0], axis=0))
            values[quarter, :, p * LANES : (p + 1) * LANES] = jnp.concatenate(pieces[1], axis=0)

    def one(step, _):
        query = got_ref[step, 0:ROWS]
        own = jnp.transpose(meta_ref[step + 1])
        request, offset, chosen = own[:, 0:1], own[:, 1:2], own[:, 2:3]
        zero = jnp.zeros_like(query)
        stacked = jnp.concatenate([jnp.where(low, query, zero), jnp.where(low, zero, query)], axis=0)
        second = jnp.concatenate([chosen, chosen], axis=0) > 0.5
        zeros = jnp.zeros_like(stacked)
        split = jnp.concatenate(
            [jnp.where(second, zeros, stacked), jnp.where(second, stacked, zeros)], axis=1
        )
        far_keys = jnp.concatenate([keys[b] for b in range(4)], axis=1)
        far_scores = jnp.dot(split, far_keys, preferred_element_type=jnp.float32)
        near_keys = jnp.concatenate([kwin[step + b] for b in range(3)], axis=1)
        near_scores = jnp.dot(stacked, near_keys, preferred_element_type=jnp.float32)
        tail_at = jnp.minimum(LANES - lane + offset.astype(jnp.int32), LANES - 1)
        line = line_ref[...]
        tail = jnp.take_along_axis(line, jnp.concatenate([tail_at, tail_at], axis=0), axis=1)
        full = line[:, LANES - 1 :]
        parts = [far_scores[:, b * LANES : (b + 1) * LANES] + full for b in range(3)]
        parts.append(far_scores[:, 3 * LANES :] + tail)
        for b in range(3):
            mine = meta_ref[step + b, 0:1, :] == request
            mine = jnp.concatenate([mine, mine], axis=0)
            at = slice(b * LANES, (b + 1) * LANES)
            parts.append(jnp.where(mine, near_scores[:, at] + near_ref[:, at], masked_score))
        row_max = jnp.max(functools.reduce(jnp.maximum, parts), axis=1, keepdims=True)
        terms = [jnp.exp(part - row_max) for part in parts]
        row_sum = jnp.sum(functools.reduce(jnp.add, terms), axis=1, keepdims=True)
        weights = [t.astype(jnp.bfloat16) for t in terms]
        far_out = jnp.dot(
            jnp.concatenate(weights[:4], axis=1),
            values[...].reshape(PLEN, PREF_GRP * LANES),
            preferred_element_type=jnp.float32,
        )
        near_values = jnp.concatenate([vwin[step + b] for b in range(3)], axis=0)
        near_out = jnp.dot(
            jnp.concatenate(weights[4:], axis=1), near_values, preferred_element_type=jnp.float32
        )
        total = jnp.where(second, far_out[:, LANES:], far_out[:, :LANES]) + near_out
        total = total / row_sum
        out_ref[step] = jnp.where(low, total[:ROWS], total[ROWS:]).astype(jnp.bfloat16)
        return 0

    lax.fori_loop(0, PAIRS, one, 0)


def attend(place, got, prev, after_it, far, made):
    return pl.pallas_call(
        attend_kernel,
        in_specs=[SMEM_SPEC] + [VMEM_SPEC] * 7,
        out_specs=VMEM_SPEC,
        out_shape=pltpu.VMEM((PAIRS, ROWS, LANES), jnp.bfloat16),
        scratch_shapes=[
            pltpu.VMEM((4, PREF_GRP * LANES, PLEN // 4), jnp.bfloat16),
            pltpu.VMEM((4, PLEN // 4, PREF_GRP * LANES), jnp.bfloat16),
            pltpu.VMEM((PAIRS + 2, LANES, ROWS), jnp.bfloat16),
            pltpu.VMEM((PAIRS + 2, ROWS, LANES), jnp.bfloat16),
        ],
        compiler_params=pltpu.CompilerParams(vmem_limit_bytes=VMEM_LIMIT),
        name="attend",
    )(place, *on_chip(got, prev, after_it, far, *made))


def join_kernel(att_ref, w_ref, tok_ref, gain_ref, hidden_ref, normed_ref):
    attended = jnp.concatenate([att_ref[j] for j in range(PAIRS)], axis=1)
    got = jnp.dot(attended, w_ref[...], preferred_element_type=jnp.float32)
    hidden = (tok_ref[...].astype(jnp.float32) + got).astype(jnp.bfloat16)
    hidden_ref[...] = hidden
    normed_ref[...] = norm_rows(hidden, gain_ref[...])


def join(att, w_attn_out, tokens, gain):
    shape = pltpu.VMEM((ROWS, D), jnp.bfloat16)
    return pl.pallas_call(
        join_kernel,
        in_specs=[VMEM_SPEC] * 4,
        out_specs=(VMEM_SPEC,) * 2,
        out_shape=(shape, shape),
        compiler_params=pltpu.CompilerParams(vmem_limit_bytes=VMEM_LIMIT),
        name="join",
    )(*on_chip(att, w_attn_out, tokens, gain.reshape(1, D)))


def feed_kernel(one_ref, two_ref, in_ref, out_ref, first_ref, second_ref):
    two = two_ref[...] if len(two_ref.shape) == 2 else two_ref[0]
    rows = jnp.concatenate([one_ref[...], two], axis=0)
    units = lax.dot_general(
        rows, in_ref[...], (((1,), (1,)), ((), ())), preferred_element_type=jnp.float32
    )
    units = jnp.maximum(units, 0.0).astype(jnp.bfloat16)
    got = jnp.dot(units, out_ref[...], preferred_element_type=jnp.float32).astype(jnp.bfloat16)
    first_ref[...] = got[:ROWS]
    second_ref[...] = got[ROWS:]


def feed(one, two, w_in, w_out):
    shape = pltpu.VMEM((ROWS, D), jnp.bfloat16)
    return pl.pallas_call(
        feed_kernel,
        in_specs=[VMEM_SPEC] * 4,
        out_specs=(VMEM_SPEC,) * 2,
        out_shape=(shape, shape),
        compiler_params=pltpu.CompilerParams(vmem_limit_bytes=VMEM_LIMIT),
        name="feed",
    )(*on_chip(one, two, w_in, w_out))


def pack_kernel(one_ref, two_ref, out_ref):
    out_ref[0] = one_ref[...]
    out_ref[1] = two_ref[...]


def pack(one, two):
    return pl.pallas_call(
        pack_kernel,
        in_specs=[VMEM_SPEC] * 2,
        out_specs=VMEM_SPEC,
        out_shape=pltpu.VMEM((2,) + one.shape, one.dtype),
        compiler_params=pltpu.CompilerParams(vmem_limit_bytes=VMEM_LIMIT),
        name="pack",
    )(*on_chip(one, two))


def total_kernel(*refs):
    out_ref = refs[-1]
    values = [ref[...] if len(ref.shape) == 2 else ref[1] for ref in refs[:-1]]
    total = functools.reduce(jnp.add, [value.astype(jnp.float32) for value in values])
    out_ref[...] = total.astype(out_ref.dtype)


def total(dtype, *arrays, last=False):
    return pl.pallas_call(
        total_kernel,
        in_specs=[VMEM_SPEC] * len(arrays),
        out_specs=VMEM_SPEC,
        out_shape=(jax.ShapeDtypeStruct if last else pltpu.VMEM)(arrays[0].shape, dtype),
        compiler_params=pltpu.CompilerParams(vmem_limit_bytes=VMEM_LIMIT),
        name="total",
    )(*on_chip(*arrays))


def body(
    tokens,
    attn_gain,
    w_query,
    w_key,
    w_value,
    w_attn_out,
    rel_bias,
    prefix_cache,
    lengths,
    prefix_map,
    mlp_gain,
    w_in,
    w_out,
):
    count_x = lax.axis_size("x")
    plane = lax.axis_index("z") * 2 + lax.axis_index("ylo")
    place = jnp.stack([lax.axis_index("x"), plane]).astype(jnp.int32)
    made = tables(place, rel_bias, lengths, prefix_map)

    blocks = project(tokens, attn_gain, w_query, w_key, w_value, prefix_cache)
    got = lax.all_to_all(blocks, PLANE, 0, 0, tiled=True)
    up, down, far = spread(got)
    by = lambda d: [(i, (i + d) % count_x) for i in range(count_x)]
    prev = lax.ppermute(up, "x", by(1))
    later = lax.ppermute(down, "x", by(-1))
    opposite = lax.ppermute(far, "x", by(2))
    mixed = attend(place, got, prev, later, opposite, made)
    att = lax.all_to_all(mixed, PLANE, 0, 0, tiled=True)
    hidden, normed = join(att, w_attn_out, tokens, mlp_gain)

    mirrored = ("yhi", "ylo")
    far = lax.ppermute(normed, mirrored, MIRROR)
    other = lax.ppermute(normed, "core", SWAP)
    mine, theirs = feed(normed, other, w_in, w_out)
    pair_swap = lax.ppermute(pack(far, theirs), "core", SWAP)
    far_mine, far_theirs = feed(far, pair_swap, w_in, w_out)
    far_sum = total(jnp.bfloat16, far_mine, lax.ppermute(far_theirs, "core", SWAP))
    back = lax.ppermute(far_sum, mirrored, MIRROR)
    local = total(jnp.float32, hidden, mine, pair_swap)
    return total(jnp.bfloat16, local, back, last=True)


def solution(mesh):
    split = Mesh(mesh.devices.reshape(2, 2, 4, 4, 2), AXES)
    grp, req = ("yhi", "core"), REQ
    return jax.shard_map(
        body,
        mesh=split,
        in_specs=(
            P(grp + req, None),
            P(),
            P(),
            P(),
            P(),
            P(),
            P(),
            P(grp, req, None),
            P(grp, None),
            P(grp, None),
            P(),
            P(grp, None),
            P(grp, None),
        ),
        out_specs=P(grp + req, None),
        check_vma=False,
    )
```

```python
import functools

import jax
import jax.numpy as jnp
from jax import lax
from jax.experimental import pallas as pl
from jax.experimental.pallas import tpu as pltpu
from jax.sharding import Mesh, PartitionSpec as P

D = 1024
H = 16
DK = 64
PLEN = 512
PREF_GRP = 2
ROWS = 128
PAIRS = 8
LANES = 128
CHUNK = 512
SHARE = 16
SENT = 3 * ROWS + 2 * PREF_GRP * SHARE
QUARTER = PAIRS * 2 * PREF_GRP * SHARE

epsilon = 1e-06
far_marks = (12, 16, 23, 32, 46, 64, 91)
masked_score = -1e30
VMEM_LIMIT = 16 * 1024 * 1024

AXES = ("yhi", "core", "x", "z", "ylo")
REQ = ("x", "z", "ylo")
PLANE = ("z", "ylo")
MIRROR = [(0, 3), (3, 0), (1, 2), (2, 1)]
SWAP = [(0, 1), (1, 0)]


def norm_rows(values_in, gain):
    widened = values_in.astype(jnp.float32)
    scale = lax.rsqrt(jnp.mean(widened * widened, axis=-1, keepdims=True) + epsilon)
    return (widened * scale * gain).astype(jnp.bfloat16)


def on_chip(*arrays):
    return tuple(pltpu.with_memory_space_constraint(a, pltpu.VMEM) for a in arrays)


VMEM_SPEC = pl.BlockSpec(memory_space=pltpu.VMEM)
SMEM_SPEC = pl.BlockSpec(memory_space=pltpu.SMEM)


def project_kernel(
    tok_hbm, gain_hbm, cache_hbm, wq_hbm, wk_hbm, wv_hbm, out_ref, tok, gain, cache, held, arrived, landed
):
    columns = [slice(c * CHUNK, (c + 1) * CHUNK) for c in range(D // CHUNK)]
    first = [
        pltpu.make_async_copy(source, target, landed.at[i])
        for i, (source, target) in enumerate(((tok_hbm, tok), (gain_hbm, gain), (cache_hbm, cache)))
    ]
    copies = [
        [
            pltpu.make_async_copy(w_hbm.at[:, cut], held.at[kind, c], arrived.at[kind, c])
            for c, cut in enumerate(columns)
        ]
        for kind, w_hbm in enumerate((wq_hbm, wk_hbm, wv_hbm))
    ]
    for copy in first:
        copy.start()
    for row in copies:
        for copy in row:
            copy.start()
    for copy in first:
        copy.wait()
    normed = norm_rows(tok[...], gain[...])
    for part in range(PAIRS):
        for kind in range(2):
            for p in range(PREF_GRP):
                at = 3 * ROWS + (kind * PREF_GRP + p) * SHARE
                cut = slice(kind * D + part * LANES, kind * D + (part + 1) * LANES)
                out_ref[part, at : at + SHARE] = cache[p, :, cut]
    for kind, row in enumerate(copies):
        for c, copy in enumerate(row):
            copy.wait()
            got = jnp.dot(normed, held[kind, c], preferred_element_type=jnp.float32)
            got = got.astype(jnp.bfloat16)
            for part in range(CHUNK // LANES):
                to = c * (CHUNK // LANES) + part
                out_ref[to, kind * ROWS : (kind + 1) * ROWS] = got[:, part * LANES : (part + 1) * LANES]


def project(tokens, gain, w_query, w_key, w_value, prefix_cache):
    operands = (tokens, gain.reshape(1, D), prefix_cache, w_query, w_key, w_value)
    return pl.pallas_call(
        project_kernel,
        in_specs=[pl.BlockSpec(memory_space=pltpu.HBM)] * 6,
        out_specs=VMEM_SPEC,
        out_shape=pltpu.VMEM((PAIRS, SENT, LANES), jnp.bfloat16),
        scratch_shapes=[
            pltpu.VMEM((ROWS, D), jnp.bfloat16),
            pltpu.VMEM((1, D), jnp.float32),
            pltpu.VMEM(prefix_cache.shape, jnp.bfloat16),
            pltpu.VMEM((3, D // CHUNK, D, CHUNK), jnp.bfloat16),
            pltpu.SemaphoreType.DMA((3, D // CHUNK)),
            pltpu.SemaphoreType.DMA((3,)),
        ],
        compiler_params=pltpu.CompilerParams(vmem_limit_bytes=VMEM_LIMIT),
        name="project",
    )(*(pltpu.with_memory_space_constraint(a, pltpu.HBM) for a in operands))


def spread_kernel(got_ref, tok_ref, up_ref, down_ref, far_ref, same_ref):
    same_ref[...] = tok_ref[...]
    for source in range(PAIRS):
        rows = slice(source * 4 * SHARE, (source + 1) * 4 * SHARE)
        held = got_ref[source, 3 * ROWS :]
        up_ref[rows] = held
        down_ref[rows] = held
        far_ref[rows] = held
    up_ref[QUARTER:] = got_ref[PAIRS - 1, ROWS : 3 * ROWS]
    down_ref[QUARTER:] = got_ref[0, ROWS : 3 * ROWS]


def spread(got, tokens):
    shape = pltpu.VMEM((QUARTER + 2 * ROWS, LANES), jnp.bfloat16)
    return pl.pallas_call(
        spread_kernel,
        in_specs=[VMEM_SPEC] * 2,
        out_specs=(VMEM_SPEC,) * 4,
        out_shape=(
            shape,
            shape,
            pltpu.VMEM((QUARTER, LANES), jnp.bfloat16),
            pltpu.VMEM((ROWS, D), jnp.bfloat16),
        ),
        compiler_params=pltpu.CompilerParams(vmem_limit_bytes=VMEM_LIMIT),
        name="spread",
    )(*on_chip(got, tokens))


def bias_line(rel_ref, head, first_bucket):
    lane = lax.broadcasted_iota(jnp.int32, (ROWS, LANES), 1)
    line = jnp.full((ROWS, LANES), rel_ref[head, first_bucket], jnp.float32)
    for bucket in range(1, 16):
        mark = bucket if bucket <= 8 else far_marks[bucket - 9]
        line = jnp.where(lane >= mark, rel_ref[head, first_bucket + bucket], line)
    return line


def tables_kernel(place_ref, rel_ref, len_ref, map_ref, near_ref, line_ref, meta_ref):
    row = lax.broadcasted_iota(jnp.int32, (ROWS, LANES), 0)
    lane = lax.broadcasted_iota(jnp.int32, (ROWS, LANES), 1)
    for h in range(2):
        head = place_ref[1] * 2 + h
        before = bias_line(rel_ref, head, 0)
        after_it = bias_line(rel_ref, head, 16)

        def pick(line, distance):
            return jnp.take_along_axis(line, jnp.clip(distance, 0, LANES - 1), axis=1)

        rows = slice(h * ROWS, (h + 1) * ROWS)
        near_ref[rows, 0:LANES] = pick(before, row + LANES - lane)
        near_ref[rows, LANES : 2 * LANES] = jnp.where(
            lane > row, pick(after_it, lane - row), pick(before, row - lane)
        )
        near_ref[rows, 2 * LANES : 3 * LANES] = pick(after_it, lane + LANES - row)
        line_ref[rows, :] = before

    requests = len_ref.shape[1]
    down_it = lax.broadcasted_iota(jnp.int32, (requests, requests), 0)
    along = lax.broadcasted_iota(jnp.int32, (requests, requests), 1)
    length = jnp.broadcast_to(len_ref[...], (requests, requests)).astype(jnp.float32)
    prefix = jnp.broadcast_to(map_ref[...], (requests, requests)).astype(jnp.float32)

    def column(keep, values):
        return jnp.sum(jnp.where(keep, values, 0.0), axis=1, keepdims=True)

    starts = column(along < down_it, length)
    ends = column(along <= down_it, length)
    prefixes = column(along == down_it, prefix)
    number = lax.broadcasted_iota(jnp.int32, (requests, LANES), 0).astype(jnp.float32) + 1.0
    first = place_ref[0] * (PAIRS * ROWS) - ROWS
    for b in range(PAIRS + 2):
        ids = lax.broadcasted_iota(jnp.int32, (requests, LANES), 1) + (first + b * ROWS)
        ids = ids.astype(jnp.float32)
        member = (ids >= starts) & (ids < ends)
        request = jnp.sum(jnp.where(member, number, 0.0), axis=0, keepdims=True) - 1.0
        offset = ids[0:1] - jnp.sum(jnp.where(member, starts, 0.0), axis=0, keepdims=True)
        chosen = jnp.sum(jnp.where(member, prefixes, 0.0), axis=0, keepdims=True)
        meta_ref[b] = jnp.concatenate([request, offset, chosen] + [request] * 5, axis=0)


def tables(place, rel_bias, lengths, prefix_map):
    return pl.pallas_call(
        tables_kernel,
        in_specs=[SMEM_SPEC, SMEM_SPEC, VMEM_SPEC, VMEM_SPEC],
        out_specs=(VMEM_SPEC,) * 3,
        out_shape=(
            pltpu.VMEM((2 * ROWS, 3 * LANES), jnp.float32),
            pltpu.VMEM((2 * ROWS, LANES), jnp.float32),
            pltpu.VMEM((PAIRS + 2, 8, ROWS), jnp.float32),
        ),
        compiler_params=pltpu.CompilerParams(vmem_limit_bytes=VMEM_LIMIT),
        name="tables",
    )(place, rel_bias.T, *on_chip(lengths, prefix_map))


def attend_kernel(
    place_ref,
    got_ref,
    prev_ref,
    next_ref,
    far_ref,
    near_ref,
    line_ref,
    meta_ref,
    _,
    w1_hbm,
    w2_hbm,
    w3_hbm,
    out_ref,
    w1_ref,
    w2_ref,
    w3_ref,
    keys,
    values,
    kwin,
    vwin,
    landed,
):
    copies = [
        pltpu.make_async_copy(source, target, landed.at[i])
        for i, (source, target) in enumerate(((w1_hbm, w1_ref), (w2_hbm, w2_ref), (w3_hbm, w3_ref)))
    ]
    for copy in copies:
        copy.start()
    lane = lax.broadcasted_iota(jnp.int32, (ROWS, LANES), 1)
    low = lane < DK
    for b in range(PAIRS + 2):
        if b == 0:
            key, value = prev_ref[QUARTER : QUARTER + ROWS], prev_ref[QUARTER + ROWS :]
        elif b == PAIRS + 1:
            key, value = next_ref[QUARTER : QUARTER + ROWS], next_ref[QUARTER + ROWS :]
        else:
            key, value = got_ref[b - 1, ROWS : 2 * ROWS], got_ref[b - 1, 2 * ROWS : 3 * ROWS]
        kwin[b] = jnp.transpose(key)
        vwin[b] = value
    for turn, ref in ((0, None), (3, prev_ref), (1, next_ref), (2, far_ref)):
        quarter = lax.rem(place_ref[0] + turn, 4)
        for p in range(PREF_GRP):
            pieces = [[], []]
            for source in range(PAIRS):
                for kind in range(2):
                    at = (kind * PREF_GRP + p) * SHARE
                    if ref is None:
                        piece = got_ref[source, 3 * ROWS + at : 3 * ROWS + at + SHARE]
                    else:
                        at = at + source * 4 * SHARE
                        piece = ref[at : at + SHARE]
                    pieces[kind].append(piece)
            keys[quarter, p * LANES : (p + 1) * LANES] = jnp.transpose(jnp.concatenate(pieces[0], axis=0))
            values[quarter, :, p * LANES : (p + 1) * LANES] = jnp.concatenate(pieces[1], axis=0)

    def one(step, _):
        query = got_ref[step, 0:ROWS]
        own = jnp.transpose(meta_ref[step + 1])
        request, offset, chosen = own[:, 0:1], own[:, 1:2], own[:, 2:3]
        zero = jnp.zeros_like(query)
        stacked = jnp.concatenate([jnp.where(low, query, zero), jnp.where(low, zero, query)], axis=0)
        second = jnp.concatenate([chosen, chosen], axis=0) > 0.5
        zeros = jnp.zeros_like(stacked)
        split = jnp.concatenate(
            [jnp.where(second, zeros, stacked), jnp.where(second, stacked, zeros)], axis=1
        )
        far_keys = jnp.concatenate([keys[b] for b in range(4)], axis=1)
        far_scores = jnp.dot(split, far_keys, preferred_element_type=jnp.float32)
        near_keys = jnp.concatenate([kwin[step + b] for b in range(3)], axis=1)
        near_scores = jnp.dot(stacked, near_keys, preferred_element_type=jnp.float32)
        tail_at = jnp.minimum(LANES - lane + offset.astype(jnp.int32), LANES - 1)
        line = line_ref[...]
        tail = jnp.take_along_axis(line, jnp.concatenate([tail_at, tail_at], axis=0), axis=1)
        full = line[:, LANES - 1 :]
        parts = [far_scores[:, b * LANES : (b + 1) * LANES] + full for b in range(3)]
        parts.append(far_scores[:, 3 * LANES :] + tail)
        for b in range(3):
            mine = meta_ref[step + b, 0:1, :] == request
            mine = jnp.concatenate([mine, mine], axis=0)
            at = slice(b * LANES, (b + 1) * LANES)
            parts.append(jnp.where(mine, near_scores[:, at] + near_ref[:, at], masked_score))
        row_max = jnp.max(functools.reduce(jnp.maximum, parts), axis=1, keepdims=True)
        terms = [jnp.exp(part - row_max) for part in parts]
        row_sum = jnp.sum(functools.reduce(jnp.add, terms), axis=1, keepdims=True)
        weights = [t.astype(jnp.bfloat16) for t in terms]
        far_out = jnp.dot(
            jnp.concatenate(weights[:4], axis=1),
            values[...].reshape(PLEN, PREF_GRP * LANES),
            preferred_element_type=jnp.float32,
        )
        near_values = jnp.concatenate([vwin[step + b] for b in range(3)], axis=0)
        near_out = jnp.dot(
            jnp.concatenate(weights[4:], axis=1), near_values, preferred_element_type=jnp.float32
        )
        total = jnp.where(second, far_out[:, LANES:], far_out[:, :LANES]) + near_out
        total = total / row_sum
        done = jnp.where(low, total[:ROWS], total[ROWS:]).astype(jnp.bfloat16)
        side = place_ref[2]
        out_ref[side * PAIRS + step] = done
        out_ref[(1 - side) * PAIRS + jnp.bitwise_xor(step, 1)] = done
        return 0

    lax.fori_loop(0, PAIRS, one, 0)
    for copy in copies:
        copy.wait()


def attend(place, got, prev, after_it, far, made, ready, later_weights):
    hbm = pl.BlockSpec(memory_space=pltpu.HBM)
    return pl.pallas_call(
        attend_kernel,
        in_specs=[SMEM_SPEC] + [VMEM_SPEC] * 8 + [hbm] * 3,
        out_specs=(VMEM_SPEC,) * 4,
        out_shape=(pltpu.VMEM((2 * PAIRS, ROWS, LANES), jnp.bfloat16),)
        + tuple(pltpu.VMEM(w.shape, w.dtype) for w in later_weights),
        scratch_shapes=[
            pltpu.VMEM((4, PREF_GRP * LANES, PLEN // 4), jnp.bfloat16),
            pltpu.VMEM((4, PLEN // 4, PREF_GRP * LANES), jnp.bfloat16),
            pltpu.VMEM((PAIRS + 2, LANES, ROWS), jnp.bfloat16),
            pltpu.VMEM((PAIRS + 2, ROWS, LANES), jnp.bfloat16),
            pltpu.SemaphoreType.DMA((3,)),
        ],
        compiler_params=pltpu.CompilerParams(vmem_limit_bytes=VMEM_LIMIT),
        name="attend",
    )(
        place,
        *on_chip(got, prev, after_it, far, *made, ready),
        *(pltpu.with_memory_space_constraint(w, pltpu.HBM) for w in later_weights),
    )


def join_kernel(place_ref, att_ref, w_ref, tok_ref, far_tok_ref, gain_ref, hidden_ref, normed_ref):
    side = place_ref[2]
    halves = [
        jnp.concatenate([att_ref[at * PAIRS + j] for j in range(PAIRS)], axis=1) for at in (side, 1 - side)
    ]
    got = jnp.dot(jnp.concatenate(halves, axis=0), w_ref[...], preferred_element_type=jnp.float32)
    for half, ref in enumerate((tok_ref, far_tok_ref)):
        mine = got[half * ROWS : (half + 1) * ROWS]
        hidden = (ref[...].astype(jnp.float32) + mine).astype(jnp.bfloat16)
        if half == 0:
            hidden_ref[...] = hidden
        normed_ref[half] = norm_rows(hidden, gain_ref[...])


def join(place, att, w_attn_out, tokens, far_tokens, gain):
    return pl.pallas_call(
        join_kernel,
        in_specs=[SMEM_SPEC] + [VMEM_SPEC] * 5,
        out_specs=(VMEM_SPEC,) * 2,
        out_shape=(pltpu.VMEM((ROWS, D), jnp.bfloat16), pltpu.VMEM((2, ROWS, D), jnp.bfloat16)),
        compiler_params=pltpu.CompilerParams(vmem_limit_bytes=VMEM_LIMIT),
        name="join",
    )(place, *on_chip(att, w_attn_out, tokens, far_tokens, gain.reshape(1, D)))


def feed_kernel(picked, rows_ref, in_ref, out_w_ref, *rest):
    out_refs = rest[len(rest) - len(picked) :]
    rows = jnp.concatenate([rows_ref[half] for half in picked], axis=0)
    units = lax.dot_general(
        rows, in_ref[...], (((1,), (1,)), ((), ())), preferred_element_type=jnp.float32
    )
    units = jnp.maximum(units, 0.0).astype(jnp.bfloat16)
    got = jnp.dot(units, out_w_ref[...], preferred_element_type=jnp.float32).astype(jnp.bfloat16)
    for at, ref in enumerate(out_refs):
        ref[...] = got[at * ROWS : (at + 1) * ROWS]


def feed(picked, rows, w_in, w_out, *ready):
    shape = pltpu.VMEM((ROWS, D), jnp.bfloat16)
    return pl.pallas_call(
        functools.partial(feed_kernel, picked),
        in_specs=[VMEM_SPEC] * (3 + len(ready)),
        out_specs=(VMEM_SPEC,) * len(picked),
        out_shape=(shape,) * len(picked),
        compiler_params=pltpu.CompilerParams(vmem_limit_bytes=VMEM_LIMIT),
        name="feed",
    )(*on_chip(rows, w_in, w_out, *ready))


def total_kernel(*refs):
    out_ref = refs[-1]
    total = functools.reduce(jnp.add, [ref[...].astype(jnp.float32) for ref in refs[:-1]])
    out_ref[...] = total.astype(out_ref.dtype)


def total(dtype, *arrays, last=False):
    return pl.pallas_call(
        total_kernel,
        in_specs=[VMEM_SPEC] * len(arrays),
        out_specs=VMEM_SPEC,
        out_shape=(jax.ShapeDtypeStruct if last else pltpu.VMEM)(arrays[0].shape, dtype),
        compiler_params=pltpu.CompilerParams(vmem_limit_bytes=VMEM_LIMIT),
        name="total",
    )(*on_chip(*arrays))


def body(
    tokens,
    attn_gain,
    w_query,
    w_key,
    w_value,
    w_attn_out,
    rel_bias,
    prefix_cache,
    lengths,
    prefix_map,
    mlp_gain,
    w_in,
    w_out,
):
    count_x = lax.axis_size("x")
    plane = lax.axis_index("z") * 2 + lax.axis_index("ylo")
    place = jnp.stack([lax.axis_index("x"), plane, lax.axis_index("yhi")]).astype(jnp.int32)
    made = tables(place, rel_bias, lengths, prefix_map)

    blocks = project(tokens, attn_gain, w_query, w_key, w_value, prefix_cache)
    got = lax.all_to_all(blocks, PLANE, 0, 0, tiled=True)
    up, down, far, same = spread(got, tokens)
    by = lambda d: [(i, (i + d) % count_x) for i in range(count_x)]
    prev = lax.ppermute(up, "x", by(1))
    later = lax.ppermute(down, "x", by(-1))
    opposite = lax.ppermute(far, "x", by(2))
    mirrored = ("yhi", "ylo")
    far_tokens = lax.ppermute(same, mirrored, MIRROR)
    mixed, w_attn_out, w_in, w_out = attend(
        place, got, prev, later, opposite, made, far_tokens, (w_attn_out, w_in, w_out)
    )
    att = lax.all_to_all(mixed, ("yhi",) + PLANE, 0, 0, tiled=True)
    hidden, normed = join(place, att, w_attn_out, tokens, far_tokens, mlp_gain)

    other = lax.ppermute(normed, "core", SWAP)
    mine, far_mine = feed((0, 1), normed, w_in, w_out)
    (far_theirs,) = feed((1,), other, w_in, w_out, mine)
    far_sum = total(jnp.bfloat16, far_mine, lax.ppermute(far_theirs, "core", SWAP))
    back = lax.ppermute(far_sum, mirrored, MIRROR)
    (theirs,) = feed((0,), other, w_in, w_out, far_theirs)
    local = total(jnp.float32, hidden, mine, lax.ppermute(theirs, "core", SWAP))
    return total(jnp.bfloat16, local, back, last=True)


def solution(mesh):
    split = Mesh(mesh.devices.reshape(2, 2, 4, 4, 2), AXES)
    grp, req = ("yhi", "core"), REQ
    return jax.shard_map(
        body,
        mesh=split,
        in_specs=(
            P(grp + req, None),
            P(),
            P(),
            P(),
            P(),
            P(),
            P(),
            P(grp, req, None),
            P(grp, None),
            P(grp, None),
            P(),
            P(grp, None),
            P(grp, None),
        ),
        out_specs=P(grp + req, None),
        check_vma=False,
    )
```

```python
import functools

import jax
import jax.numpy as jnp
from jax import lax
from jax.experimental import pallas as pl
from jax.experimental.pallas import tpu as pltpu
from jax.sharding import Mesh, PartitionSpec as P

D = 1024
H = 16
DK = 64
PLEN = 512
PREF_GRP = 2
ROWS = 128
PAIRS = 8
LANES = 128
CHUNK = 512
SHARE = 16
SENT = 3 * ROWS + 2 * PREF_GRP * SHARE
QUARTER = PAIRS * 2 * PREF_GRP * SHARE

epsilon = 1e-06
far_marks = (12, 16, 23, 32, 46, 64, 91)
masked_score = -1e30
VMEM_LIMIT = 16 * 1024 * 1024
COST = pl.CostEstimate(flops=1000, transcendentals=0, bytes_accessed=1000)

AXES = ("yhi", "core", "x", "z", "ylo")
REQ = ("x", "z", "ylo")
PLANE = ("z", "ylo")
MIRROR = [(0, 3), (3, 0), (1, 2), (2, 1)]
SWAP = [(0, 1), (1, 0)]


def norm_rows(values_in, gain):
    widened = values_in.astype(jnp.float32)
    scale = lax.rsqrt(jnp.mean(widened * widened, axis=-1, keepdims=True) + epsilon)
    return (widened * scale * gain).astype(jnp.bfloat16)


def on_chip(*arrays):
    return tuple(pltpu.with_memory_space_constraint(a, pltpu.VMEM) for a in arrays)


def off_chip(*arrays):
    return tuple(pltpu.with_memory_space_constraint(a, pltpu.HBM) for a in arrays)


VMEM_SPEC = pl.BlockSpec(memory_space=pltpu.VMEM)
HBM_SPEC = pl.BlockSpec(memory_space=pltpu.HBM)
SMEM_SPEC = pl.BlockSpec(memory_space=pltpu.SMEM)


def project_kernel(
    tok_hbm, gain_hbm, cache_hbm, wq_hbm, wk_hbm, wv_hbm, out_ref, tok, gain, cache, held, arrived, landed
):
    columns = [slice(c * CHUNK, (c + 1) * CHUNK) for c in range(D // CHUNK)]
    first = [
        pltpu.make_async_copy(source, target, landed.at[i])
        for i, (source, target) in enumerate(((tok_hbm, tok), (gain_hbm, gain), (cache_hbm, cache)))
    ]
    copies = [
        [
            pltpu.make_async_copy(w_hbm.at[:, cut], held.at[kind, c], arrived.at[kind, c])
            for c, cut in enumerate(columns)
        ]
        for kind, w_hbm in enumerate((wq_hbm, wk_hbm, wv_hbm))
    ]
    for copy in first:
        copy.start()
    for row in copies:
        for copy in row:
            copy.start()
    for copy in first:
        copy.wait()
    normed = norm_rows(tok[...], gain[...])
    for part in range(PAIRS):
        for kind in range(2):
            for p in range(PREF_GRP):
                at = 3 * ROWS + (kind * PREF_GRP + p) * SHARE
                cut = slice(kind * D + part * LANES, kind * D + (part + 1) * LANES)
                out_ref[part, at : at + SHARE] = cache[p, :, cut]
    for kind, row in enumerate(copies):
        for c, copy in enumerate(row):
            copy.wait()
            got = jnp.dot(normed, held[kind, c], preferred_element_type=jnp.float32)
            got = got.astype(jnp.bfloat16)
            for part in range(CHUNK // LANES):
                to = c * (CHUNK // LANES) + part
                out_ref[to, kind * ROWS : (kind + 1) * ROWS] = got[:, part * LANES : (part + 1) * LANES]


def project(tokens, gain, w_query, w_key, w_value, prefix_cache):
    operands = (tokens, gain.reshape(1, D), prefix_cache, w_query, w_key, w_value)
    return pl.pallas_call(
        project_kernel,
        in_specs=[HBM_SPEC] * 6,
        out_specs=VMEM_SPEC,
        out_shape=pltpu.HBM((PAIRS, SENT, LANES), jnp.bfloat16),
        scratch_shapes=[
            pltpu.VMEM((ROWS, D), jnp.bfloat16),
            pltpu.VMEM((1, D), jnp.float32),
            pltpu.VMEM(prefix_cache.shape, jnp.bfloat16),
            pltpu.VMEM((3, D // CHUNK, D, CHUNK), jnp.bfloat16),
            pltpu.SemaphoreType.DMA((3, D // CHUNK)),
            pltpu.SemaphoreType.DMA((3,)),
        ],
        compiler_params=pltpu.CompilerParams(vmem_limit_bytes=VMEM_LIMIT),
        cost_estimate=COST,
        name="project",
    )(*off_chip(*operands))


def spread_kernel(got_ref, *rest):
    up_ref, down_ref, far_ref = rest[-3:]
    for source in range(PAIRS):
        rows = slice(source * 4 * SHARE, (source + 1) * 4 * SHARE)
        held = got_ref[source, 3 * ROWS :]
        up_ref[rows] = held
        down_ref[rows] = held
        far_ref[rows] = held
    up_ref[QUARTER:] = got_ref[PAIRS - 1, ROWS : 3 * ROWS]
    down_ref[QUARTER:] = got_ref[0, ROWS : 3 * ROWS]


def spread(got, *ready):
    shape = pltpu.VMEM((QUARTER + 2 * ROWS, LANES), jnp.bfloat16)
    return pl.pallas_call(
        spread_kernel,
        in_specs=[VMEM_SPEC] * (1 + len(ready)),
        out_specs=(VMEM_SPEC,) * 3,
        out_shape=(shape, shape, pltpu.VMEM((QUARTER, LANES), jnp.bfloat16)),
        compiler_params=pltpu.CompilerParams(vmem_limit_bytes=VMEM_LIMIT),
        cost_estimate=COST,
        name="spread",
    )(*on_chip(got, *ready))


def bias_line(rel_ref, head, first_bucket):
    lane = lax.broadcasted_iota(jnp.int32, (ROWS, LANES), 1)
    line = jnp.full((ROWS, LANES), rel_ref[head, first_bucket], jnp.float32)
    for bucket in range(1, 16):
        mark = bucket if bucket <= 8 else far_marks[bucket - 9]
        line = jnp.where(lane >= mark, rel_ref[head, first_bucket + bucket], line)
    return line


def tables_kernel(place_ref, rel_ref, len_ref, map_ref, near_ref, line_ref, meta_ref):
    row = lax.broadcasted_iota(jnp.int32, (ROWS, LANES), 0)
    lane = lax.broadcasted_iota(jnp.int32, (ROWS, LANES), 1)
    for h in range(2):
        head = place_ref[1] * 2 + h
        before = bias_line(rel_ref, head, 0)
        after_it = bias_line(rel_ref, head, 16)

        def pick(line, distance):
            return jnp.take_along_axis(line, jnp.clip(distance, 0, LANES - 1), axis=1)

        rows = slice(h * ROWS, (h + 1) * ROWS)
        near_ref[rows, 0:LANES] = pick(before, row + LANES - lane)
        near_ref[rows, LANES : 2 * LANES] = jnp.where(
            lane > row, pick(after_it, lane - row), pick(before, row - lane)
        )
        near_ref[rows, 2 * LANES : 3 * LANES] = pick(after_it, lane + LANES - row)
        line_ref[rows, :] = before

    requests = len_ref.shape[1]
    down_it = lax.broadcasted_iota(jnp.int32, (requests, requests), 0)
    along = lax.broadcasted_iota(jnp.int32, (requests, requests), 1)
    length = jnp.broadcast_to(len_ref[...], (requests, requests)).astype(jnp.float32)
    prefix = jnp.broadcast_to(map_ref[...], (requests, requests)).astype(jnp.float32)

    def column(keep, values):
        return jnp.sum(jnp.where(keep, values, 0.0), axis=1, keepdims=True)

    starts = column(along < down_it, length)
    ends = column(along <= down_it, length)
    prefixes = column(along == down_it, prefix)
    number = lax.broadcasted_iota(jnp.int32, (requests, LANES), 0).astype(jnp.float32) + 1.0
    first = place_ref[0] * (PAIRS * ROWS) - ROWS
    for b in range(PAIRS + 2):
        ids = lax.broadcasted_iota(jnp.int32, (requests, LANES), 1) + (first + b * ROWS)
        ids = ids.astype(jnp.float32)
        member = (ids >= starts) & (ids < ends)
        request = jnp.sum(jnp.where(member, number, 0.0), axis=0, keepdims=True) - 1.0
        offset = ids[0:1] - jnp.sum(jnp.where(member, starts, 0.0), axis=0, keepdims=True)
        chosen = jnp.sum(jnp.where(member, prefixes, 0.0), axis=0, keepdims=True)
        meta_ref[b] = jnp.concatenate([request, offset, chosen] + [request] * 5, axis=0)


def tables(place, rel_bias, lengths, prefix_map):
    return pl.pallas_call(
        tables_kernel,
        in_specs=[SMEM_SPEC, SMEM_SPEC, VMEM_SPEC, VMEM_SPEC],
        out_specs=(VMEM_SPEC,) * 3,
        out_shape=(
            pltpu.VMEM((2 * ROWS, 3 * LANES), jnp.float32),
            pltpu.VMEM((2 * ROWS, LANES), jnp.float32),
            pltpu.VMEM((PAIRS + 2, 8, ROWS), jnp.float32),
        ),
        compiler_params=pltpu.CompilerParams(vmem_limit_bytes=VMEM_LIMIT),
        cost_estimate=COST,
        name="tables",
    )(place, rel_bias.T, *on_chip(lengths, prefix_map))


def masks_of(meta_ref, step):
    own = jnp.transpose(meta_ref[step + 1])
    second = jnp.concatenate([own[:, 2:3], own[:, 2:3]], axis=0) > 0.5
    return own[:, 0:1], own[:, 1:2], second


def queries(got_ref, step, second):
    lane = lax.broadcasted_iota(jnp.int32, (ROWS, LANES), 1)
    query = got_ref[step, 0:ROWS]
    zero = jnp.zeros_like(query)
    stacked = jnp.concatenate(
        [jnp.where(lane < DK, query, zero), jnp.where(lane < DK, zero, query)], axis=0
    )
    zeros = jnp.zeros_like(stacked)
    split = jnp.concatenate(
        [jnp.where(second, zeros, stacked), jnp.where(second, stacked, zeros)], axis=1
    )
    return stacked, split


def prefix_bias(line_ref, offset):
    lane = lax.broadcasted_iota(jnp.int32, (ROWS, LANES), 1)
    at = jnp.minimum(LANES - lane + offset.astype(jnp.int32), LANES - 1)
    line = line_ref[...]
    tail = jnp.take_along_axis(line, jnp.concatenate([at, at], axis=0), axis=1)
    return tail, line[:, LANES - 1 :]


def quarter_of(rows_at, keys_ref, values_ref):
    for p in range(PREF_GRP):
        pieces = [
            jnp.concatenate(
                [rows_at(source, (kind * PREF_GRP + p) * SHARE) for source in range(PAIRS)], axis=0
            )
            for kind in range(2)
        ]
        keys_ref[p * LANES : (p + 1) * LANES, :] = jnp.transpose(pieces[0])
        values_ref[:, p * LANES : (p + 1) * LANES] = pieces[1]


def dot(a, b):
    return jnp.dot(a, b, preferred_element_type=jnp.float32)


def start_copies(pairs, landed):
    copies = [pltpu.make_async_copy(a, b, landed.at[i]) for i, (a, b) in enumerate(pairs)]
    for copy in copies:
        copy.start()
    return copies


def own_kernel(
    place_ref, got_ref, near_ref, line_ref, meta_ref, w1_hbm, w2_hbm,
    stat_ref, acc_ref, w1_ref, w2_ref, keys, values, kwin, vwin, landed,
):
    copies = start_copies(((w1_hbm, w1_ref), (w2_hbm, w2_ref)), landed)
    for b in (0, PAIRS + 1):
        kwin[b] = jnp.zeros((LANES, ROWS), jnp.bfloat16)
        vwin[b] = jnp.zeros((ROWS, LANES), jnp.bfloat16)
    for b in range(PAIRS):
        kwin[b + 1] = jnp.transpose(got_ref[b, ROWS : 2 * ROWS])
        vwin[b + 1] = got_ref[b, 2 * ROWS : 3 * ROWS]
    quarter_of(lambda s, at: got_ref[s, 3 * ROWS + at : 3 * ROWS + at + SHARE], keys, values)
    is_last = place_ref[0] == 3

    def one(step, _):
        request, offset, second = masks_of(meta_ref, step)
        stacked, split = queries(got_ref, step, second)
        tail, full = prefix_bias(line_ref, offset)
        parts = [dot(split, keys[...]) + jnp.where(is_last, tail, full)]
        near_scores = dot(stacked, jnp.concatenate([kwin[step + b] for b in range(3)], axis=1))
        for b in range(3):
            at_edge = (step + b == 0) | (step + b == PAIRS + 1)
            names = jnp.where(at_edge, -2.0, meta_ref[step + b, 0:1, :])
            mine = names == request
            mine = jnp.concatenate([mine, mine], axis=0)
            at = slice(b * LANES, (b + 1) * LANES)
            parts.append(jnp.where(mine, near_scores[:, at] + near_ref[:, at], masked_score))
        row_max = jnp.max(functools.reduce(jnp.maximum, parts), axis=1, keepdims=True)
        terms = [jnp.exp(part - row_max) for part in parts]
        row_sum = jnp.sum(functools.reduce(jnp.add, terms), axis=1, keepdims=True)
        weights = [t.astype(jnp.bfloat16) for t in terms]
        far_out = dot(weights[0], values[...])
        near_values = jnp.concatenate([vwin[step + b] for b in range(3)], axis=0)
        acc = jnp.where(second, far_out[:, LANES:], far_out[:, :LANES])
        acc_ref[step] = acc + dot(jnp.concatenate(weights[1:], axis=1), near_values)
        stat_ref[step, :, 0:1] = row_max
        stat_ref[step, :, 1:2] = row_sum
        return 0

    lax.fori_loop(0, PAIRS, one, 0, unroll=2)
    for copy in copies:
        copy.wait()


def attend_own(place, got, made, later_weights):
    return pl.pallas_call(
        own_kernel,
        in_specs=[SMEM_SPEC] + [VMEM_SPEC] * 4 + [HBM_SPEC] * 2,
        out_specs=(VMEM_SPEC,) * 4,
        out_shape=(
            pltpu.VMEM((PAIRS, 2 * ROWS, 2), jnp.float32),
            pltpu.VMEM((PAIRS, 2 * ROWS, LANES), jnp.float32),
        )
        + tuple(pltpu.VMEM(w.shape, w.dtype) for w in later_weights),
        scratch_shapes=[
            pltpu.VMEM((PREF_GRP * LANES, PLEN // 4), jnp.bfloat16),
            pltpu.VMEM((PLEN // 4, PREF_GRP * LANES), jnp.bfloat16),
            pltpu.VMEM((PAIRS + 2, LANES, ROWS), jnp.bfloat16),
            pltpu.VMEM((PAIRS + 2, ROWS, LANES), jnp.bfloat16),
            pltpu.SemaphoreType.DMA((2,)),
        ],
        compiler_params=pltpu.CompilerParams(vmem_limit_bytes=VMEM_LIMIT),
        cost_estimate=COST,
        name="attend_own",
    )(place, *on_chip(got, *made), *off_chip(*later_weights))


def rest_kernel(
    place_ref, got_ref, prev_ref, next_ref, far_ref, near_ref, line_ref, meta_ref, stat_ref, acc_ref, w_hbm,
    out_ref, w_ref, keys, values, kwin, vwin, landed,
):
    copies = start_copies(((w_hbm, w_ref),), landed)
    turns = ((3, prev_ref), (1, next_ref), (2, far_ref))
    for i, (_, ref) in enumerate(turns):
        quarter_of(
            lambda s, at, ref=ref: ref[s * 4 * SHARE + at : s * 4 * SHARE + at + SHARE], keys.at[i], values.at[i]
        )
    for i, ref in enumerate((prev_ref, next_ref)):
        kwin[i] = jnp.transpose(ref[QUARTER : QUARTER + ROWS])
        vwin[i] = ref[QUARTER + ROWS :]
    is_last = [lax.rem(place_ref[0] + turn, 4) == 3 for turn, _ in turns]
    side = place_ref[2]
    low = lax.broadcasted_iota(jnp.int32, (ROWS, LANES), 1) < DK

    def one(step, edge=None):
        request, offset, second = masks_of(meta_ref, step)
        stacked, split = queries(got_ref, step, second)
        tail, full = prefix_bias(line_ref, offset)
        scores = dot(split, jnp.concatenate([keys[i] for i in range(3)], axis=1))
        parts = [
            scores[:, i * LANES : (i + 1) * LANES] + jnp.where(is_last[i], tail, full) for i in range(3)
        ]
        if edge is not None:
            mine = meta_ref[edge * (PAIRS + 1), 0:1, :] == request
            mine = jnp.concatenate([mine, mine], axis=0)
            bias = near_ref[:, edge * 2 * LANES : (edge * 2 + 1) * LANES]
            parts.append(jnp.where(mine, dot(stacked, kwin[edge]) + bias, masked_score))
        before = stat_ref[step, :, 0:1]
        row_max = jnp.max(functools.reduce(jnp.maximum, parts), axis=1, keepdims=True)
        row_max = jnp.maximum(row_max, before)
        shrink = jnp.exp(before - row_max)
        terms = [jnp.exp(part - row_max) for part in parts]
        row_sum = jnp.sum(functools.reduce(jnp.add, terms), axis=1, keepdims=True)
        row_sum = row_sum + stat_ref[step, :, 1:2] * shrink
        weights = [t.astype(jnp.bfloat16) for t in terms]
        far_out = dot(
            jnp.concatenate(weights[:3], axis=1), values[...].reshape(3 * PLEN // 4, PREF_GRP * LANES)
        )
        acc = acc_ref[step] * shrink + jnp.where(second, far_out[:, LANES:], far_out[:, :LANES])
        if edge is not None:
            acc = acc + dot(weights[3], vwin[edge])
        acc = acc / row_sum
        done = jnp.where(low, acc[:ROWS], acc[ROWS:]).astype(jnp.bfloat16)
        out_ref[side * PAIRS + step] = done
        out_ref[(1 - side) * PAIRS + jnp.bitwise_xor(step, 1)] = done

    def middle(step, _):
        one(step)
        return 0

    one(jnp.int32(0), 0)
    lax.fori_loop(1, PAIRS - 1, middle, 0, unroll=2)
    one(jnp.int32(PAIRS - 1), 1)
    for copy in copies:
        copy.wait()


def attend_rest(place, got, prev, after_it, far, made, part, weight):
    return pl.pallas_call(
        rest_kernel,
        in_specs=[SMEM_SPEC] + [VMEM_SPEC] * 9 + [HBM_SPEC],
        out_specs=(VMEM_SPEC,) * 2,
        out_shape=(
            pltpu.VMEM((2 * PAIRS, ROWS, LANES), jnp.bfloat16),
            pltpu.VMEM(weight.shape, weight.dtype),
        ),
        scratch_shapes=[
            pltpu.VMEM((3, PREF_GRP * LANES, PLEN // 4), jnp.bfloat16),
            pltpu.VMEM((3, PLEN // 4, PREF_GRP * LANES), jnp.bfloat16),
            pltpu.VMEM((2, LANES, ROWS), jnp.bfloat16),
            pltpu.VMEM((2, ROWS, LANES), jnp.bfloat16),
            pltpu.SemaphoreType.DMA((1,)),
        ],
        compiler_params=pltpu.CompilerParams(vmem_limit_bytes=VMEM_LIMIT),
        cost_estimate=COST,
        name="attend_rest",
    )(place, *on_chip(got, prev, after_it, far, *made, *part), *off_chip(weight))


def join_kernel(place_ref, att_ref, w_ref, tok_ref, far_tok_ref, gain_ref, hidden_ref, normed_ref):
    side = place_ref[2]
    halves = [
        jnp.concatenate([att_ref[at * PAIRS + j] for j in range(PAIRS)], axis=1) for at in (side, 1 - side)
    ]
    got = jnp.dot(jnp.concatenate(halves, axis=0), w_ref[...], preferred_element_type=jnp.float32)
    for half, ref in enumerate((tok_ref, far_tok_ref)):
        mine = got[half * ROWS : (half + 1) * ROWS]
        hidden = (ref[...].astype(jnp.float32) + mine).astype(jnp.bfloat16)
        if half == 0:
            hidden_ref[...] = hidden
        normed_ref[half] = norm_rows(hidden, gain_ref[...])


def join(place, att, w_attn_out, tokens, far_tokens, gain):
    return pl.pallas_call(
        join_kernel,
        in_specs=[SMEM_SPEC] + [VMEM_SPEC] * 5,
        out_specs=(VMEM_SPEC,) * 2,
        out_shape=(pltpu.VMEM((ROWS, D), jnp.bfloat16), pltpu.VMEM((2, ROWS, D), jnp.bfloat16)),
        compiler_params=pltpu.CompilerParams(vmem_limit_bytes=VMEM_LIMIT),
        cost_estimate=COST,
        name="join",
    )(place, *on_chip(att, w_attn_out, tokens, far_tokens, gain.reshape(1, D)))


def feed_kernel(picked, rows_ref, in_ref, out_w_ref, *rest):
    out_refs = rest[len(rest) - len(picked) :]
    rows = jnp.concatenate([rows_ref[half] for half in picked], axis=0)
    units = lax.dot_general(
        rows, in_ref[...], (((1,), (1,)), ((), ())), preferred_element_type=jnp.float32
    )
    units = jnp.maximum(units, 0.0).astype(jnp.bfloat16)
    got = jnp.dot(units, out_w_ref[...], preferred_element_type=jnp.float32).astype(jnp.bfloat16)
    for at, ref in enumerate(out_refs):
        ref[...] = got[at * ROWS : (at + 1) * ROWS]


def feed(picked, rows, w_in, w_out, *ready):
    shape = pltpu.VMEM((ROWS, D), jnp.bfloat16)
    return pl.pallas_call(
        functools.partial(feed_kernel, picked),
        in_specs=[VMEM_SPEC] * (3 + len(ready)),
        out_specs=(VMEM_SPEC,) * len(picked),
        out_shape=(shape,) * len(picked),
        compiler_params=pltpu.CompilerParams(vmem_limit_bytes=VMEM_LIMIT),
        cost_estimate=COST,
        name="feed",
    )(*on_chip(rows, w_in, w_out, *ready))


def total_kernel(*refs):
    out_ref = refs[-1]
    total = functools.reduce(jnp.add, [ref[...].astype(jnp.float32) for ref in refs[:-1]])
    out_ref[...] = total.astype(out_ref.dtype)


def total(dtype, *arrays, last=False):
    return pl.pallas_call(
        total_kernel,
        in_specs=[VMEM_SPEC] * len(arrays),
        out_specs=VMEM_SPEC,
        out_shape=(jax.ShapeDtypeStruct if last else pltpu.VMEM)(arrays[0].shape, dtype),
        compiler_params=pltpu.CompilerParams(vmem_limit_bytes=VMEM_LIMIT),
        cost_estimate=COST,
        name="total",
    )(*on_chip(*arrays))


def body(
    tokens,
    attn_gain,
    w_query,
    w_key,
    w_value,
    w_attn_out,
    rel_bias,
    prefix_cache,
    lengths,
    prefix_map,
    mlp_gain,
    w_in,
    w_out,
):
    count_x = lax.axis_size("x")
    plane = lax.axis_index("z") * 2 + lax.axis_index("ylo")
    place = jnp.stack([lax.axis_index("x"), plane, lax.axis_index("yhi")]).astype(jnp.int32)
    made = tables(place, rel_bias, lengths, prefix_map)

    blocks = project(tokens, attn_gain, w_query, w_key, w_value, prefix_cache)
    got = lax.all_to_all(blocks, PLANE, 0, 0, tiled=True)
    mirrored = ("yhi", "ylo")
    far_tokens = lax.ppermute(tokens, mirrored, MIRROR)
    up, down, far = spread(got, far_tokens, *made)
    by = lambda d: [(i, (i + d) % count_x) for i in range(count_x)]
    prev = lax.ppermute(up, "x", by(1))
    later = lax.ppermute(down, "x", by(-1))
    opposite = lax.ppermute(far, "x", by(2))
    stat, acc, w_attn_out, w_in = attend_own(place, got, made, (w_attn_out, w_in))
    mixed, w_out = attend_rest(place, got, prev, later, opposite, made, (stat, acc), w_out)
    att = lax.all_to_all(mixed, ("yhi",) + PLANE, 0, 0, tiled=True)

    hidden, normed = join(place, att, w_attn_out, tokens, far_tokens, mlp_gain)
    other = lax.ppermute(normed, "core", SWAP)
    mine, far_mine = feed((0, 1), normed, w_in, w_out)
    (far_theirs,) = feed((1,), other, w_in, w_out, mine)
    far_sum = total(jnp.bfloat16, far_mine, lax.ppermute(far_theirs, "core", SWAP))
    back = lax.ppermute(far_sum, mirrored, MIRROR)
    (theirs,) = feed((0,), other, w_in, w_out, far_theirs)
    local = total(jnp.float32, hidden, mine, lax.ppermute(theirs, "core", SWAP))
    return total(jnp.bfloat16, local, back, last=True)


def solution(mesh):
    split = Mesh(mesh.devices.reshape(2, 2, 4, 4, 2), AXES)
    grp, req = ("yhi", "core"), REQ
    return jax.shard_map(
        body,
        mesh=split,
        in_specs=(
            P(grp + req, None),
            P(),
            P(),
            P(),
            P(),
            P(),
            P(),
            P(grp, req, None),
            P(grp, None),
            P(grp, None),
            P(),
            P(grp, None),
            P(grp, None),
        ),
        out_specs=P(grp + req, None),
        check_vma=False,
    )
```

```python
import functools

import jax
import jax.numpy as jnp
from jax import lax
from jax.experimental import pallas as pl
from jax.experimental.pallas import tpu as pltpu
from jax.sharding import Mesh, PartitionSpec as P

D = 1024
H = 16
DK = 64
PLEN = 512
PREF_GRP = 2
ROWS = 128
PAIRS = 8
LANES = 128
CHUNK = 512
SHARE = 16
SENT = 3 * ROWS + 2 * PREF_GRP * SHARE
QUARTER = PAIRS * 2 * PREF_GRP * SHARE

epsilon = 1e-06
far_marks = (12, 16, 23, 32, 46, 64, 91)
masked_score = -1e30
VMEM_LIMIT = 16 * 1024 * 1024
COST = pl.CostEstimate(flops=1000, transcendentals=0, bytes_accessed=1000)

AXES = ("yhi", "core", "x", "z", "ylo")
REQ = ("x", "z", "ylo")
PLANE = ("z", "ylo")
MIRROR = [(0, 3), (3, 0), (1, 2), (2, 1)]
SWAP = [(0, 1), (1, 0)]


def norm_rows(values_in, gain):
    widened = values_in.astype(jnp.float32)
    scale = lax.rsqrt(jnp.mean(widened * widened, axis=-1, keepdims=True) + epsilon)
    return (widened * scale * gain).astype(jnp.bfloat16)


def on_chip(*arrays):
    return tuple(pltpu.with_memory_space_constraint(a, pltpu.VMEM) for a in arrays)


def off_chip(*arrays):
    return tuple(pltpu.with_memory_space_constraint(a, pltpu.HBM) for a in arrays)


VMEM_SPEC = pl.BlockSpec(memory_space=pltpu.VMEM)
HBM_SPEC = pl.BlockSpec(memory_space=pltpu.HBM)
SMEM_SPEC = pl.BlockSpec(memory_space=pltpu.SMEM)


def project_kernel(
    tok_hbm, gain_hbm, cache_hbm, wq_hbm, wk_hbm, wv_hbm, out_hbm, tok, gain, cache, held, out_ref, arrived, landed, left
):
    columns = [slice(c * CHUNK, (c + 1) * CHUNK) for c in range(D // CHUNK)]
    first = [
        pltpu.make_async_copy(source, target, landed.at[i])
        for i, (source, target) in enumerate(((tok_hbm, tok), (gain_hbm, gain), (cache_hbm, cache)))
    ]
    copies = [
        [
            pltpu.make_async_copy(w_hbm.at[:, cut], held.at[kind, c], arrived.at[kind, c])
            for c, cut in enumerate(columns)
        ]
        for kind, w_hbm in enumerate((wq_hbm, wk_hbm, wv_hbm))
    ]
    for copy in first:
        copy.start()
    for row in copies:
        for copy in row:
            copy.start()
    for copy in first:
        copy.wait()
    normed = norm_rows(tok[...], gain[...])
    for part in range(PAIRS):
        for kind in range(2):
            for p in range(PREF_GRP):
                at = 3 * ROWS + (kind * PREF_GRP + p) * SHARE
                cut = slice(kind * D + part * LANES, kind * D + (part + 1) * LANES)
                out_ref[part, at : at + SHARE] = cache[p, :, cut]
    def send(at, i):
        copy = pltpu.make_async_copy(out_ref.at[:, at], out_hbm.at[:, at], left.at[i])
        copy.start()
        return copy

    sends = [send(slice(3 * ROWS, SENT), 3)]
    for kind, row in enumerate(copies):
        for c, copy in enumerate(row):
            copy.wait()
            got = jnp.dot(normed, held[kind, c], preferred_element_type=jnp.float32)
            got = got.astype(jnp.bfloat16)
            for part in range(CHUNK // LANES):
                to = c * (CHUNK // LANES) + part
                out_ref[to, kind * ROWS : (kind + 1) * ROWS] = got[:, part * LANES : (part + 1) * LANES]
        sends.append(send(slice(kind * ROWS, (kind + 1) * ROWS), kind))
    for copy in sends:
        copy.wait()


def project(tokens, gain, w_query, w_key, w_value, prefix_cache):
    operands = (tokens, gain.reshape(1, D), prefix_cache, w_query, w_key, w_value)
    return pl.pallas_call(
        project_kernel,
        in_specs=[HBM_SPEC] * 6,
        out_specs=HBM_SPEC,
        out_shape=pltpu.HBM((PAIRS, SENT, LANES), jnp.bfloat16),
        scratch_shapes=[
            pltpu.VMEM((ROWS, D), jnp.bfloat16),
            pltpu.VMEM((1, D), jnp.float32),
            pltpu.VMEM(prefix_cache.shape, jnp.bfloat16),
            pltpu.VMEM((3, D // CHUNK, D, CHUNK), jnp.bfloat16),
            pltpu.VMEM((PAIRS, SENT, LANES), jnp.bfloat16),
            pltpu.SemaphoreType.DMA((3, D // CHUNK)),
            pltpu.SemaphoreType.DMA((3,)),
            pltpu.SemaphoreType.DMA((4,)),
        ],
        compiler_params=pltpu.CompilerParams(vmem_limit_bytes=VMEM_LIMIT),
        cost_estimate=COST,
        name="project",
    )(*off_chip(*operands))


def spread_kernel(got_ref, *rest):
    up_ref, down_ref, far_ref = rest[-3:]
    for source in range(PAIRS):
        rows = slice(source * 4 * SHARE, (source + 1) * 4 * SHARE)
        held = got_ref[source, 3 * ROWS :]
        up_ref[rows] = held
        down_ref[rows] = held
        far_ref[rows] = held
    up_ref[QUARTER:] = got_ref[PAIRS - 1, ROWS : 3 * ROWS]
    down_ref[QUARTER:] = got_ref[0, ROWS : 3 * ROWS]


def spread(got, *ready):
    shape = pltpu.VMEM((QUARTER + 2 * ROWS, LANES), jnp.bfloat16)
    return pl.pallas_call(
        spread_kernel,
        in_specs=[VMEM_SPEC] * (1 + len(ready)),
        out_specs=(VMEM_SPEC,) * 3,
        out_shape=(shape, shape, pltpu.VMEM((QUARTER, LANES), jnp.bfloat16)),
        compiler_params=pltpu.CompilerParams(vmem_limit_bytes=VMEM_LIMIT),
        cost_estimate=COST,
        name="spread",
    )(*on_chip(got, *ready))


def bias_line(rel_ref, head, first_bucket):
    lane = lax.broadcasted_iota(jnp.int32, (ROWS, LANES), 1)
    line = jnp.full((ROWS, LANES), rel_ref[head, first_bucket], jnp.float32)
    for bucket in range(1, 16):
        mark = bucket if bucket <= 8 else far_marks[bucket - 9]
        line = jnp.where(lane >= mark, rel_ref[head, first_bucket + bucket], line)
    return line


def tables_kernel(
    place_ref, rel_ref, len_ref, map_ref, near_ref, name_ref, asked_ref, tail_ref, chosen_ref
):
    row = lax.broadcasted_iota(jnp.int32, (ROWS, LANES), 0)
    lane = lax.broadcasted_iota(jnp.int32, (ROWS, LANES), 1)
    lines = []
    for h in range(2):
        head = place_ref[1] * 2 + h
        before = bias_line(rel_ref, head, 0)
        after_it = bias_line(rel_ref, head, 16)

        def pick(line, distance):
            return jnp.take_along_axis(line, jnp.clip(distance, 0, LANES - 1), axis=1)

        rows = slice(h * ROWS, (h + 1) * ROWS)
        near_ref[rows, 0:LANES] = pick(before, row + LANES - lane)
        near_ref[rows, LANES : 2 * LANES] = jnp.where(
            lane > row, pick(after_it, lane - row), pick(before, row - lane)
        )
        near_ref[rows, 2 * LANES : 3 * LANES] = pick(after_it, lane + LANES - row)
        lines.append(before)

    requests = len_ref.shape[1]
    down_it = lax.broadcasted_iota(jnp.int32, (requests, requests), 0)
    along = lax.broadcasted_iota(jnp.int32, (requests, requests), 1)
    length = jnp.broadcast_to(len_ref[...], (requests, requests)).astype(jnp.float32)
    prefix = jnp.broadcast_to(map_ref[...], (requests, requests)).astype(jnp.float32)

    def column(keep, values):
        return jnp.sum(jnp.where(keep, values, 0.0), axis=1, keepdims=True)

    starts = column(along < down_it, length)
    ends = column(along <= down_it, length)
    prefixes = column(along == down_it, prefix)
    number = lax.broadcasted_iota(jnp.int32, (requests, LANES), 0).astype(jnp.float32) + 1.0
    first = place_ref[0] * (PAIRS * ROWS) - ROWS
    facts = []
    for b in range(PAIRS + 2):
        ids = lax.broadcasted_iota(jnp.int32, (requests, LANES), 1) + (first + b * ROWS)
        ids = ids.astype(jnp.float32)
        member = (ids >= starts) & (ids < ends)
        request = jnp.sum(jnp.where(member, number, 0.0), axis=0, keepdims=True) - 1.0
        offset = ids[0:1] - jnp.sum(jnp.where(member, starts, 0.0), axis=0, keepdims=True)
        chosen = jnp.sum(jnp.where(member, prefixes, 0.0), axis=0, keepdims=True)
        name_ref[b] = jnp.broadcast_to(request, (8, LANES))
        facts.append(jnp.concatenate([request, offset, chosen] + [request] * 5, axis=0))

    for step in range(PAIRS):
        own = jnp.transpose(facts[step + 1])
        asked_ref[step] = jnp.broadcast_to(own[:, 0:1], (ROWS, LANES))
        chosen_ref[step] = jnp.broadcast_to(own[:, 2:3], (ROWS, LANES)).astype(jnp.bfloat16)
        offset = jnp.broadcast_to(own[:, 1:2], (ROWS, LANES)).astype(jnp.int32)
        at = jnp.minimum(LANES - lane + offset, LANES - 1)
        for h in range(2):
            tail_ref[step, h * ROWS : (h + 1) * ROWS] = jnp.take_along_axis(lines[h], at, axis=1)


def tables(place, rel_bias, lengths, prefix_map):
    return pl.pallas_call(
        tables_kernel,
        in_specs=[SMEM_SPEC, SMEM_SPEC, VMEM_SPEC, VMEM_SPEC],
        out_specs=(VMEM_SPEC,) * 5,
        out_shape=(
            pltpu.VMEM((2 * ROWS, 3 * LANES), jnp.float32),
            pltpu.VMEM((PAIRS + 2, 8, LANES), jnp.float32),
            pltpu.VMEM((PAIRS, ROWS, LANES), jnp.float32),
            pltpu.VMEM((PAIRS, 2 * ROWS, LANES), jnp.float32),
            pltpu.VMEM((PAIRS, ROWS, LANES), jnp.bfloat16),
        ),
        compiler_params=pltpu.CompilerParams(vmem_limit_bytes=VMEM_LIMIT),
        cost_estimate=COST,
        name="tables",
    )(place, rel_bias.T, *on_chip(lengths, prefix_map))


def queries(got_ref, chosen_ref, step):
    query = got_ref[step, 0:ROWS]
    low = (lax.broadcasted_iota(jnp.int32, (ROWS, LANES), 1) < DK).astype(jnp.bfloat16)
    stacked = jnp.concatenate([query * low, query * (1 - low)], axis=0)
    chosen = chosen_ref[step]
    chosen = jnp.concatenate([chosen, chosen], axis=0)
    return stacked, jnp.concatenate([stacked * (1 - chosen), stacked * chosen], axis=1)


def masked(scores, name_ref, block, asked_ref, step, bias):
    mine = name_ref[block, 0:1] == asked_ref[step]
    mine = jnp.concatenate([mine, mine], axis=0)
    return jnp.where(mine, scores + bias, masked_score)


def far_bias(place_ref, rel_ref):
    return jnp.concatenate(
        [jnp.full((ROWS, LANES), rel_ref[place_ref[1] * 2 + h, 15], jnp.float32) for h in range(2)], axis=0
    )


def select(chosen_ref, step, far_out):
    second = chosen_ref[step].astype(jnp.float32) > 0.5
    second = jnp.concatenate([second, second], axis=0)
    return jnp.where(second, far_out[:, LANES:], far_out[:, :LANES])


def quarter_of(rows_at, keys_ref, values_ref):
    for p in range(PREF_GRP):
        pieces = [
            jnp.concatenate(
                [rows_at(source, (kind * PREF_GRP + p) * SHARE) for source in range(PAIRS)], axis=0
            )
            for kind in range(2)
        ]
        keys_ref[p * LANES : (p + 1) * LANES, :] = jnp.transpose(pieces[0])
        values_ref[:, p * LANES : (p + 1) * LANES] = pieces[1]


def dot(a, b):
    return jnp.dot(a, b, preferred_element_type=jnp.float32)


def start_copies(pairs, landed):
    copies = [pltpu.make_async_copy(a, b, landed.at[i]) for i, (a, b) in enumerate(pairs)]
    for copy in copies:
        copy.start()
    return copies


def own_kernel(
    place_ref, rel_ref, got_ref, near_ref, name_ref, asked_ref, tail_ref, chosen_ref, w1_hbm, w2_hbm, w3_hbm,
    stat_ref, acc_ref, w1_ref, w2_ref, w3_ref, keys, values, kwin, vwin, landed,
):
    copies = start_copies(((w1_hbm, w1_ref), (w2_hbm, w2_ref), (w3_hbm, w3_ref)), landed)
    for b in (0, PAIRS + 1):
        kwin[b] = jnp.zeros((LANES, ROWS), jnp.bfloat16)
        vwin[b] = jnp.zeros((ROWS, LANES), jnp.bfloat16)
    for b in range(PAIRS):
        kwin[b + 1] = jnp.transpose(got_ref[b, ROWS : 2 * ROWS])
        vwin[b + 1] = got_ref[b, 2 * ROWS : 3 * ROWS]
    quarter_of(lambda s, at: got_ref[s, 3 * ROWS + at : 3 * ROWS + at + SHARE], keys, values)
    is_last = place_ref[0] == 3
    full = far_bias(place_ref, rel_ref)

    def one(step, _):
        stacked, split = queries(got_ref, chosen_ref, step)
        parts = [dot(split, keys[...]) + jnp.where(is_last, tail_ref[step], full)]
        near_scores = dot(stacked, jnp.concatenate([kwin[step + b] for b in range(3)], axis=1))
        for b in range(3):
            at_edge = (step + b == 0) | (step + b == PAIRS + 1)
            cut = slice(b * LANES, (b + 1) * LANES)
            bias = near_ref[:, cut] + jnp.where(at_edge, masked_score, 0.0)
            parts.append(masked(near_scores[:, cut], name_ref, step + b, asked_ref, step, bias))
        row_max = jnp.max(functools.reduce(jnp.maximum, parts), axis=1, keepdims=True)
        terms = [jnp.exp(part - row_max) for part in parts]
        row_sum = jnp.sum(functools.reduce(jnp.add, terms), axis=1, keepdims=True)
        weights = [t.astype(jnp.bfloat16) for t in terms]
        far_out = dot(weights[0], values[...])
        near_values = jnp.concatenate([vwin[step + b] for b in range(3)], axis=0)
        acc = select(chosen_ref, step, far_out)
        acc_ref[step] = acc + dot(jnp.concatenate(weights[1:], axis=1), near_values)
        stat_ref[step, :, 0:1] = row_max
        stat_ref[step, :, 1:2] = row_sum
        return 0

    lax.fori_loop(0, PAIRS, one, 0, unroll=2)
    for copy in copies:
        copy.wait()


def attend_own(place, rel_bias, got, made, later_weights):
    return pl.pallas_call(
        own_kernel,
        in_specs=[SMEM_SPEC] * 2 + [VMEM_SPEC] * 6 + [HBM_SPEC] * 3,
        out_specs=(VMEM_SPEC,) * 5,
        out_shape=(
            pltpu.VMEM((PAIRS, 2 * ROWS, 2), jnp.float32),
            pltpu.VMEM((PAIRS, 2 * ROWS, LANES), jnp.float32),
        )
        + tuple(pltpu.VMEM(w.shape, w.dtype) for w in later_weights),
        scratch_shapes=[
            pltpu.VMEM((PREF_GRP * LANES, PLEN // 4), jnp.bfloat16),
            pltpu.VMEM((PLEN // 4, PREF_GRP * LANES), jnp.bfloat16),
            pltpu.VMEM((PAIRS + 2, LANES, ROWS), jnp.bfloat16),
            pltpu.VMEM((PAIRS + 2, ROWS, LANES), jnp.bfloat16),
            pltpu.SemaphoreType.DMA((3,)),
        ],
        compiler_params=pltpu.CompilerParams(vmem_limit_bytes=VMEM_LIMIT),
        cost_estimate=COST,
        name="attend_own",
    )(place, rel_bias.T, *on_chip(got, *made), *off_chip(*later_weights))


def rest_kernel(
    place_ref, rel_ref, got_ref, prev_ref, next_ref, far_ref, near_ref, name_ref, asked_ref, tail_ref, chosen_ref,
    stat_ref, acc_ref, w1_hbm, w2_hbm, out_ref, w1_ref, w2_ref, keys, values, kwin, vwin, landed,
):
    copies = start_copies(((w1_hbm, w1_ref), (w2_hbm, w2_ref)), landed)
    turns = ((3, prev_ref), (1, next_ref), (2, far_ref))
    for i, (_, ref) in enumerate(turns):
        quarter_of(
            lambda s, at, ref=ref: ref[s * 4 * SHARE + at : s * 4 * SHARE + at + SHARE], keys.at[i], values.at[i]
        )
    for i, ref in enumerate((prev_ref, next_ref)):
        kwin[i] = jnp.transpose(ref[QUARTER : QUARTER + ROWS])
        vwin[i] = ref[QUARTER + ROWS :]
    is_last = [lax.rem(place_ref[0] + turn, 4) == 3 for turn, _ in turns]
    side = place_ref[2]
    low = lax.broadcasted_iota(jnp.int32, (ROWS, LANES), 1) < DK
    full = far_bias(place_ref, rel_ref)

    def one(step, edge=None):
        stacked, split = queries(got_ref, chosen_ref, step)
        tail = tail_ref[step]
        scores = dot(split, jnp.concatenate([keys[i] for i in range(3)], axis=1))
        parts = [
            scores[:, i * LANES : (i + 1) * LANES] + jnp.where(is_last[i], tail, full) for i in range(3)
        ]
        if edge is not None:
            bias = near_ref[:, edge * 2 * LANES : (edge * 2 + 1) * LANES]
            parts.append(
                masked(dot(stacked, kwin[edge]), name_ref, edge * (PAIRS + 1), asked_ref, step, bias)
            )
        before = stat_ref[step, :, 0:1]
        row_max = jnp.max(functools.reduce(jnp.maximum, parts), axis=1, keepdims=True)
        row_max = jnp.maximum(row_max, before)
        shrink = jnp.exp(before - row_max)
        terms = [jnp.exp(part - row_max) for part in parts]
        row_sum = jnp.sum(functools.reduce(jnp.add, terms), axis=1, keepdims=True)
        row_sum = row_sum + stat_ref[step, :, 1:2] * shrink
        weights = [t.astype(jnp.bfloat16) for t in terms]
        far_out = dot(
            jnp.concatenate(weights[:3], axis=1), values[...].reshape(3 * PLEN // 4, PREF_GRP * LANES)
        )
        acc = acc_ref[step] * shrink + select(chosen_ref, step, far_out)
        if edge is not None:
            acc = acc + dot(weights[3], vwin[edge])
        acc = acc / row_sum
        done = jnp.where(low, acc[:ROWS], acc[ROWS:]).astype(jnp.bfloat16)
        out_ref[side * PAIRS + step] = done
        out_ref[(1 - side) * PAIRS + jnp.bitwise_xor(step, 1)] = done

    def middle(step, _):
        one(step)
        return 0

    one(jnp.int32(0), 0)
    lax.fori_loop(1, PAIRS - 1, middle, 0, unroll=2)
    one(jnp.int32(PAIRS - 1), 1)
    for copy in copies:
        copy.wait()


def attend_rest(place, rel_bias, got, prev, after_it, far, made, part, later_weights):
    return pl.pallas_call(
        rest_kernel,
        in_specs=[SMEM_SPEC] * 2 + [VMEM_SPEC] * 11 + [HBM_SPEC] * 2,
        out_specs=(VMEM_SPEC,) * 3,
        out_shape=(pltpu.VMEM((2 * PAIRS, ROWS, LANES), jnp.bfloat16),)
        + tuple(pltpu.VMEM(w.shape, w.dtype) for w in later_weights),
        scratch_shapes=[
            pltpu.VMEM((3, PREF_GRP * LANES, PLEN // 4), jnp.bfloat16),
            pltpu.VMEM((3, PLEN // 4, PREF_GRP * LANES), jnp.bfloat16),
            pltpu.VMEM((2, LANES, ROWS), jnp.bfloat16),
            pltpu.VMEM((2, ROWS, LANES), jnp.bfloat16),
            pltpu.SemaphoreType.DMA((2,)),
        ],
        compiler_params=pltpu.CompilerParams(vmem_limit_bytes=VMEM_LIMIT),
        cost_estimate=COST,
        name="attend_rest",
    )(place, rel_bias.T, *on_chip(got, prev, after_it, far, *made, *part), *off_chip(*later_weights))


def join_kernel(away, place_ref, att_ref, w_ref, tok_ref, gain_ref, *rest):
    at = (1 - place_ref[2] if away else place_ref[2]) * PAIRS
    attended = jnp.concatenate([att_ref[at + j] for j in range(PAIRS)], axis=1)
    hidden = (tok_ref[...].astype(jnp.float32) + dot(attended, w_ref[...])).astype(jnp.bfloat16)
    rest[-1][...] = norm_rows(hidden, gain_ref[...])
    if not away:
        rest[-2][...] = hidden


def join(away, place, att, w_attn_out, tokens, gain, *ready):
    count = 1 if away else 2
    return pl.pallas_call(
        functools.partial(join_kernel, away),
        in_specs=[SMEM_SPEC] + [VMEM_SPEC] * (4 + len(ready)),
        out_specs=(VMEM_SPEC,) * count,
        out_shape=(pltpu.VMEM((ROWS, D), jnp.bfloat16),) * count,
        compiler_params=pltpu.CompilerParams(vmem_limit_bytes=VMEM_LIMIT),
        cost_estimate=COST,
        name="join",
    )(place, *on_chip(att, w_attn_out, tokens, gain.reshape(1, D), *ready))


def feed_kernel(rows_ref, in_one, in_two, out_one, out_two, *rest):
    got = None
    for in_ref, out_w_ref in ((in_one, out_one), (in_two, out_two)):
        units = lax.dot_general(
            rows_ref[...], in_ref[...], (((1,), (1,)), ((), ())), preferred_element_type=jnp.float32
        )
        part = dot(jnp.maximum(units, 0.0).astype(jnp.bfloat16), out_w_ref[...])
        got = part if got is None else got + part
    rest[-1][...] = got.astype(rest[-1].dtype)


def feed(dtype, rows, weights):
    return pl.pallas_call(
        feed_kernel,
        in_specs=[VMEM_SPEC] * 5,
        out_specs=VMEM_SPEC,
        out_shape=pltpu.VMEM((ROWS, D), dtype),
        compiler_params=pltpu.CompilerParams(vmem_limit_bytes=VMEM_LIMIT),
        cost_estimate=COST,
        name="feed",
    )(*on_chip(rows, *weights))


def total_kernel(*refs):
    out_ref = refs[-1]
    total = functools.reduce(jnp.add, [ref[...].astype(jnp.float32) for ref in refs[:-1]])
    out_ref[...] = total.astype(out_ref.dtype)


def total(dtype, *arrays, last=False):
    return pl.pallas_call(
        total_kernel,
        in_specs=[VMEM_SPEC] * len(arrays),
        out_specs=VMEM_SPEC,
        out_shape=(jax.ShapeDtypeStruct if last else pltpu.VMEM)(arrays[0].shape, dtype),
        compiler_params=pltpu.CompilerParams(vmem_limit_bytes=VMEM_LIMIT),
        cost_estimate=COST,
        name="total",
    )(*on_chip(*arrays))


def body(
    tokens,
    attn_gain,
    w_query,
    w_key,
    w_value,
    w_attn_out,
    rel_bias,
    prefix_cache,
    lengths,
    prefix_map,
    mlp_gain,
    w_in,
    w_out,
):
    count_x = lax.axis_size("x")
    plane = lax.axis_index("z") * 2 + lax.axis_index("ylo")
    place = jnp.stack([lax.axis_index("x"), plane, lax.axis_index("yhi")]).astype(jnp.int32)
    made = tables(place, rel_bias, lengths, prefix_map)

    blocks = project(tokens, attn_gain, w_query, w_key, w_value, prefix_cache)
    got = lax.all_to_all(blocks, PLANE, 0, 0, tiled=True)
    mirrored = ("yhi", "ylo")
    far_tokens = lax.ppermute(tokens, mirrored, MIRROR)
    other_in = lax.ppermute(w_in, "core", SWAP)
    other_out = lax.ppermute(w_out, "core", SWAP)
    up, down, far = spread(got, far_tokens, *made)
    by = lambda d: [(i, (i + d) % count_x) for i in range(count_x)]
    prev = lax.ppermute(up, "x", by(1))
    later = lax.ppermute(down, "x", by(-1))
    opposite = lax.ppermute(far, "x", by(2))
    stat, acc, *own_weights = attend_own(place, rel_bias, got, made, (w_attn_out, w_in, w_out))
    mixed, *other_weights = attend_rest(
        place, rel_bias, got, prev, later, opposite, made, (stat, acc), (other_in, other_out)
    )
    w_attn_out = own_weights[0]
    weights = (own_weights[1], other_weights[0], own_weights[2], other_weights[1])
    att = lax.all_to_all(mixed, ("yhi",) + PLANE, 0, 0, tiled=True)

    (far_normed,) = join(True, place, att, w_attn_out, far_tokens, mlp_gain)
    far_sum = feed(jnp.bfloat16, far_normed, weights)
    back = lax.ppermute(far_sum, mirrored, MIRROR)
    hidden, normed = join(False, place, att, w_attn_out, tokens, mlp_gain, far_sum)
    mine = feed(jnp.float32, normed, weights)
    return total(jnp.bfloat16, hidden, mine, back, last=True)


def solution(mesh):
    split = Mesh(mesh.devices.reshape(2, 2, 4, 4, 2), AXES)
    grp, req = ("yhi", "core"), REQ
    return jax.shard_map(
        body,
        mesh=split,
        in_specs=(
            P(grp + req, None),
            P(),
            P(),
            P(),
            P(),
            P(),
            P(),
            P(grp, req, None),
            P(grp, None),
            P(grp, None),
            P(),
            P(grp, None),
            P(grp, None),
        ),
        out_specs=P(grp + req, None),
        check_vma=False,
    )
```

```python
import functools

import jax
import jax.numpy as jnp
from jax import lax
from jax.experimental import pallas as pl
from jax.experimental.pallas import tpu as pltpu
from jax.sharding import Mesh, PartitionSpec as P

D = 1024
H = 16
DK = 64
PLEN = 512
PREF_GRP = 2
ROWS = 128
PAIRS = 8
LANES = 128
CHUNK = 1024
SHARE = 16
SENT = 3 * ROWS + 2 * PREF_GRP * SHARE
QUARTER = PAIRS * 2 * PREF_GRP * SHARE

epsilon = 1e-06
far_marks = (12, 16, 23, 32, 46, 64, 91)
masked_score = -1e30
VMEM_LIMIT = 16 * 1024 * 1024
COST = pl.CostEstimate(flops=1000, transcendentals=0, bytes_accessed=1000)

AXES = ("yhi", "core", "x", "z", "ylo")
REQ = ("x", "z", "ylo")
PLANE = ("z", "ylo")
MIRROR = [(0, 3), (3, 0), (1, 2), (2, 1)]
SWAP = [(0, 1), (1, 0)]


def norm_rows(values_in, gain):
    widened = values_in.astype(jnp.float32)
    scale = lax.rsqrt(jnp.mean(widened * widened, axis=-1, keepdims=True) + epsilon)
    return (widened * scale * gain).astype(jnp.bfloat16)


def dot(a, b):
    return jnp.dot(a, b, preferred_element_type=jnp.float32)


def on_chip(*arrays):
    return tuple(pltpu.with_memory_space_constraint(a, pltpu.VMEM) for a in arrays)


def off_chip(*arrays):
    return tuple(pltpu.with_memory_space_constraint(a, pltpu.HBM) for a in arrays)


VMEM_SPEC = pl.BlockSpec(memory_space=pltpu.VMEM)
HBM_SPEC = pl.BlockSpec(memory_space=pltpu.HBM)
SMEM_SPEC = pl.BlockSpec(memory_space=pltpu.SMEM)


def project_kernel(
    tok_hbm, gain_hbm, cache_hbm, wq_hbm, wk_hbm, wv_hbm, out_hbm, tok, gain, cache, held, out_ref, arrived, landed, left
):
    chunks = [slice(c * CHUNK, (c + 1) * CHUNK) for c in range(D // CHUNK)]
    first = [
        pltpu.make_async_copy(source, target, landed.at[i])
        for i, (source, target) in enumerate(((tok_hbm, tok), (gain_hbm, gain), (cache_hbm, cache)))
    ]
    copies = [
        [
            pltpu.make_async_copy(w_hbm.at[cut], held.at[kind, cut], arrived.at[kind, c])
            for c, cut in enumerate(chunks)
        ]
        for kind, w_hbm in enumerate((wq_hbm, wk_hbm, wv_hbm))
    ]
    for copy in first:
        copy.start()
    for row in copies:
        for copy in row:
            copy.start()
    for copy in first:
        copy.wait()
    normed = norm_rows(tok[...], gain[...])
    for part in range(PAIRS):
        for kind in range(2):
            for p in range(PREF_GRP):
                at = 3 * ROWS + (kind * PREF_GRP + p) * SHARE
                cut = slice(kind * D + part * LANES, kind * D + (part + 1) * LANES)
                out_ref[part, at : at + SHARE] = cache[p, :, cut]
    def send(at, i):
        copy = pltpu.make_async_copy(out_ref.at[:, at], out_hbm.at[:, at], left.at[i])
        copy.start()
        return copy

    sends = [send(slice(3 * ROWS, SENT), 3)]
    for kind, row in enumerate(copies):
        got = None
        for cut, copy in zip(chunks, row):
            copy.wait()
            part = dot(normed[:, cut], held[kind, cut])
            got = part if got is None else got + part
        got = got.astype(jnp.bfloat16)
        for to in range(PAIRS):
            out_ref[to, kind * ROWS : (kind + 1) * ROWS] = got[:, to * LANES : (to + 1) * LANES]
        sends.append(send(slice(kind * ROWS, (kind + 1) * ROWS), kind))
    for copy in sends:
        copy.wait()


def project(tokens, gain, w_query, w_key, w_value, prefix_cache):
    operands = (tokens, gain.reshape(1, D), prefix_cache, w_query, w_key, w_value)
    return pl.pallas_call(
        project_kernel,
        in_specs=[HBM_SPEC] * 6,
        out_specs=HBM_SPEC,
        out_shape=pltpu.HBM((PAIRS, SENT, LANES), jnp.bfloat16),
        scratch_shapes=[
            pltpu.VMEM((ROWS, D), jnp.bfloat16),
            pltpu.VMEM((1, D), jnp.float32),
            pltpu.VMEM(prefix_cache.shape, jnp.bfloat16),
            pltpu.VMEM((3, D, D), jnp.bfloat16),
            pltpu.VMEM((PAIRS, SENT, LANES), jnp.bfloat16),
            pltpu.SemaphoreType.DMA((3, D // CHUNK)),
            pltpu.SemaphoreType.DMA((3,)),
            pltpu.SemaphoreType.DMA((4,)),
        ],
        compiler_params=pltpu.CompilerParams(vmem_limit_bytes=VMEM_LIMIT),
        cost_estimate=COST,
        name="project",
    )(*off_chip(*operands))


def spread_kernel(got_ref, *rest):
    up_ref, down_ref, far_ref = rest[-3:]
    for source in range(PAIRS):
        rows = slice(source * 4 * SHARE, (source + 1) * 4 * SHARE)
        held = got_ref[source, 3 * ROWS :]
        up_ref[rows] = held
        down_ref[rows] = held
        far_ref[rows] = held
    up_ref[QUARTER:] = got_ref[PAIRS - 1, ROWS : 3 * ROWS]
    down_ref[QUARTER:] = got_ref[0, ROWS : 3 * ROWS]


def spread(got, arrived, *ready):
    shape = pltpu.VMEM((QUARTER + 2 * ROWS, LANES), jnp.bfloat16)
    return pl.pallas_call(
        spread_kernel,
        in_specs=[VMEM_SPEC] * (1 + len(ready)) + [HBM_SPEC],
        out_specs=(VMEM_SPEC,) * 3,
        out_shape=(shape, shape, pltpu.VMEM((QUARTER, LANES), jnp.bfloat16)),
        compiler_params=pltpu.CompilerParams(vmem_limit_bytes=VMEM_LIMIT),
        cost_estimate=COST,
        name="spread",
    )(*on_chip(got, *ready), *off_chip(arrived))


def bias_line(rel_ref, head, first_bucket):
    lane = lax.broadcasted_iota(jnp.int32, (ROWS, LANES), 1)
    line = jnp.full((ROWS, LANES), rel_ref[head, first_bucket], jnp.float32)
    for bucket in range(1, 16):
        mark = bucket if bucket <= 8 else far_marks[bucket - 9]
        line = jnp.where(lane >= mark, rel_ref[head, first_bucket + bucket], line)
    return line


def tables_kernel(
    place_ref, rel_ref, len_ref, map_ref, near_ref, name_ref, asked_ref, tail_ref, chosen_ref
):
    row = lax.broadcasted_iota(jnp.int32, (ROWS, LANES), 0)
    lane = lax.broadcasted_iota(jnp.int32, (ROWS, LANES), 1)
    lines = []
    for h in range(2):
        head = place_ref[1] * 2 + h
        before = bias_line(rel_ref, head, 0)
        after_it = bias_line(rel_ref, head, 16)

        def pick(line, distance):
            return jnp.take_along_axis(line, jnp.clip(distance, 0, LANES - 1), axis=1)

        cut = slice(h * ROWS, (h + 1) * ROWS)
        near_ref[0:ROWS, cut] = pick(before, lane + ROWS - row)
        near_ref[ROWS : 2 * ROWS, cut] = jnp.where(
            row > lane, pick(after_it, row - lane), pick(before, lane - row)
        )
        near_ref[2 * ROWS : 3 * ROWS, cut] = pick(after_it, row + ROWS - lane)
        lines.append(before)

    requests = len_ref.shape[1]
    down_it = lax.broadcasted_iota(jnp.int32, (requests, requests), 0)
    along = lax.broadcasted_iota(jnp.int32, (requests, requests), 1)
    length = jnp.broadcast_to(len_ref[...], (requests, requests)).astype(jnp.float32)
    prefix = jnp.broadcast_to(map_ref[...], (requests, requests)).astype(jnp.float32)

    def column(keep, values):
        return jnp.sum(jnp.where(keep, values, 0.0), axis=1, keepdims=True)

    starts = column(along < down_it, length)
    ends = column(along <= down_it, length)
    prefixes = column(along == down_it, prefix)
    number = lax.broadcasted_iota(jnp.int32, (requests, LANES), 0).astype(jnp.float32) + 1.0
    first = place_ref[0] * (PAIRS * ROWS) - ROWS
    for b in range(PAIRS + 2):
        ids = lax.broadcasted_iota(jnp.int32, (requests, LANES), 1) + (first + b * ROWS)
        ids = ids.astype(jnp.float32)
        member = (ids >= starts) & (ids < ends)
        request = jnp.sum(jnp.where(member, number, 0.0), axis=0, keepdims=True) - 1.0
        offset = ids[0:1] - jnp.sum(jnp.where(member, starts, 0.0), axis=0, keepdims=True)
        chosen = jnp.sum(jnp.where(member, prefixes, 0.0), axis=0, keepdims=True)
        facts = jnp.concatenate([request, offset, chosen] + [request] * 5, axis=0)
        name_ref[b] = jnp.broadcast_to(jnp.transpose(facts)[:, 0:1], (ROWS, LANES)).astype(jnp.bfloat16)
        if 0 < b < PAIRS + 1:
            step = b - 1
            asked_ref[step] = facts
            chosen_ref[step] = jnp.broadcast_to(chosen, (ROWS, LANES)).astype(jnp.bfloat16)
            at = jnp.minimum(ROWS - row + jnp.broadcast_to(offset, (ROWS, LANES)).astype(jnp.int32), LANES - 1)
            for h in range(2):
                tail_ref[step, :, h * ROWS : (h + 1) * ROWS] = jnp.take_along_axis(lines[h], at, axis=1)


def tables(place, rel_bias, lengths, prefix_map):
    return pl.pallas_call(
        tables_kernel,
        in_specs=[SMEM_SPEC, SMEM_SPEC, VMEM_SPEC, VMEM_SPEC],
        out_specs=(VMEM_SPEC,) * 5,
        out_shape=(
            pltpu.VMEM((3 * ROWS, 2 * ROWS), jnp.float32),
            pltpu.VMEM((PAIRS + 2, ROWS, LANES), jnp.bfloat16),
            pltpu.VMEM((PAIRS, 8, ROWS), jnp.float32),
            pltpu.VMEM((PAIRS, ROWS, 2 * ROWS), jnp.float32),
            pltpu.VMEM((PAIRS, ROWS, ROWS), jnp.bfloat16),
        ),
        compiler_params=pltpu.CompilerParams(vmem_limit_bytes=VMEM_LIMIT),
        cost_estimate=COST,
        name="tables",
    )(place, rel_bias.T, *on_chip(lengths, prefix_map))


def queries(got_ref, chosen_ref, step):
    query = jnp.transpose(got_ref[step, 0:ROWS])
    zero = jnp.zeros((DK, ROWS), jnp.bfloat16)
    stacked = jnp.concatenate(
        [jnp.concatenate([query[:DK], zero], axis=0), jnp.concatenate([zero, query[DK:]], axis=0)], axis=1
    )
    chosen = jnp.concatenate([chosen_ref[step], chosen_ref[step]], axis=1)
    return stacked, jnp.concatenate([stacked * (1 - chosen), stacked * chosen], axis=0)


def masked(scores, name_ref, block, asked_ref, step, bias):
    mine = name_ref[block].astype(jnp.float32) == asked_ref[step, 0:1]
    mine = jnp.concatenate([mine, mine], axis=1)
    return jnp.where(mine, scores + bias, masked_score)


def far_bias(place_ref, rel_ref):
    lane = lax.broadcasted_iota(jnp.int32, (1, 2 * ROWS), 1)
    head = place_ref[1] * 2
    return jnp.where(lane < ROWS, rel_ref[head, 15], rel_ref[head + 1, 15])


def own_head(values):
    return jnp.concatenate([values[:DK, :ROWS], values[DK:, ROWS:]], axis=0)


def by_feature(line):
    return jnp.concatenate(
        [jnp.broadcast_to(line[:, :ROWS], (DK, ROWS)), jnp.broadcast_to(line[:, ROWS:], (DK, ROWS))], axis=0
    )


def select(asked_ref, step, far_out):
    second = jnp.broadcast_to(asked_ref[step, 2:3], (LANES, ROWS)) > 0.5
    return jnp.where(second, own_head(far_out[LANES:]), own_head(far_out[:LANES]))


def quarter_of(rows_at, keys_ref, values_ref):
    for p in range(PREF_GRP):
        pieces = [
            jnp.concatenate(
                [rows_at(source, (kind * PREF_GRP + p) * SHARE) for source in range(PAIRS)], axis=0
            )
            for kind in range(2)
        ]
        keys_ref[:, p * LANES : (p + 1) * LANES] = pieces[0]
        values_ref[p * LANES : (p + 1) * LANES, :] = jnp.transpose(pieces[1])


def start_copies(pairs, landed):
    copies = [pltpu.make_async_copy(a, b, landed.at[i]) for i, (a, b) in enumerate(pairs)]
    for copy in copies:
        copy.start()
    return copies


def own_kernel(
    place_ref, rel_ref, got_ref, near_ref, name_ref, asked_ref, tail_ref, chosen_ref, w1_hbm, w2_hbm, w3_hbm,
    stat_ref, acc_ref, w1_ref, w2_ref, w3_ref, keys, values, kwin, vwin, landed,
):
    copies = start_copies(((w1_hbm, w1_ref), (w2_hbm, w2_ref), (w3_hbm, w3_ref)), landed)
    for b in (0, PAIRS + 1):
        kwin[b] = jnp.zeros((ROWS, LANES), jnp.bfloat16)
        vwin[b] = jnp.zeros((LANES, ROWS), jnp.bfloat16)
    for b in range(PAIRS):
        kwin[b + 1] = got_ref[b, ROWS : 2 * ROWS]
        vwin[b + 1] = jnp.transpose(got_ref[b, 2 * ROWS : 3 * ROWS])
    quarter_of(lambda s, at: got_ref[s, 3 * ROWS + at : 3 * ROWS + at + SHARE], keys, values)
    is_last = place_ref[0] == 3
    full = far_bias(place_ref, rel_ref)

    def one(step, _):
        stacked, split = queries(got_ref, chosen_ref, step)
        parts = [dot(keys[...], split) + jnp.where(is_last, tail_ref[step], full)]
        near_scores = dot(kwin[pl.ds(step, 3)].reshape(3 * ROWS, LANES), stacked)
        for b in range(3):
            at_edge = (step + b == 0) | (step + b == PAIRS + 1)
            cut = slice(b * ROWS, (b + 1) * ROWS)
            bias = near_ref[cut] + jnp.where(at_edge, masked_score, 0.0)
            parts.append(masked(near_scores[cut], name_ref, step + b, asked_ref, step, bias))
        top = jnp.max(functools.reduce(jnp.maximum, parts), axis=0, keepdims=True)
        terms = [jnp.exp(part - top) for part in parts]
        row_sum = jnp.sum(functools.reduce(jnp.add, terms), axis=0, keepdims=True)
        weights = [t.astype(jnp.bfloat16) for t in terms]
        near_values = jnp.concatenate([vwin[step + b] for b in range(3)], axis=1)
        near_out = dot(near_values, jnp.concatenate(weights[1:], axis=0))
        acc_ref[step] = select(asked_ref, step, dot(values[...], weights[0])) + own_head(near_out)
        stat_ref[step, 0:1] = top
        stat_ref[step, 1:2] = row_sum
        return 0

    lax.fori_loop(0, PAIRS, one, 0, unroll=4)
    for copy in copies:
        copy.wait()


def attend_own(place, rel_bias, got, made, later_weights):
    return pl.pallas_call(
        own_kernel,
        in_specs=[SMEM_SPEC] * 2 + [VMEM_SPEC] * 6 + [HBM_SPEC] * 3,
        out_specs=(VMEM_SPEC,) * 5,
        out_shape=(
            pltpu.VMEM((PAIRS, 8, 2 * ROWS), jnp.float32),
            pltpu.VMEM((PAIRS, LANES, ROWS), jnp.float32),
        )
        + tuple(pltpu.VMEM(w.shape, w.dtype) for w in later_weights),
        scratch_shapes=[
            pltpu.VMEM((PLEN // 4, PREF_GRP * LANES), jnp.bfloat16),
            pltpu.VMEM((PREF_GRP * LANES, PLEN // 4), jnp.bfloat16),
            pltpu.VMEM((PAIRS + 2, ROWS, LANES), jnp.bfloat16),
            pltpu.VMEM((PAIRS + 2, LANES, ROWS), jnp.bfloat16),
            pltpu.SemaphoreType.DMA((3,)),
        ],
        compiler_params=pltpu.CompilerParams(vmem_limit_bytes=VMEM_LIMIT),
        cost_estimate=COST,
        name="attend_own",
    )(place, rel_bias.T, *on_chip(got, *made), *off_chip(*later_weights))


def rest_kernel(
    place_ref, rel_ref, got_ref, prev_ref, next_ref, far_ref, near_ref, name_ref, asked_ref, tail_ref, chosen_ref,
    stat_ref, acc_ref, w1_hbm, w2_hbm, w3_hbm, out_ref, w1_ref, w2_ref, w3_ref, keys, values, kwin, vwin, landed,
):
    copies = start_copies(((w1_hbm, w1_ref), (w2_hbm, w2_ref), (w3_hbm, w3_ref)), landed)
    turns = ((3, prev_ref), (1, next_ref), (2, far_ref))
    for i, (_, ref) in enumerate(turns):
        quarter_of(
            lambda s, at, ref=ref: ref[s * 4 * SHARE + at : s * 4 * SHARE + at + SHARE], keys.at[i], values.at[i]
        )
    for i, ref in enumerate((prev_ref, next_ref)):
        kwin[i] = ref[QUARTER : QUARTER + ROWS]
        vwin[i] = jnp.transpose(ref[QUARTER + ROWS :])
    is_last = [lax.rem(place_ref[0] + turn, 4) == 3 for turn, _ in turns]
    side = place_ref[2]
    full = far_bias(place_ref, rel_ref)

    def one(step, edge=None):
        stacked, split = queries(got_ref, chosen_ref, step)
        tail = tail_ref[step]
        scores = dot(keys[...].reshape(3 * PLEN // 4, PREF_GRP * LANES), split)
        parts = [
            scores[i * ROWS : (i + 1) * ROWS] + jnp.where(is_last[i], tail, full) for i in range(3)
        ]
        if edge is not None:
            bias = near_ref[edge * 2 * ROWS : (edge * 2 + 1) * ROWS]
            parts.append(
                masked(dot(kwin[edge], stacked), name_ref, edge * (PAIRS + 1), asked_ref, step, bias)
            )
        before = stat_ref[step, 0:1]
        top = jnp.max(functools.reduce(jnp.maximum, parts), axis=0, keepdims=True)
        top = jnp.maximum(top, before)
        shrink = jnp.exp(before - top)
        terms = [jnp.exp(part - top) for part in parts]
        row_sum = jnp.sum(functools.reduce(jnp.add, terms), axis=0, keepdims=True)
        row_sum = row_sum + stat_ref[step, 1:2] * shrink
        weights = [t.astype(jnp.bfloat16) for t in terms]
        far_values = jnp.concatenate([values[i] for i in range(3)], axis=1)
        far_out = dot(far_values, jnp.concatenate(weights[:3], axis=0))
        acc = acc_ref[step] * by_feature(shrink) + select(asked_ref, step, far_out)
        if edge is not None:
            acc = acc + own_head(dot(vwin[edge], weights[3]))
        done = jnp.transpose(acc * by_feature(1.0 / row_sum)).astype(jnp.bfloat16)
        out_ref[side * PAIRS + step] = done
        out_ref[(1 - side) * PAIRS + jnp.bitwise_xor(step, 1)] = done

    def middle(step, _):
        one(step)
        return 0

    one(jnp.int32(0), 0)
    lax.fori_loop(1, PAIRS - 1, middle, 0, unroll=3)
    one(jnp.int32(PAIRS - 1), 1)
    for copy in copies:
        copy.wait()


def attend_rest(place, rel_bias, got, prev, after_it, far, made, part, later_weights):
    return pl.pallas_call(
        rest_kernel,
        in_specs=[SMEM_SPEC] * 2 + [VMEM_SPEC] * 11 + [HBM_SPEC] * 3,
        out_specs=(VMEM_SPEC,) * 4,
        out_shape=(pltpu.VMEM((2 * PAIRS, ROWS, LANES), jnp.bfloat16),)
        + tuple(pltpu.VMEM(w.shape, w.dtype) for w in later_weights),
        scratch_shapes=[
            pltpu.VMEM((3, PLEN // 4, PREF_GRP * LANES), jnp.bfloat16),
            pltpu.VMEM((3, PREF_GRP * LANES, PLEN // 4), jnp.bfloat16),
            pltpu.VMEM((2, ROWS, LANES), jnp.bfloat16),
            pltpu.VMEM((2, LANES, ROWS), jnp.bfloat16),
            pltpu.SemaphoreType.DMA((3,)),
        ],
        compiler_params=pltpu.CompilerParams(vmem_limit_bytes=VMEM_LIMIT),
        cost_estimate=COST,
        name="attend_rest",
    )(place, rel_bias.T, *on_chip(got, prev, after_it, far, *made, *part), *off_chip(*later_weights))


def finish_kernel(away, place_ref, att_ref, w_ref, tok_ref, gain_ref, in_one, in_two, out_one, out_two, *rest):
    at = (1 - place_ref[2] if away else place_ref[2]) * PAIRS
    attended = jnp.concatenate([att_ref[at + j] for j in range(PAIRS)], axis=1)
    hidden = (tok_ref[...].astype(jnp.float32) + dot(attended, w_ref[...])).astype(jnp.bfloat16)
    normed = norm_rows(hidden, gain_ref[...])
    got = None if away else hidden.astype(jnp.float32)
    for in_ref, out_w_ref in ((in_one, out_one), (in_two, out_two)):
        units = lax.dot_general(
            normed, in_ref[...], (((1,), (1,)), ((), ())), preferred_element_type=jnp.float32
        )
        part = dot(jnp.maximum(units, 0.0).astype(jnp.bfloat16), out_w_ref[...])
        got = part if got is None else got + part
    rest[-1][...] = got.astype(rest[-1].dtype)


def finish(away, place, att, w_attn_out, tokens, gain, weights, *ready):
    return pl.pallas_call(
        functools.partial(finish_kernel, away),
        in_specs=[SMEM_SPEC] + [VMEM_SPEC] * (8 + len(ready)),
        out_specs=VMEM_SPEC,
        out_shape=pltpu.VMEM((ROWS, D), jnp.bfloat16 if away else jnp.float32),
        compiler_params=pltpu.CompilerParams(vmem_limit_bytes=VMEM_LIMIT),
        cost_estimate=COST,
        name="finish",
    )(place, *on_chip(att, w_attn_out, tokens, gain.reshape(1, D), *weights, *ready))


def total_kernel(*refs):
    out_ref = refs[-1]
    total = functools.reduce(jnp.add, [ref[...].astype(jnp.float32) for ref in refs[:-1]])
    out_ref[...] = total.astype(out_ref.dtype)


def total(dtype, *arrays, last=False):
    return pl.pallas_call(
        total_kernel,
        in_specs=[VMEM_SPEC] * len(arrays),
        out_specs=VMEM_SPEC,
        out_shape=(jax.ShapeDtypeStruct if last else pltpu.VMEM)(arrays[0].shape, dtype),
        compiler_params=pltpu.CompilerParams(vmem_limit_bytes=VMEM_LIMIT),
        cost_estimate=COST,
        name="total",
    )(*on_chip(*arrays))


def body(
    tokens,
    attn_gain,
    w_query,
    w_key,
    w_value,
    w_attn_out,
    rel_bias,
    prefix_cache,
    lengths,
    prefix_map,
    mlp_gain,
    w_in,
    w_out,
):
    count_x = lax.axis_size("x")
    plane = lax.axis_index("z") * 2 + lax.axis_index("ylo")
    place = jnp.stack([lax.axis_index("x"), plane, lax.axis_index("yhi")]).astype(jnp.int32)
    made = tables(place, rel_bias, lengths, prefix_map)

    blocks = project(tokens, attn_gain, w_query, w_key, w_value, prefix_cache)
    got = lax.all_to_all(blocks, PLANE, 0, 0, tiled=True)
    mirrored = ("yhi", "ylo")
    far_tokens = lax.ppermute(tokens, mirrored, MIRROR)
    other_in = lax.ppermute(w_in, "core", SWAP)
    other_out = lax.ppermute(w_out, "core", SWAP)
    up, down, far = spread(got, far_tokens, *made)
    by = lambda d: [(i, (i + d) % count_x) for i in range(count_x)]
    prev = lax.ppermute(up, "x", by(1))
    later = lax.ppermute(down, "x", by(-1))
    opposite = lax.ppermute(far, "x", by(2))
    stat, acc, *own_weights = attend_own(place, rel_bias, got, made, (w_attn_out, w_in, w_out))
    mixed, *other_weights = attend_rest(
        place, rel_bias, got, prev, later, opposite, made, (stat, acc), (other_in, other_out, far_tokens)
    )
    w_attn_out = own_weights[0]
    weights = (own_weights[1], other_weights[0], own_weights[2], other_weights[1])
    att = lax.all_to_all(mixed, ("yhi",) + PLANE, 0, 0, tiled=True)

    far_sum = finish(True, place, att, w_attn_out, other_weights[2], mlp_gain, weights)
    back = lax.ppermute(far_sum, mirrored, MIRROR)
    local = finish(False, place, att, w_attn_out, tokens, mlp_gain, weights, far_sum)
    return total(jnp.bfloat16, local, back, last=True)


def solution(mesh):
    split = Mesh(mesh.devices.reshape(2, 2, 4, 4, 2), AXES)
    grp, req = ("yhi", "core"), REQ
    return jax.shard_map(
        body,
        mesh=split,
        in_specs=(
            P(grp + req, None),
            P(),
            P(),
            P(),
            P(),
            P(),
            P(),
            P(grp, req, None),
            P(grp, None),
            P(grp, None),
            P(),
            P(grp, None),
            P(grp, None),
        ),
        out_specs=P(grp + req, None),
        check_vma=False,
    )
```

```python
import functools

import jax
import jax.numpy as jnp
from jax import lax
from jax.experimental import pallas as pl
from jax.experimental.pallas import tpu as pltpu
from jax.sharding import Mesh, PartitionSpec as P

D = 1024
H = 16
DK = 64
PLEN = 512
PREF_GRP = 2
ROWS = 128
PAIRS = 8
LANES = 128
SHARE = 16
SENT = 3 * ROWS + 2 * PREF_GRP * SHARE
QUARTER = PAIRS * 2 * PREF_GRP * SHARE

epsilon = 1e-06
far_marks = (12, 16, 23, 32, 46, 64, 91)
masked_score = -1e30
VMEM_LIMIT = 16 * 1024 * 1024
COST = pl.CostEstimate(flops=1000, transcendentals=0, bytes_accessed=1000)

AXES = ("yhi", "core", "x", "z", "ylo")
REQ = ("x", "z", "ylo")
PLANE = ("z", "ylo")
MIRROR = [(0, 3), (3, 0), (1, 2), (2, 1)]
SWAP = [(0, 1), (1, 0)]


def norm_rows(values_in, gain):
    widened = values_in.astype(jnp.float32)
    scale = lax.rsqrt(jnp.mean(widened * widened, axis=-1, keepdims=True) + epsilon)
    return (widened * scale * gain).astype(jnp.bfloat16)


def dot(a, b):
    return jnp.dot(a, b, preferred_element_type=jnp.float32)


def on_chip(*arrays):
    return tuple(pltpu.with_memory_space_constraint(a, pltpu.VMEM) for a in arrays)


def off_chip(*arrays):
    return tuple(pltpu.with_memory_space_constraint(a, pltpu.HBM) for a in arrays)


VMEM_SPEC = pl.BlockSpec(memory_space=pltpu.VMEM)
HBM_SPEC = pl.BlockSpec(memory_space=pltpu.HBM)
SMEM_SPEC = pl.BlockSpec(memory_space=pltpu.SMEM)


def bias_line(rel_ref, head, first_bucket):
    lane = lax.broadcasted_iota(jnp.int32, (8, LANES), 1)

    def of(bucket):
        return rel_ref[pl.ds(head, 1), first_bucket + bucket : first_bucket + bucket + 1]

    line = jnp.broadcast_to(of(0), (8, LANES))
    for bucket in range(1, 16):
        mark = bucket if bucket <= 8 else far_marks[bucket - 9]
        line = jnp.where(lane >= mark, of(bucket), line)
    return jnp.broadcast_to(line[0:1], (ROWS, LANES))


def write_tables(
    place_ref, rel_ref, len_ref, map_ref, near_ref, name_ref, asked_ref, tail_ref, chosen_ref
):
    row = lax.broadcasted_iota(jnp.int32, (ROWS, LANES), 0)
    lane = lax.broadcasted_iota(jnp.int32, (ROWS, LANES), 1)
    lines = []
    for h in range(2):
        head = place_ref[1] * 2 + h
        before = bias_line(rel_ref, head, 0)
        after_it = bias_line(rel_ref, head, 16)

        def pick(line, distance):
            return jnp.take_along_axis(line, jnp.clip(distance, 0, LANES - 1), axis=1)

        cut = slice(h * ROWS, (h + 1) * ROWS)
        near_ref[0:ROWS, cut] = pick(before, lane + ROWS - row)
        near_ref[ROWS : 2 * ROWS, cut] = jnp.where(
            row > lane, pick(after_it, row - lane), pick(before, lane - row)
        )
        near_ref[2 * ROWS : 3 * ROWS, cut] = pick(after_it, row + ROWS - lane)
        lines.append(before)

    requests = len_ref.shape[1]
    down_it = lax.broadcasted_iota(jnp.int32, (requests, requests), 0)
    along = lax.broadcasted_iota(jnp.int32, (requests, requests), 1)
    length = jnp.broadcast_to(len_ref[...], (requests, requests)).astype(jnp.float32)
    prefix = jnp.broadcast_to(map_ref[...], (requests, requests)).astype(jnp.float32)

    def column(keep, values):
        return jnp.sum(jnp.where(keep, values, 0.0), axis=1, keepdims=True)

    starts = column(along < down_it, length)
    ends = column(along <= down_it, length)
    prefixes = column(along == down_it, prefix)
    number = lax.broadcasted_iota(jnp.int32, (requests, LANES), 0).astype(jnp.float32) + 1.0
    first = place_ref[0] * (PAIRS * ROWS) - ROWS
    for b in range(PAIRS + 2):
        ids = lax.broadcasted_iota(jnp.int32, (requests, LANES), 1) + (first + b * ROWS)
        ids = ids.astype(jnp.float32)
        member = (ids >= starts) & (ids < ends)
        request = jnp.sum(jnp.where(member, number, 0.0), axis=0, keepdims=True) - 1.0
        offset = ids[0:1] - jnp.sum(jnp.where(member, starts, 0.0), axis=0, keepdims=True)
        chosen = jnp.sum(jnp.where(member, prefixes, 0.0), axis=0, keepdims=True)
        facts = jnp.concatenate([request, offset, chosen] + [request] * 5, axis=0)
        name_ref[b] = jnp.broadcast_to(jnp.transpose(facts)[:, 0:1], (ROWS, LANES)).astype(jnp.bfloat16)
        if 0 < b < PAIRS + 1:
            step = b - 1
            asked_ref[step] = facts
            chosen_ref[step] = jnp.broadcast_to(chosen, (ROWS, LANES)).astype(jnp.bfloat16)
            at = jnp.minimum(ROWS - row + jnp.broadcast_to(offset, (ROWS, LANES)).astype(jnp.int32), LANES - 1)
            for h in range(2):
                tail_ref[step, :, h * ROWS : (h + 1) * ROWS] = jnp.take_along_axis(lines[h], at, axis=1)


def project_kernel(
    x_ref, pair_ref, side_ref, tok_hbm, gain_hbm, cache_hbm, rel_hbm, len_hbm, map_hbm, wq_hbm, wk_hbm, wv_hbm,
    out_ref, near_ref, name_ref, asked_ref, tail_ref, chosen_ref,
    tok, gain, cache, rel, lengths, prefix_map, held, arrived, landed,
):
    place_ref = (x_ref[0], pair_ref[0], side_ref[0])
    first = [
        pltpu.make_async_copy(source, target, landed.at[i])
        for i, (source, target) in enumerate(
            (
                (tok_hbm, tok), (gain_hbm, gain), (cache_hbm, cache),
                (rel_hbm, rel), (len_hbm, lengths), (map_hbm, prefix_map),
            )
        )
    ]
    copies = [
        pltpu.make_async_copy(w_hbm, held.at[kind], arrived.at[kind])
        for kind, w_hbm in enumerate((wq_hbm, wk_hbm, wv_hbm))
    ]
    for copy in first + copies:
        copy.start()
    for copy in first:
        copy.wait()
    normed = norm_rows(tok[...], gain[...])
    for part in range(PAIRS):
        for kind in range(2):
            for p in range(PREF_GRP):
                at = 3 * ROWS + (kind * PREF_GRP + p) * SHARE
                cut = slice(kind * D + part * LANES, kind * D + (part + 1) * LANES)
                out_ref[part, at : at + SHARE] = cache[p, :, cut]
    write_tables(
        place_ref, rel, lengths, prefix_map, near_ref, name_ref, asked_ref, tail_ref, chosen_ref
    )
    for kind, copy in enumerate(copies):
        copy.wait()
        got = dot(normed, held[kind]).astype(jnp.bfloat16)
        for to in range(PAIRS):
            out_ref[to, kind * ROWS : (kind + 1) * ROWS] = got[:, to * LANES : (to + 1) * LANES]


def project(place, tokens, gain, prefix_cache, rel_bias, lengths, prefix_map, w_query, w_key, w_value):
    small = (tokens, gain.reshape(1, D), prefix_cache, rel_bias.T, lengths, prefix_map)
    out_shape = (
        pltpu.VMEM((PAIRS, SENT, LANES), jnp.bfloat16),
        pltpu.VMEM((3 * ROWS, 2 * ROWS), jnp.float32),
        pltpu.VMEM((PAIRS + 2, ROWS, LANES), jnp.bfloat16),
        pltpu.VMEM((PAIRS, 8, ROWS), jnp.float32),
        pltpu.VMEM((PAIRS, ROWS, 2 * ROWS), jnp.float32),
        pltpu.VMEM((PAIRS, ROWS, ROWS), jnp.bfloat16),
    )
    blocks, *made = pl.pallas_call(
        project_kernel,
        in_specs=[SMEM_SPEC] * 3 + [HBM_SPEC] * 9,
        out_specs=(VMEM_SPEC,) * 6,
        out_shape=out_shape,
        scratch_shapes=[pltpu.VMEM(value.shape, value.dtype) for value in small]
        + [
            pltpu.VMEM((3, D, D), jnp.bfloat16),
            pltpu.SemaphoreType.DMA((3,)),
            pltpu.SemaphoreType.DMA((6,)),
        ],
        compiler_params=pltpu.CompilerParams(vmem_limit_bytes=VMEM_LIMIT),
        cost_estimate=COST,
        name="project",
    )(*place, *off_chip(*small, w_query, w_key, w_value))
    return blocks, made


def spread_kernel(got_ref, tok_ref, *rest):
    up_ref, down_ref, far_ref, same_ref = rest[-4:]
    for source in range(PAIRS):
        rows = slice(source * 4 * SHARE, (source + 1) * 4 * SHARE)
        held = got_ref[source, 3 * ROWS :]
        up_ref[rows] = held
        down_ref[rows] = held
        far_ref[rows] = held
    up_ref[QUARTER:] = got_ref[PAIRS - 1, ROWS : 3 * ROWS]
    down_ref[QUARTER:] = got_ref[0, ROWS : 3 * ROWS]
    same_ref[...] = tok_ref[...]


def spread(got, tokens, on, off):
    shape = pltpu.VMEM((QUARTER + 2 * ROWS, LANES), jnp.bfloat16)
    return pl.pallas_call(
        spread_kernel,
        in_specs=[VMEM_SPEC] * 3 + [HBM_SPEC],
        out_specs=(VMEM_SPEC,) * 4,
        out_shape=(
            shape,
            shape,
            pltpu.VMEM((QUARTER, LANES), jnp.bfloat16),
            pltpu.VMEM((ROWS, D), jnp.bfloat16),
        ),
        compiler_params=pltpu.CompilerParams(vmem_limit_bytes=VMEM_LIMIT),
        cost_estimate=COST,
        name="spread",
    )(*on_chip(got, tokens, on), *off_chip(off))


def queries(got_ref, chosen_ref, step):
    query = jnp.transpose(got_ref[step, 0:ROWS])
    zero = jnp.zeros((DK, ROWS), jnp.bfloat16)
    stacked = jnp.concatenate(
        [jnp.concatenate([query[:DK], zero], axis=0), jnp.concatenate([zero, query[DK:]], axis=0)], axis=1
    )
    chosen = jnp.concatenate([chosen_ref[step], chosen_ref[step]], axis=1)
    return stacked, jnp.concatenate([stacked * (1 - chosen), stacked * chosen], axis=0)


def masked(scores, name_ref, block, asked_ref, step, bias):
    mine = name_ref[block].astype(jnp.float32) == asked_ref[step, 0:1]
    mine = jnp.concatenate([mine, mine], axis=1)
    return jnp.where(mine, scores + bias, masked_score)


def far_bias(place_ref, rel_ref):
    lane = lax.broadcasted_iota(jnp.int32, (1, 2 * ROWS), 1)
    head = place_ref[1] * 2
    return jnp.where(lane < ROWS, rel_ref[head, 15], rel_ref[head + 1, 15])


def own_head(values):
    return jnp.concatenate([values[:DK, :ROWS], values[DK:, ROWS:]], axis=0)


def by_feature(line):
    return jnp.concatenate(
        [jnp.broadcast_to(line[:, :ROWS], (DK, ROWS)), jnp.broadcast_to(line[:, ROWS:], (DK, ROWS))], axis=0
    )


def select(asked_ref, step, far_out):
    second = jnp.broadcast_to(asked_ref[step, 2:3], (LANES, ROWS)) > 0.5
    return jnp.where(second, own_head(far_out[LANES:]), own_head(far_out[:LANES]))


def quarter_of(rows_at, keys_ref, values_ref):
    for p in range(PREF_GRP):
        pieces = [
            jnp.concatenate(
                [rows_at(source, (kind * PREF_GRP + p) * SHARE) for source in range(PAIRS)], axis=0
            )
            for kind in range(2)
        ]
        keys_ref[:, p * LANES : (p + 1) * LANES] = pieces[0]
        values_ref[p * LANES : (p + 1) * LANES, :] = jnp.transpose(pieces[1])


def start_copies(pairs, landed):
    copies = [pltpu.make_async_copy(a, b, landed.at[i]) for i, (a, b) in enumerate(pairs)]
    for copy in copies:
        copy.start()
    return copies


def own_kernel(
    x_ref, pair_ref, side_ref, rel_ref, got_ref, near_ref, name_ref, asked_ref, tail_ref, chosen_ref, w1_hbm,
    stat_ref, acc_ref, w1_ref, keys, values, kwin, vwin, landed,
):
    place_ref = (x_ref[0], pair_ref[0], side_ref[0])
    copies = start_copies(((w1_hbm, w1_ref),), landed)
    for b in (0, PAIRS + 1):
        kwin[b] = jnp.zeros((ROWS, LANES), jnp.bfloat16)
        vwin[b] = jnp.zeros((LANES, ROWS), jnp.bfloat16)
    for b in range(PAIRS):
        kwin[b + 1] = got_ref[b, ROWS : 2 * ROWS]
        vwin[b + 1] = jnp.transpose(got_ref[b, 2 * ROWS : 3 * ROWS])
    quarter_of(lambda s, at: got_ref[s, 3 * ROWS + at : 3 * ROWS + at + SHARE], keys, values)
    is_last = place_ref[0] == 3
    full = far_bias(place_ref, rel_ref)

    def one(step, _):
        stacked, split = queries(got_ref, chosen_ref, step)
        parts = [dot(keys[...], split) + jnp.where(is_last, tail_ref[step], full)]
        near_scores = dot(kwin[pl.ds(step, 3)].reshape(3 * ROWS, LANES), stacked)
        for b in range(3):
            at_edge = (step + b == 0) | (step + b == PAIRS + 1)
            cut = slice(b * ROWS, (b + 1) * ROWS)
            bias = near_ref[cut] + jnp.where(at_edge, masked_score, 0.0)
            parts.append(masked(near_scores[cut], name_ref, step + b, asked_ref, step, bias))
        top = jnp.max(functools.reduce(jnp.maximum, parts), axis=0, keepdims=True)
        terms = [jnp.exp(part - top) for part in parts]
        row_sum = jnp.sum(functools.reduce(jnp.add, terms), axis=0, keepdims=True)
        weights = [t.astype(jnp.bfloat16) for t in terms]
        near_values = jnp.concatenate([vwin[step + b] for b in range(3)], axis=1)
        near_out = dot(near_values, jnp.concatenate(weights[1:], axis=0))
        acc_ref[step] = select(asked_ref, step, dot(values[...], weights[0])) + own_head(near_out)
        stat_ref[step, 0:1] = top
        stat_ref[step, 1:2] = row_sum
        return 0

    lax.fori_loop(0, PAIRS, one, 0, unroll=4)
    for copy in copies:
        copy.wait()


def attend_own(place, rel_bias, got, made, later_weights):
    return pl.pallas_call(
        own_kernel,
        in_specs=[SMEM_SPEC] * 4 + [VMEM_SPEC] * 6 + [HBM_SPEC],
        out_specs=(VMEM_SPEC,) * 3,
        out_shape=(
            pltpu.VMEM((PAIRS, 8, 2 * ROWS), jnp.float32),
            pltpu.VMEM((PAIRS, LANES, ROWS), jnp.float32),
        )
        + tuple(pltpu.VMEM(w.shape, w.dtype) for w in later_weights),
        scratch_shapes=[
            pltpu.VMEM((PLEN // 4, PREF_GRP * LANES), jnp.bfloat16),
            pltpu.VMEM((PREF_GRP * LANES, PLEN // 4), jnp.bfloat16),
            pltpu.VMEM((PAIRS + 2, ROWS, LANES), jnp.bfloat16),
            pltpu.VMEM((PAIRS + 2, LANES, ROWS), jnp.bfloat16),
            pltpu.SemaphoreType.DMA((1,)),
        ],
        compiler_params=pltpu.CompilerParams(vmem_limit_bytes=VMEM_LIMIT),
        cost_estimate=COST,
        name="attend_own",
    )(*place, rel_bias.T, *on_chip(got, *made), *off_chip(*later_weights))


def rest_kernel(
    x_ref, pair_ref, side_ref, rel_ref, got_ref, prev_ref, next_ref, far_ref, near_ref, name_ref, asked_ref, tail_ref, chosen_ref,
    stat_ref, acc_ref, _, out_ref, keys, values, kwin, vwin,
):
    place_ref = (x_ref[0], pair_ref[0], side_ref[0])
    turns = ((3, prev_ref), (1, next_ref), (2, far_ref))
    for i, (_, ref) in enumerate(turns):
        quarter_of(
            lambda s, at, ref=ref: ref[s * 4 * SHARE + at : s * 4 * SHARE + at + SHARE], keys.at[i], values.at[i]
        )
    for i, ref in enumerate((prev_ref, next_ref)):
        kwin[i] = ref[QUARTER : QUARTER + ROWS]
        vwin[i] = jnp.transpose(ref[QUARTER + ROWS :])
    is_last = [lax.rem(place_ref[0] + turn, 4) == 3 for turn, _ in turns]
    side = place_ref[2]
    full = far_bias(place_ref, rel_ref)

    def one(step, edge=None):
        stacked, split = queries(got_ref, chosen_ref, step)
        tail = tail_ref[step]
        scores = dot(keys[...].reshape(3 * PLEN // 4, PREF_GRP * LANES), split)
        parts = [
            scores[i * ROWS : (i + 1) * ROWS] + jnp.where(is_last[i], tail, full) for i in range(3)
        ]
        if edge is not None:
            bias = near_ref[edge * 2 * ROWS : (edge * 2 + 1) * ROWS]
            parts.append(
                masked(dot(kwin[edge], stacked), name_ref, edge * (PAIRS + 1), asked_ref, step, bias)
            )
        before = stat_ref[step, 0:1]
        top = jnp.max(functools.reduce(jnp.maximum, parts), axis=0, keepdims=True)
        top = jnp.maximum(top, before)
        shrink = jnp.exp(before - top)
        terms = [jnp.exp(part - top) for part in parts]
        row_sum = jnp.sum(functools.reduce(jnp.add, terms), axis=0, keepdims=True)
        row_sum = row_sum + stat_ref[step, 1:2] * shrink
        weights = [t.astype(jnp.bfloat16) for t in terms]
        far_values = jnp.concatenate([values[i] for i in range(3)], axis=1)
        far_out = dot(far_values, jnp.concatenate(weights[:3], axis=0))
        acc = acc_ref[step] * by_feature(shrink) + select(asked_ref, step, far_out)
        if edge is not None:
            acc = acc + own_head(dot(vwin[edge], weights[3]))
        done = jnp.transpose(acc * by_feature(1.0 / row_sum)).astype(jnp.bfloat16)
        out_ref[side * PAIRS + step] = done
        out_ref[(1 - side) * PAIRS + jnp.bitwise_xor(step, 1)] = done

    def middle(step, _):
        one(step)
        return 0

    one(jnp.int32(0), 0)
    lax.fori_loop(1, PAIRS - 1, middle, 0, unroll=3)
    one(jnp.int32(PAIRS - 1), 1)


def attend_rest(place, rel_bias, got, prev, after_it, far, made, part, ready):
    return pl.pallas_call(
        rest_kernel,
        in_specs=[SMEM_SPEC] * 4 + [VMEM_SPEC] * 12,
        out_specs=VMEM_SPEC,
        out_shape=pltpu.VMEM((2 * PAIRS, ROWS, LANES), jnp.bfloat16),
        scratch_shapes=[
            pltpu.VMEM((3, PLEN // 4, PREF_GRP * LANES), jnp.bfloat16),
            pltpu.VMEM((3, PREF_GRP * LANES, PLEN // 4), jnp.bfloat16),
            pltpu.VMEM((2, ROWS, LANES), jnp.bfloat16),
            pltpu.VMEM((2, LANES, ROWS), jnp.bfloat16),
        ],
        compiler_params=pltpu.CompilerParams(vmem_limit_bytes=VMEM_LIMIT),
        cost_estimate=COST,
        name="attend_rest",
    )(*place, rel_bias.T, *on_chip(got, prev, after_it, far, *made, *part, ready))


def finish_kernel(away, side_ref, att_ref, w_ref, tok_ref, gain_ref, in_one, in_two, out_one, out_two, *rest):
    at = (1 - side_ref[0] if away else side_ref[0]) * PAIRS
    attended = jnp.concatenate([att_ref[at + j] for j in range(PAIRS)], axis=1)
    hidden = (tok_ref[...].astype(jnp.float32) + dot(attended, w_ref[...])).astype(jnp.bfloat16)
    normed = norm_rows(hidden, gain_ref[...])
    got = None if away else hidden.astype(jnp.float32)
    for in_ref, out_w_ref in ((in_one, out_one), (in_two, out_two)):
        units = lax.dot_general(
            normed, in_ref[...], (((1,), (1,)), ((), ())), preferred_element_type=jnp.float32
        )
        part = dot(jnp.maximum(units, 0.0).astype(jnp.bfloat16), out_w_ref[...])
        got = part if got is None else got + part
    rest[-1][...] = got.astype(rest[-1].dtype)


def finish(away, side, att, w_attn_out, tokens, gain, weights, *ready):
    return pl.pallas_call(
        functools.partial(finish_kernel, away),
        in_specs=[SMEM_SPEC] + [VMEM_SPEC] * (8 + len(ready)),
        out_specs=VMEM_SPEC,
        out_shape=pltpu.VMEM((ROWS, D), jnp.bfloat16 if away else jnp.float32),
        compiler_params=pltpu.CompilerParams(vmem_limit_bytes=VMEM_LIMIT),
        cost_estimate=COST,
        name="finish",
    )(side, *on_chip(att, w_attn_out, tokens, gain.reshape(1, D), *weights, *ready))


def total_kernel(*refs):
    out_ref = refs[-1]
    total = functools.reduce(jnp.add, [ref[...].astype(jnp.float32) for ref in refs[:-1]])
    out_ref[...] = total.astype(out_ref.dtype)


def total(dtype, *arrays, last=False):
    return pl.pallas_call(
        total_kernel,
        in_specs=[VMEM_SPEC] * len(arrays),
        out_specs=VMEM_SPEC,
        out_shape=(jax.ShapeDtypeStruct if last else pltpu.VMEM)(arrays[0].shape, dtype),
        compiler_params=pltpu.CompilerParams(vmem_limit_bytes=VMEM_LIMIT),
        cost_estimate=COST,
        name="total",
    )(*on_chip(*arrays))


def body(
    tokens,
    attn_gain,
    w_query,
    w_key,
    w_value,
    w_attn_out,
    rel_bias,
    prefix_cache,
    lengths,
    prefix_map,
    mlp_gain,
    w_in,
    w_out,
):
    count_x = lax.axis_size("x")
    plane = lax.axis_index("z") * 2 + lax.axis_index("ylo")
    place = tuple(
        at.astype(jnp.int32).reshape(1) for at in (lax.axis_index("x"), plane, lax.axis_index("yhi"))
    )
    other_in = lax.ppermute(w_in, "core", SWAP)
    other_out = lax.ppermute(w_out, "core", SWAP)
    blocks, made = project(
        place, tokens, attn_gain, prefix_cache, rel_bias, lengths, prefix_map, w_query, w_key, w_value
    )
    got = lax.all_to_all(blocks, PLANE, 0, 0, tiled=True)
    mirrored = ("yhi", "ylo")
    up, down, far, same = spread(got, tokens, other_in, other_out)
    by = lambda d: [(i, (i + d) % count_x) for i in range(count_x)]
    opposite = lax.ppermute(far, "x", by(2))
    prev = lax.ppermute(up, "x", by(1))
    later = lax.ppermute(down, "x", by(-1))
    far_tokens = lax.ppermute(same, mirrored, MIRROR)
    stat, acc, other_out = attend_own(place, rel_bias, got, made, (other_out,))
    mixed = attend_rest(place, rel_bias, got, prev, later, opposite, made, (stat, acc), far_tokens)
    weights = (w_in, other_in, w_out, other_out)
    att = lax.all_to_all(mixed, ("yhi",) + PLANE, 0, 0, tiled=True)

    far_sum = finish(True, place[2], att, w_attn_out, far_tokens, mlp_gain, weights)
    back = lax.ppermute(far_sum, mirrored, MIRROR)
    local = finish(False, place[2], att, w_attn_out, tokens, mlp_gain, weights, far_sum)
    return total(jnp.bfloat16, local, back, last=True)


def solution(mesh):
    split = Mesh(mesh.devices.reshape(2, 2, 4, 4, 2), AXES)
    grp, req = ("yhi", "core"), REQ
    return jax.shard_map(
        body,
        mesh=split,
        in_specs=(
            P(grp + req, None),
            P(),
            P(),
            P(),
            P(),
            P(),
            P(),
            P(grp, req, None),
            P(grp, None),
            P(grp, None),
            P(),
            P(grp, None),
            P(grp, None),
        ),
        out_specs=P(grp + req, None),
        check_vma=False,
    )
```

```python
import functools

import jax
import jax.numpy as jnp
from jax import lax
from jax.experimental import pallas as pl
from jax.experimental.pallas import tpu as pltpu
from jax.sharding import Mesh, PartitionSpec as P

D = 1024
H = 16
DK = 64
PLEN = 512
PREF_GRP = 2
ROWS = 128
PAIRS = 8
LANES = 128
SHARE = 16
SENT = 3 * ROWS + 2 * PREF_GRP * SHARE
QUARTER = PAIRS * 2 * PREF_GRP * SHARE

epsilon = 1e-06
far_marks = (12, 16, 23, 32, 46, 64, 91)
masked_score = -1e30
VMEM_LIMIT = 16 * 1024 * 1024
COST = pl.CostEstimate(flops=1000, transcendentals=0, bytes_accessed=1000)

AXES = ("yhi", "core", "x", "z", "ylo")
REQ = ("x", "z", "ylo")
PLANE = ("z", "ylo")
MIRROR = [(0, 3), (3, 0), (1, 2), (2, 1)]
SWAP = [(0, 1), (1, 0)]


def norm_rows(values_in, gain):
    widened = values_in.astype(jnp.float32)
    scale = lax.rsqrt(jnp.mean(widened * widened, axis=-1, keepdims=True) + epsilon)
    return (widened * scale * gain).astype(jnp.bfloat16)


def dot(a, b):
    return jnp.dot(a, b, preferred_element_type=jnp.float32)


def on_chip(*arrays):
    return tuple(pltpu.with_memory_space_constraint(a, pltpu.VMEM) for a in arrays)


def off_chip(*arrays):
    return tuple(pltpu.with_memory_space_constraint(a, pltpu.HBM) for a in arrays)


VMEM_SPEC = pl.BlockSpec(memory_space=pltpu.VMEM)
HBM_SPEC = pl.BlockSpec(memory_space=pltpu.HBM)
SMEM_SPEC = pl.BlockSpec(memory_space=pltpu.SMEM)


def bias_line(rel_ref, head, first_bucket):
    lane = lax.broadcasted_iota(jnp.int32, (8, LANES), 1)

    def of(bucket):
        return rel_ref[pl.ds(head, 1), first_bucket + bucket : first_bucket + bucket + 1]

    line = jnp.broadcast_to(of(0), (8, LANES))
    for bucket in range(1, 16):
        mark = bucket if bucket <= 8 else far_marks[bucket - 9]
        line = jnp.where(lane >= mark, of(bucket), line)
    return jnp.broadcast_to(line[0:1], (ROWS, LANES))


def write_tables(
    place_ref, rel_ref, len_ref, map_ref, near_ref, name_ref, asked_ref, tail_ref, chosen_ref
):
    row = lax.broadcasted_iota(jnp.int32, (ROWS, LANES), 0)
    lane = lax.broadcasted_iota(jnp.int32, (ROWS, LANES), 1)
    lines = []
    for h in range(2):
        head = place_ref[1] * 2 + h
        before = bias_line(rel_ref, head, 0)
        after_it = bias_line(rel_ref, head, 16)

        def pick(line, distance):
            return jnp.take_along_axis(line, jnp.clip(distance, 0, LANES - 1), axis=1)

        cut = slice(h * ROWS, (h + 1) * ROWS)
        near_ref[0:ROWS, cut] = pick(before, lane + ROWS - row)
        near_ref[ROWS : 2 * ROWS, cut] = jnp.where(
            row > lane, pick(after_it, row - lane), pick(before, lane - row)
        )
        near_ref[2 * ROWS : 3 * ROWS, cut] = pick(after_it, row + ROWS - lane)
        lines.append(before)

    requests = len_ref.shape[1]
    down_it = lax.broadcasted_iota(jnp.int32, (requests, requests), 0)
    along = lax.broadcasted_iota(jnp.int32, (requests, requests), 1)
    length = jnp.broadcast_to(len_ref[...], (requests, requests)).astype(jnp.float32)
    prefix = jnp.broadcast_to(map_ref[...], (requests, requests)).astype(jnp.float32)

    def column(keep, values):
        return jnp.sum(jnp.where(keep, values, 0.0), axis=1, keepdims=True)

    starts = column(along < down_it, length)
    ends = column(along <= down_it, length)
    prefixes = column(along == down_it, prefix)
    number = lax.broadcasted_iota(jnp.int32, (requests, LANES), 0).astype(jnp.float32) + 1.0
    first = place_ref[0] * (PAIRS * ROWS) - ROWS
    for b in range(PAIRS + 2):
        ids = lax.broadcasted_iota(jnp.int32, (requests, LANES), 1) + (first + b * ROWS)
        ids = ids.astype(jnp.float32)
        member = (ids >= starts) & (ids < ends)
        request = jnp.sum(jnp.where(member, number, 0.0), axis=0, keepdims=True) - 1.0
        offset = ids[0:1] - jnp.sum(jnp.where(member, starts, 0.0), axis=0, keepdims=True)
        chosen = jnp.sum(jnp.where(member, prefixes, 0.0), axis=0, keepdims=True)
        facts = jnp.concatenate([request, offset, chosen] + [request] * 5, axis=0)
        name_ref[b] = jnp.broadcast_to(jnp.transpose(facts)[:, 0:1], (ROWS, LANES)).astype(jnp.bfloat16)
        if 0 < b < PAIRS + 1:
            step = b - 1
            asked_ref[step] = facts
            chosen_ref[step] = jnp.broadcast_to(chosen, (ROWS, LANES)).astype(jnp.bfloat16)
            at = jnp.minimum(ROWS - row + jnp.broadcast_to(offset, (ROWS, LANES)).astype(jnp.int32), LANES - 1)
            for h in range(2):
                tail_ref[step, :, h * ROWS : (h + 1) * ROWS] = jnp.take_along_axis(lines[h], at, axis=1)


def project_kernel(
    x_ref, pair_ref, side_ref, tok_hbm, gain_hbm, cache_hbm, rel_hbm, len_hbm, map_hbm, wq_hbm, wk_hbm, wv_hbm,
    out_ref, near_ref, name_ref, asked_ref, tail_ref, chosen_ref,
    tok, gain, cache, rel, lengths, prefix_map, held, arrived, landed,
):
    place_ref = (x_ref[0], pair_ref[0], side_ref[0])
    first = [
        pltpu.make_async_copy(source, target, landed.at[i])
        for i, (source, target) in enumerate(
            (
                (tok_hbm, tok), (gain_hbm, gain), (cache_hbm, cache),
                (rel_hbm, rel), (len_hbm, lengths), (map_hbm, prefix_map),
            )
        )
    ]
    copies = [
        pltpu.make_async_copy(w_hbm, held.at[kind], arrived.at[kind])
        for kind, w_hbm in enumerate((wq_hbm, wk_hbm, wv_hbm))
    ]
    for copy in first + copies[:2]:
        copy.start()
    for copy in first:
        copy.wait()
    normed = norm_rows(tok[...], gain[...])
    for part in range(PAIRS):
        for kind in range(2):
            for p in range(PREF_GRP):
                at = 3 * ROWS + (kind * PREF_GRP + p) * SHARE
                cut = slice(kind * D + part * LANES, kind * D + (part + 1) * LANES)
                out_ref[part, at : at + SHARE] = cache[p, :, cut]
    write_tables(
        place_ref, rel, lengths, prefix_map, near_ref, name_ref, asked_ref, tail_ref, chosen_ref
    )
    for kind, copy in enumerate(copies):
        copy.wait()
        if kind == 0:
            copies[2].start()
        got = dot(normed, held[kind]).astype(jnp.bfloat16)
        for to in range(PAIRS):
            out_ref[to, kind * ROWS : (kind + 1) * ROWS] = got[:, to * LANES : (to + 1) * LANES]


def project(place, tokens, gain, prefix_cache, rel_bias, lengths, prefix_map, w_query, w_key, w_value):
    small = (tokens, gain.reshape(1, D), prefix_cache, rel_bias.T, lengths, prefix_map)
    out_shape = (
        pltpu.VMEM((PAIRS, SENT, LANES), jnp.bfloat16),
        pltpu.VMEM((3 * ROWS, 2 * ROWS), jnp.float32),
        pltpu.VMEM((PAIRS + 2, ROWS, LANES), jnp.bfloat16),
        pltpu.VMEM((PAIRS, 8, ROWS), jnp.float32),
        pltpu.VMEM((PAIRS, ROWS, 2 * ROWS), jnp.float32),
        pltpu.VMEM((PAIRS, ROWS, ROWS), jnp.bfloat16),
    )
    blocks, *made = pl.pallas_call(
        project_kernel,
        in_specs=[SMEM_SPEC] * 3 + [HBM_SPEC] * 9,
        out_specs=(VMEM_SPEC,) * 6,
        out_shape=out_shape,
        scratch_shapes=[pltpu.VMEM(value.shape, value.dtype) for value in small]
        + [
            pltpu.VMEM((3, D, D), jnp.bfloat16),
            pltpu.SemaphoreType.DMA((3,)),
            pltpu.SemaphoreType.DMA((6,)),
        ],
        compiler_params=pltpu.CompilerParams(vmem_limit_bytes=VMEM_LIMIT),
        cost_estimate=COST,
        name="project",
    )(*place, *off_chip(*small, w_query, w_key, w_value))
    return blocks, made


def hold(value, arrived):
    return pl.pallas_call(
        lambda value_ref, arrived_ref, out_ref: None,
        in_specs=[VMEM_SPEC] * 2,
        out_specs=VMEM_SPEC,
        out_shape=pltpu.VMEM(value.shape, value.dtype),
        input_output_aliases={0: 0},
        compiler_params=pltpu.CompilerParams(vmem_limit_bytes=VMEM_LIMIT),
        cost_estimate=COST,
        name="hold",
    )(*on_chip(value, arrived))


def spread_kernel(got_ref, *rest):
    up_ref, down_ref, far_ref = rest[-3:]
    for source in range(PAIRS):
        rows = slice(source * 4 * SHARE, (source + 1) * 4 * SHARE)
        held = got_ref[source, 3 * ROWS :]
        up_ref[rows] = held
        down_ref[rows] = held
        far_ref[rows] = held
    up_ref[QUARTER:] = got_ref[PAIRS - 1, ROWS : 3 * ROWS]
    down_ref[QUARTER:] = got_ref[0, ROWS : 3 * ROWS]


def spread(got, on, off):
    shape = pltpu.VMEM((QUARTER + 2 * ROWS, LANES), jnp.bfloat16)
    return pl.pallas_call(
        spread_kernel,
        in_specs=[VMEM_SPEC] * 2 + [HBM_SPEC],
        out_specs=(VMEM_SPEC,) * 3,
        out_shape=(shape, shape, pltpu.VMEM((QUARTER, LANES), jnp.bfloat16)),
        compiler_params=pltpu.CompilerParams(vmem_limit_bytes=VMEM_LIMIT),
        cost_estimate=COST,
        name="spread",
    )(*on_chip(got, on), *off_chip(off))


def queries(got_ref, chosen_ref, step):
    query = jnp.transpose(got_ref[step, 0:ROWS])
    zero = jnp.zeros((DK, ROWS), jnp.bfloat16)
    stacked = jnp.concatenate(
        [jnp.concatenate([query[:DK], zero], axis=0), jnp.concatenate([zero, query[DK:]], axis=0)], axis=1
    )
    chosen = jnp.concatenate([chosen_ref[step], chosen_ref[step]], axis=1)
    return stacked, jnp.concatenate([stacked * (1 - chosen), stacked * chosen], axis=0)


def masked(scores, name_ref, block, asked_ref, step, bias):
    mine = name_ref[block].astype(jnp.float32) == asked_ref[step, 0:1]
    mine = jnp.concatenate([mine, mine], axis=1)
    return jnp.where(mine, scores + bias, masked_score)


def far_bias(place_ref, rel_ref):
    lane = lax.broadcasted_iota(jnp.int32, (1, 2 * ROWS), 1)
    head = place_ref[1] * 2
    return jnp.where(lane < ROWS, rel_ref[head, 15], rel_ref[head + 1, 15])


def own_head(values):
    return jnp.concatenate([values[:DK, :ROWS], values[DK:, ROWS:]], axis=0)


def by_feature(line):
    return jnp.concatenate(
        [jnp.broadcast_to(line[:, :ROWS], (DK, ROWS)), jnp.broadcast_to(line[:, ROWS:], (DK, ROWS))], axis=0
    )


def select(asked_ref, step, far_out):
    second = jnp.broadcast_to(asked_ref[step, 2:3], (LANES, ROWS)) > 0.5
    return jnp.where(second, own_head(far_out[LANES:]), own_head(far_out[:LANES]))


def quarter_of(rows_at, keys_ref, values_ref):
    for p in range(PREF_GRP):
        pieces = [
            jnp.concatenate(
                [rows_at(source, (kind * PREF_GRP + p) * SHARE) for source in range(PAIRS)], axis=0
            )
            for kind in range(2)
        ]
        keys_ref[:, p * LANES : (p + 1) * LANES] = pieces[0]
        values_ref[p * LANES : (p + 1) * LANES, :] = jnp.transpose(pieces[1])


def start_copies(pairs, landed):
    copies = [pltpu.make_async_copy(a, b, landed.at[i]) for i, (a, b) in enumerate(pairs)]
    for copy in copies:
        copy.start()
    return copies


def own_kernel(
    x_ref, pair_ref, side_ref, rel_ref, got_ref, near_ref, name_ref, asked_ref, tail_ref, chosen_ref, w1_hbm,
    stat_ref, acc_ref, split_ref, w1_ref, keys, values, kwin, vwin, landed,
):
    place_ref = (x_ref[0], pair_ref[0], side_ref[0])
    copies = start_copies(((w1_hbm, w1_ref),), landed)
    for b in (0, PAIRS + 1):
        kwin[b] = jnp.zeros((ROWS, LANES), jnp.bfloat16)
        vwin[b] = jnp.zeros((LANES, ROWS), jnp.bfloat16)
    for b in range(PAIRS):
        kwin[b + 1] = got_ref[b, ROWS : 2 * ROWS]
        vwin[b + 1] = jnp.transpose(got_ref[b, 2 * ROWS : 3 * ROWS])
    quarter_of(lambda s, at: got_ref[s, 3 * ROWS + at : 3 * ROWS + at + SHARE], keys, values)
    is_last = place_ref[0] == 3
    full = far_bias(place_ref, rel_ref)

    def one(step, _):
        stacked, split = queries(got_ref, chosen_ref, step)
        split_ref[step] = split
        parts = [dot(keys[...], split) + jnp.where(is_last, tail_ref[step], full)]
        near_scores = dot(kwin[pl.ds(step, 3)].reshape(3 * ROWS, LANES), stacked)
        for b in range(3):
            at_edge = (step + b == 0) | (step + b == PAIRS + 1)
            cut = slice(b * ROWS, (b + 1) * ROWS)
            bias = near_ref[cut] + jnp.where(at_edge, masked_score, 0.0)
            parts.append(masked(near_scores[cut], name_ref, step + b, asked_ref, step, bias))
        top = jnp.max(functools.reduce(jnp.maximum, parts), axis=0, keepdims=True)
        terms = [jnp.exp(part - top) for part in parts]
        row_sum = jnp.sum(functools.reduce(jnp.add, terms), axis=0, keepdims=True)
        weights = [t.astype(jnp.bfloat16) for t in terms]
        near_values = jnp.concatenate([vwin[step + b] for b in range(3)], axis=1)
        near_out = dot(near_values, jnp.concatenate(weights[1:], axis=0))
        acc_ref[step] = select(asked_ref, step, dot(values[...], weights[0])) + own_head(near_out)
        stat_ref[step, 0:1] = top
        stat_ref[step, 1:2] = row_sum
        return 0

    lax.fori_loop(0, PAIRS, one, 0, unroll=4)
    for copy in copies:
        copy.wait()


def attend_own(place, rel_bias, got, made, later_weights):
    return pl.pallas_call(
        own_kernel,
        in_specs=[SMEM_SPEC] * 4 + [VMEM_SPEC] * 6 + [HBM_SPEC],
        out_specs=(VMEM_SPEC,) * 4,
        out_shape=(
            pltpu.VMEM((PAIRS, 8, 2 * ROWS), jnp.float32),
            pltpu.VMEM((PAIRS, LANES, ROWS), jnp.float32),
            pltpu.VMEM((PAIRS, PREF_GRP * LANES, 2 * ROWS), jnp.bfloat16),
        )
        + tuple(pltpu.VMEM(w.shape, w.dtype) for w in later_weights),
        scratch_shapes=[
            pltpu.VMEM((PLEN // 4, PREF_GRP * LANES), jnp.bfloat16),
            pltpu.VMEM((PREF_GRP * LANES, PLEN // 4), jnp.bfloat16),
            pltpu.VMEM((PAIRS + 2, ROWS, LANES), jnp.bfloat16),
            pltpu.VMEM((PAIRS + 2, LANES, ROWS), jnp.bfloat16),
            pltpu.SemaphoreType.DMA((1,)),
        ],
        compiler_params=pltpu.CompilerParams(vmem_limit_bytes=VMEM_LIMIT),
        cost_estimate=COST,
        name="attend_own",
    )(*place, rel_bias.T, *on_chip(got, *made), *off_chip(*later_weights))


def rest_kernel(
    x_ref, pair_ref, side_ref, rel_ref, prev_ref, next_ref, far_ref, near_ref, name_ref, asked_ref, tail_ref,
    stat_ref, acc_ref, split_ref, out_ref, keys, values, kwin, vwin,
):
    place_ref = (x_ref[0], pair_ref[0], side_ref[0])
    turns = ((3, prev_ref), (1, next_ref), (2, far_ref))
    for i, (_, ref) in enumerate(turns):
        quarter_of(
            lambda s, at, ref=ref: ref[s * 4 * SHARE + at : s * 4 * SHARE + at + SHARE], keys.at[i], values.at[i]
        )
    for i, ref in enumerate((prev_ref, next_ref)):
        kwin[i] = ref[QUARTER : QUARTER + ROWS]
        vwin[i] = jnp.transpose(ref[QUARTER + ROWS :])
    is_last = [lax.rem(place_ref[0] + turn, 4) == 3 for turn, _ in turns]
    side = place_ref[2]
    full = far_bias(place_ref, rel_ref)

    def one(step, edge=None):
        split = split_ref[step]
        tail = tail_ref[step]
        scores = dot(keys[...].reshape(3 * PLEN // 4, PREF_GRP * LANES), split)
        parts = [
            scores[i * ROWS : (i + 1) * ROWS] + jnp.where(is_last[i], tail, full) for i in range(3)
        ]
        if edge is not None:
            bias = near_ref[edge * 2 * ROWS : (edge * 2 + 1) * ROWS]
            parts.append(
                masked(dot(kwin[edge], split[:LANES] + split[LANES:]), name_ref, edge * (PAIRS + 1), asked_ref, step, bias)
            )
        before = stat_ref[step, 0:1]
        top = jnp.max(functools.reduce(jnp.maximum, parts), axis=0, keepdims=True)
        top = jnp.maximum(top, before)
        shrink = jnp.exp(before - top)
        terms = [jnp.exp(part - top) for part in parts]
        row_sum = jnp.sum(functools.reduce(jnp.add, terms), axis=0, keepdims=True)
        row_sum = row_sum + stat_ref[step, 1:2] * shrink
        weights = [t.astype(jnp.bfloat16) for t in terms]
        far_values = jnp.concatenate([values[i] for i in range(3)], axis=1)
        far_out = dot(far_values, jnp.concatenate(weights[:3], axis=0))
        acc = acc_ref[step] * by_feature(shrink) + select(asked_ref, step, far_out)
        if edge is not None:
            acc = acc + own_head(dot(vwin[edge], weights[3]))
        done = jnp.transpose(acc * by_feature(1.0 / row_sum)).astype(jnp.bfloat16)
        out_ref[side * PAIRS + step] = done
        out_ref[(1 - side) * PAIRS + jnp.bitwise_xor(step, 1)] = done

    def middle(step, _):
        one(step)
        return 0

    one(jnp.int32(0), 0)
    lax.fori_loop(1, PAIRS - 1, middle, 0, unroll=3)
    one(jnp.int32(PAIRS - 1), 1)


def attend_rest(place, rel_bias, prev, after_it, far, made, part):
    return pl.pallas_call(
        rest_kernel,
        in_specs=[SMEM_SPEC] * 4 + [VMEM_SPEC] * 10,
        out_specs=VMEM_SPEC,
        out_shape=pltpu.VMEM((2 * PAIRS, ROWS, LANES), jnp.bfloat16),
        scratch_shapes=[
            pltpu.VMEM((3, PLEN // 4, PREF_GRP * LANES), jnp.bfloat16),
            pltpu.VMEM((3, PREF_GRP * LANES, PLEN // 4), jnp.bfloat16),
            pltpu.VMEM((2, ROWS, LANES), jnp.bfloat16),
            pltpu.VMEM((2, LANES, ROWS), jnp.bfloat16),
        ],
        compiler_params=pltpu.CompilerParams(vmem_limit_bytes=VMEM_LIMIT),
        cost_estimate=COST,
        name="attend_rest",
    )(*place, rel_bias.T, *on_chip(prev, after_it, far, *made[:-1], *part))


def finish_kernel(away, side_ref, att_ref, w_ref, tok_ref, gain_ref, in_one, in_two, out_one, out_two, *rest):
    at = (1 - side_ref[0] if away else side_ref[0]) * PAIRS
    attended = jnp.concatenate([att_ref[at + j] for j in range(PAIRS)], axis=1)
    hidden = (tok_ref[...].astype(jnp.float32) + dot(attended, w_ref[...])).astype(jnp.bfloat16)
    normed = norm_rows(hidden, gain_ref[...])
    got = None if away else hidden.astype(jnp.float32)
    for in_ref, out_w_ref in ((in_one, out_one), (in_two, out_two)):
        units = lax.dot_general(
            normed, in_ref[...], (((1,), (1,)), ((), ())), preferred_element_type=jnp.float32
        )
        part = dot(jnp.maximum(units, 0.0).astype(jnp.bfloat16), out_w_ref[...])
        got = part if got is None else got + part
    rest[-1][...] = got.astype(rest[-1].dtype)


def finish(away, side, att, w_attn_out, tokens, gain, weights, *ready):
    return pl.pallas_call(
        functools.partial(finish_kernel, away),
        in_specs=[SMEM_SPEC] + [VMEM_SPEC] * (8 + len(ready)),
        out_specs=VMEM_SPEC,
        out_shape=pltpu.VMEM((ROWS, D), jnp.bfloat16 if away else jnp.float32),
        compiler_params=pltpu.CompilerParams(vmem_limit_bytes=VMEM_LIMIT),
        cost_estimate=COST,
        name="finish",
    )(side, *on_chip(att, w_attn_out, tokens, gain.reshape(1, D), *weights, *ready))


def total_kernel(*refs):
    out_ref = refs[-1]
    total = functools.reduce(jnp.add, [ref[...].astype(jnp.float32) for ref in refs[:-1]])
    out_ref[...] = total.astype(out_ref.dtype)


def total(dtype, *arrays, last=False):
    return pl.pallas_call(
        total_kernel,
        in_specs=[VMEM_SPEC] * len(arrays),
        out_specs=VMEM_SPEC,
        out_shape=(jax.ShapeDtypeStruct if last else pltpu.VMEM)(arrays[0].shape, dtype),
        compiler_params=pltpu.CompilerParams(vmem_limit_bytes=VMEM_LIMIT),
        cost_estimate=COST,
        name="total",
    )(*on_chip(*arrays))


def body(
    tokens,
    attn_gain,
    w_query,
    w_key,
    w_value,
    w_attn_out,
    rel_bias,
    prefix_cache,
    lengths,
    prefix_map,
    mlp_gain,
    w_in,
    w_out,
):
    count_x = lax.axis_size("x")
    plane = lax.axis_index("z") * 2 + lax.axis_index("ylo")
    place = tuple(
        at.astype(jnp.int32).reshape(1) for at in (lax.axis_index("x"), plane, lax.axis_index("yhi"))
    )
    mirrored = ("yhi", "ylo")
    far_tokens = lax.ppermute(tokens, mirrored, MIRROR)
    other_in = lax.ppermute(w_in, "core", SWAP)
    other_out = lax.ppermute(w_out, "core", SWAP)
    blocks, made = project(
        place, tokens, attn_gain, prefix_cache, rel_bias, lengths, prefix_map, w_query, w_key, w_value
    )
    blocks = hold(blocks, far_tokens)
    got = lax.all_to_all(blocks, PLANE, 0, 0, tiled=True)
    up, down, far = spread(got, other_in, other_out)
    by = lambda d: [(i, (i + d) % count_x) for i in range(count_x)]
    opposite = lax.ppermute(far, "x", by(2))
    prev = lax.ppermute(up, "x", by(1))
    later = lax.ppermute(down, "x", by(-1))
    *part, other_out = attend_own(place, rel_bias, got, made, (other_out,))
    mixed = attend_rest(place, rel_bias, prev, later, opposite, made, part)
    weights = (w_in, other_in, w_out, other_out)
    att = lax.all_to_all(mixed, ("yhi",) + PLANE, 0, 0, tiled=True)

    far_sum = finish(True, place[2], att, w_attn_out, far_tokens, mlp_gain, weights)
    back = lax.ppermute(far_sum, mirrored, MIRROR)
    local = finish(False, place[2], att, w_attn_out, tokens, mlp_gain, weights, far_sum)
    return total(jnp.bfloat16, local, back, last=True)


def solution(mesh):
    split = Mesh(mesh.devices.reshape(2, 2, 4, 4, 2), AXES)
    grp, req = ("yhi", "core"), REQ
    return jax.shard_map(
        body,
        mesh=split,
        in_specs=(
            P(grp + req, None),
            P(),
            P(),
            P(),
            P(),
            P(),
            P(),
            P(grp, req, None),
            P(grp, None),
            P(grp, None),
            P(),
            P(grp, None),
            P(grp, None),
        ),
        out_specs=P(grp + req, None),
        check_vma=False,
    )
```

```python
import functools

import jax
import jax.numpy as jnp
from jax import lax
from jax.experimental import pallas as pl
from jax.experimental.pallas import tpu as pltpu
from jax.sharding import Mesh, PartitionSpec as P

D = 1024
H = 16
DK = 64
PLEN = 512
PREF_GRP = 2
ROWS = 128
PAIRS = 8
LANES = 128
SHARE = 16
SENT = 3 * ROWS + 2 * PREF_GRP * SHARE
QUARTER = PAIRS * 2 * PREF_GRP * SHARE

epsilon = 1e-06
far_marks = (12, 16, 23, 32, 46, 64, 91)
masked_score = -1e30
VMEM_LIMIT = 16 * 1024 * 1024
COST = pl.CostEstimate(flops=1000, transcendentals=0, bytes_accessed=1000)

AXES = ("yhi", "core", "x", "z", "ylo")
REQ = ("x", "z", "ylo")
PLANE = ("z", "ylo")
MIRROR = [(0, 3), (3, 0), (1, 2), (2, 1)]
SWAP = [(0, 1), (1, 0)]


def norm_rows(values_in, gain):
    widened = values_in.astype(jnp.float32)
    scale = lax.rsqrt(jnp.mean(widened * widened, axis=-1, keepdims=True) + epsilon)
    return (widened * scale * gain).astype(jnp.bfloat16)


def dot(a, b):
    return jnp.dot(a, b, preferred_element_type=jnp.float32)


def on_chip(*arrays):
    return tuple(pltpu.with_memory_space_constraint(a, pltpu.VMEM) for a in arrays)


def off_chip(*arrays):
    return tuple(pltpu.with_memory_space_constraint(a, pltpu.HBM) for a in arrays)


VMEM_SPEC = pl.BlockSpec(memory_space=pltpu.VMEM)
HBM_SPEC = pl.BlockSpec(memory_space=pltpu.HBM)
SMEM_SPEC = pl.BlockSpec(memory_space=pltpu.SMEM)


def bias_line(rel_ref, head, first_bucket):
    lane = lax.broadcasted_iota(jnp.int32, (8, LANES), 1)

    def of(bucket):
        return rel_ref[pl.ds(head, 1), first_bucket + bucket : first_bucket + bucket + 1]

    line = jnp.broadcast_to(of(0), (8, LANES))
    for bucket in range(1, 16):
        mark = bucket if bucket <= 8 else far_marks[bucket - 9]
        line = jnp.where(lane >= mark, of(bucket), line)
    return jnp.broadcast_to(line[0:1], (ROWS, LANES))


def write_tables(
    place_ref, rel_ref, len_ref, map_ref, near_ref, name_ref, asked_ref, line_ref, chosen_ref
):
    row = lax.broadcasted_iota(jnp.int32, (ROWS, LANES), 0)
    lane = lax.broadcasted_iota(jnp.int32, (ROWS, LANES), 1)
    for h in range(2):
        head = place_ref[1] * 2 + h
        before = bias_line(rel_ref, head, 0)
        after_it = bias_line(rel_ref, head, 16)

        def pick(line, distance):
            return jnp.take_along_axis(line, jnp.clip(distance, 0, LANES - 1), axis=1)

        cut = slice(h * ROWS, (h + 1) * ROWS)
        near_ref[0:ROWS, cut] = pick(before, lane + ROWS - row)
        near_ref[ROWS : 2 * ROWS, cut] = jnp.where(
            row > lane, pick(after_it, row - lane), pick(before, lane - row)
        )
        near_ref[2 * ROWS : 3 * ROWS, cut] = pick(after_it, row + ROWS - lane)
        line_ref[h] = before[:8]

    requests = len_ref.shape[1]
    down_it = lax.broadcasted_iota(jnp.int32, (requests, requests), 0)
    along = lax.broadcasted_iota(jnp.int32, (requests, requests), 1)
    length = jnp.broadcast_to(len_ref[...], (requests, requests)).astype(jnp.float32)
    prefix = jnp.broadcast_to(map_ref[...], (requests, requests)).astype(jnp.float32)

    def column(keep, values):
        return jnp.sum(jnp.where(keep, values, 0.0), axis=1, keepdims=True)

    starts = column(along < down_it, length)
    ends = column(along <= down_it, length)
    prefixes = column(along == down_it, prefix)
    number = lax.broadcasted_iota(jnp.int32, (requests, LANES), 0).astype(jnp.float32) + 1.0
    first = place_ref[0] * (PAIRS * ROWS) - ROWS
    for b in range(PAIRS + 2):
        ids = lax.broadcasted_iota(jnp.int32, (requests, LANES), 1) + (first + b * ROWS)
        ids = ids.astype(jnp.float32)
        member = (ids >= starts) & (ids < ends)
        request = jnp.sum(jnp.where(member, number, 0.0), axis=0, keepdims=True) - 1.0
        offset = ids[0:1] - jnp.sum(jnp.where(member, starts, 0.0), axis=0, keepdims=True)
        chosen = jnp.sum(jnp.where(member, prefixes, 0.0), axis=0, keepdims=True)
        facts = jnp.concatenate([request, offset, chosen] + [request] * 5, axis=0)
        name_ref[b] = jnp.broadcast_to(jnp.transpose(facts)[:, 0:1], (ROWS, LANES)).astype(jnp.bfloat16)
        if 0 < b < PAIRS + 1:
            step = b - 1
            asked_ref[step] = facts
            chosen_ref[step] = jnp.broadcast_to(chosen, (ROWS, LANES)).astype(jnp.bfloat16)


def project_kernel(
    x_ref, pair_ref, side_ref, tok_hbm, gain_hbm, cache_hbm, rel_hbm, len_hbm, map_hbm, wq_hbm, wk_hbm, wv_hbm,
    out_ref, near_ref, name_ref, asked_ref, line_ref, chosen_ref,
    tok, gain, cache, rel, lengths, prefix_map, held, arrived, landed,
):
    place_ref = (x_ref[0], pair_ref[0], side_ref[0])
    first = [
        pltpu.make_async_copy(source, target, landed.at[i])
        for i, (source, target) in enumerate(
            (
                (tok_hbm, tok), (gain_hbm, gain), (cache_hbm, cache),
                (rel_hbm, rel), (len_hbm, lengths), (map_hbm, prefix_map),
            )
        )
    ]
    copies = [
        pltpu.make_async_copy(w_hbm, held.at[kind], arrived.at[kind])
        for kind, w_hbm in enumerate((wq_hbm, wk_hbm, wv_hbm))
    ]
    for copy in first + copies:
        copy.start()
    for copy in first:
        copy.wait()
    normed = norm_rows(tok[...], gain[...])
    for part in range(PAIRS):
        for kind in range(2):
            for p in range(PREF_GRP):
                at = 3 * ROWS + (kind * PREF_GRP + p) * SHARE
                cut = slice(kind * D + part * LANES, kind * D + (part + 1) * LANES)
                out_ref[part, at : at + SHARE] = cache[p, :, cut]
    write_tables(
        place_ref, rel, lengths, prefix_map, near_ref, name_ref, asked_ref, line_ref, chosen_ref
    )
    for kind, copy in enumerate(copies):
        copy.wait()
        got = dot(normed, held[kind]).astype(jnp.bfloat16)
        for to in range(PAIRS):
            out_ref[to, kind * ROWS : (kind + 1) * ROWS] = got[:, to * LANES : (to + 1) * LANES]


def project(place, tokens, gain, prefix_cache, rel_bias, lengths, prefix_map, w_query, w_key, w_value):
    small = (tokens, gain.reshape(1, D), prefix_cache, rel_bias.T, lengths, prefix_map)
    out_shape = (
        pltpu.VMEM((PAIRS, SENT, LANES), jnp.bfloat16),
        pltpu.VMEM((3 * ROWS, 2 * ROWS), jnp.float32),
        pltpu.VMEM((PAIRS + 2, ROWS, LANES), jnp.bfloat16),
        pltpu.VMEM((PAIRS, 8, ROWS), jnp.float32),
        pltpu.VMEM((2, 8, LANES), jnp.float32),
        pltpu.VMEM((PAIRS, ROWS, ROWS), jnp.bfloat16),
    )
    blocks, *made = pl.pallas_call(
        project_kernel,
        in_specs=[SMEM_SPEC] * 3 + [HBM_SPEC] * 9,
        out_specs=(VMEM_SPEC,) * 6,
        out_shape=out_shape,
        scratch_shapes=[pltpu.VMEM(value.shape, value.dtype) for value in small]
        + [
            pltpu.VMEM((3, D, D), jnp.bfloat16),
            pltpu.SemaphoreType.DMA((3,)),
            pltpu.SemaphoreType.DMA((6,)),
        ],
        compiler_params=pltpu.CompilerParams(vmem_limit_bytes=VMEM_LIMIT),
        cost_estimate=COST,
        name="project",
    )(*place, *off_chip(*small, w_query, w_key, w_value))
    return blocks, made


def spread_kernel(got_ref, tok_ref, *rest):
    up_ref, down_ref, far_ref, same_ref = rest[-4:]
    for source in range(PAIRS):
        rows = slice(source * 4 * SHARE, (source + 1) * 4 * SHARE)
        held = got_ref[source, 3 * ROWS :]
        up_ref[rows] = held
        down_ref[rows] = held
        far_ref[rows] = held
    up_ref[QUARTER:] = got_ref[PAIRS - 1, ROWS : 3 * ROWS]
    down_ref[QUARTER:] = got_ref[0, ROWS : 3 * ROWS]
    same_ref[...] = tok_ref[...]


def spread(got, tokens, on, off):
    shape = pltpu.VMEM((QUARTER + 2 * ROWS, LANES), jnp.bfloat16)
    return pl.pallas_call(
        spread_kernel,
        in_specs=[VMEM_SPEC] * 3 + [HBM_SPEC],
        out_specs=(VMEM_SPEC,) * 4,
        out_shape=(
            shape,
            shape,
            pltpu.VMEM((QUARTER, LANES), jnp.bfloat16),
            pltpu.VMEM((ROWS, D), jnp.bfloat16),
        ),
        compiler_params=pltpu.CompilerParams(vmem_limit_bytes=VMEM_LIMIT),
        cost_estimate=COST,
        name="spread",
    )(*on_chip(got, tokens, on), *off_chip(off))


def queries(got_ref, chosen_ref, step):
    query = jnp.transpose(got_ref[step, 0:ROWS])
    zero = jnp.zeros((DK, ROWS), jnp.bfloat16)
    stacked = jnp.concatenate(
        [jnp.concatenate([query[:DK], zero], axis=0), jnp.concatenate([zero, query[DK:]], axis=0)], axis=1
    )
    chosen = jnp.concatenate([chosen_ref[step], chosen_ref[step]], axis=1)
    return stacked, jnp.concatenate([stacked * (1 - chosen), stacked * chosen], axis=0)


def masked(scores, name_ref, block, asked_ref, step, bias):
    mine = name_ref[block].astype(jnp.float32) == asked_ref[step, 0:1]
    mine = jnp.concatenate([mine, mine], axis=1)
    return jnp.where(mine, scores + bias, masked_score)


def far_bias(place_ref, rel_ref):
    lane = lax.broadcasted_iota(jnp.int32, (1, 2 * ROWS), 1)
    head = place_ref[1] * 2
    return jnp.where(lane < ROWS, rel_ref[head, 15], rel_ref[head + 1, 15])


def own_head(values):
    return jnp.concatenate([values[:DK, :ROWS], values[DK:, ROWS:]], axis=0)


def by_feature(line):
    return jnp.concatenate(
        [jnp.broadcast_to(line[:, :ROWS], (DK, ROWS)), jnp.broadcast_to(line[:, ROWS:], (DK, ROWS))], axis=0
    )


def select(asked_ref, step, far_out):
    second = jnp.broadcast_to(asked_ref[step, 2:3], (LANES, ROWS)) > 0.5
    return jnp.where(second, own_head(far_out[LANES:]), own_head(far_out[:LANES]))


def quarter_of(rows_at, keys_ref, values_ref):
    for p in range(PREF_GRP):
        pieces = [
            jnp.concatenate(
                [rows_at(source, (kind * PREF_GRP + p) * SHARE) for source in range(PAIRS)], axis=0
            )
            for kind in range(2)
        ]
        keys_ref[:, p * LANES : (p + 1) * LANES] = pieces[0]
        values_ref[p * LANES : (p + 1) * LANES, :] = jnp.transpose(pieces[1])


def start_copies(pairs, landed):
    copies = [pltpu.make_async_copy(a, b, landed.at[i]) for i, (a, b) in enumerate(pairs)]
    for copy in copies:
        copy.start()
    return copies


def own_kernel(
    x_ref, pair_ref, side_ref, rel_ref, got_ref, near_ref, name_ref, asked_ref, line_ref, chosen_ref, w1_hbm,
    stat_ref, acc_ref, tail_ref, w1_ref, keys, values, kwin, vwin, landed,
):
    place_ref = (x_ref[0], pair_ref[0], side_ref[0])
    copies = start_copies(((w1_hbm, w1_ref),), landed)
    for b in (0, PAIRS + 1):
        kwin[b] = jnp.zeros((ROWS, LANES), jnp.bfloat16)
        vwin[b] = jnp.zeros((LANES, ROWS), jnp.bfloat16)
    for b in range(PAIRS):
        kwin[b + 1] = got_ref[b, ROWS : 2 * ROWS]
        vwin[b + 1] = jnp.transpose(got_ref[b, 2 * ROWS : 3 * ROWS])
    quarter_of(lambda s, at: got_ref[s, 3 * ROWS + at : 3 * ROWS + at + SHARE], keys, values)
    is_last = place_ref[0] == 3
    full = far_bias(place_ref, rel_ref)

    row = lax.broadcasted_iota(jnp.int32, (ROWS, LANES), 0)
    lines = [jnp.broadcast_to(line_ref[h, 0:1], (ROWS, LANES)) for h in range(2)]

    def one(step, _):
        offset = jnp.broadcast_to(asked_ref[step, 1:2], (ROWS, LANES)).astype(jnp.int32)
        at = jnp.minimum(ROWS - row + offset, LANES - 1)
        tail = jnp.concatenate([jnp.take_along_axis(line, at, axis=1) for line in lines], axis=1)
        tail_ref[step] = tail
        stacked, split = queries(got_ref, chosen_ref, step)
        parts = [dot(keys[...], split) + jnp.where(is_last, tail, full)]
        near_scores = dot(kwin[pl.ds(step, 3)].reshape(3 * ROWS, LANES), stacked)
        for b in range(3):
            at_edge = (step + b == 0) | (step + b == PAIRS + 1)
            cut = slice(b * ROWS, (b + 1) * ROWS)
            bias = near_ref[cut] + jnp.where(at_edge, masked_score, 0.0)
            parts.append(masked(near_scores[cut], name_ref, step + b, asked_ref, step, bias))
        top = jnp.max(functools.reduce(jnp.maximum, parts), axis=0, keepdims=True)
        terms = [jnp.exp(part - top) for part in parts]
        row_sum = jnp.sum(functools.reduce(jnp.add, terms), axis=0, keepdims=True)
        weights = [t.astype(jnp.bfloat16) for t in terms]
        near_values = jnp.concatenate([vwin[step + b] for b in range(3)], axis=1)
        near_out = dot(near_values, jnp.concatenate(weights[1:], axis=0))
        acc_ref[step] = select(asked_ref, step, dot(values[...], weights[0])) + own_head(near_out)
        stat_ref[step, 0:1] = top
        stat_ref[step, 1:2] = row_sum
        return 0

    lax.fori_loop(0, PAIRS, one, 0, unroll=4)
    for copy in copies:
        copy.wait()


def attend_own(place, rel_bias, got, made, later_weights):
    return pl.pallas_call(
        own_kernel,
        in_specs=[SMEM_SPEC] * 4 + [VMEM_SPEC] * 6 + [HBM_SPEC],
        out_specs=(VMEM_SPEC,) * 4,
        out_shape=(
            pltpu.VMEM((PAIRS, 8, 2 * ROWS), jnp.float32),
            pltpu.VMEM((PAIRS, LANES, ROWS), jnp.float32),
            pltpu.VMEM((PAIRS, ROWS, 2 * ROWS), jnp.float32),
        )
        + tuple(pltpu.VMEM(w.shape, w.dtype) for w in later_weights),
        scratch_shapes=[
            pltpu.VMEM((PLEN // 4, PREF_GRP * LANES), jnp.bfloat16),
            pltpu.VMEM((PREF_GRP * LANES, PLEN // 4), jnp.bfloat16),
            pltpu.VMEM((PAIRS + 2, ROWS, LANES), jnp.bfloat16),
            pltpu.VMEM((PAIRS + 2, LANES, ROWS), jnp.bfloat16),
            pltpu.SemaphoreType.DMA((1,)),
        ],
        compiler_params=pltpu.CompilerParams(vmem_limit_bytes=VMEM_LIMIT),
        cost_estimate=COST,
        name="attend_own",
    )(*place, rel_bias.T, *on_chip(got, *made), *off_chip(*later_weights))


def rest_kernel(
    x_ref, pair_ref, side_ref, rel_ref, got_ref, prev_ref, next_ref, far_ref, near_ref, name_ref, asked_ref, chosen_ref,
    stat_ref, acc_ref, tail_ref, _, out_ref, keys, values, kwin, vwin,
):
    place_ref = (x_ref[0], pair_ref[0], side_ref[0])
    turns = ((3, prev_ref), (1, next_ref), (2, far_ref))
    for i, (_, ref) in enumerate(turns):
        quarter_of(
            lambda s, at, ref=ref: ref[s * 4 * SHARE + at : s * 4 * SHARE + at + SHARE], keys.at[i], values.at[i]
        )
    for i, ref in enumerate((prev_ref, next_ref)):
        kwin[i] = ref[QUARTER : QUARTER + ROWS]
        vwin[i] = jnp.transpose(ref[QUARTER + ROWS :])
    is_last = [lax.rem(place_ref[0] + turn, 4) == 3 for turn, _ in turns]
    side = place_ref[2]
    full = far_bias(place_ref, rel_ref)

    def one(step, edge=None):
        stacked, split = queries(got_ref, chosen_ref, step)
        tail = tail_ref[step]
        scores = dot(keys[...].reshape(3 * PLEN // 4, PREF_GRP * LANES), split)
        parts = [
            scores[i * ROWS : (i + 1) * ROWS] + jnp.where(is_last[i], tail, full) for i in range(3)
        ]
        if edge is not None:
            bias = near_ref[edge * 2 * ROWS : (edge * 2 + 1) * ROWS]
            parts.append(
                masked(dot(kwin[edge], stacked), name_ref, edge * (PAIRS + 1), asked_ref, step, bias)
            )
        before = stat_ref[step, 0:1]
        top = jnp.max(functools.reduce(jnp.maximum, parts), axis=0, keepdims=True)
        top = jnp.maximum(top, before)
        shrink = jnp.exp(before - top)
        terms = [jnp.exp(part - top) for part in parts]
        row_sum = jnp.sum(functools.reduce(jnp.add, terms), axis=0, keepdims=True)
        row_sum = row_sum + stat_ref[step, 1:2] * shrink
        weights = [t.astype(jnp.bfloat16) for t in terms]
        far_values = jnp.concatenate([values[i] for i in range(3)], axis=1)
        far_out = dot(far_values, jnp.concatenate(weights[:3], axis=0))
        acc = acc_ref[step] * by_feature(shrink) + select(asked_ref, step, far_out)
        if edge is not None:
            acc = acc + own_head(dot(vwin[edge], weights[3]))
        done = jnp.transpose(acc * by_feature(1.0 / row_sum)).astype(jnp.bfloat16)
        out_ref[side * PAIRS + step] = done
        out_ref[(1 - side) * PAIRS + jnp.bitwise_xor(step, 1)] = done

    def middle(step, _):
        one(step)
        return 0

    one(jnp.int32(0), 0)
    lax.fori_loop(1, PAIRS - 1, middle, 0, unroll=3)
    one(jnp.int32(PAIRS - 1), 1)


def attend_rest(place, rel_bias, got, prev, after_it, far, made, part, ready):
    return pl.pallas_call(
        rest_kernel,
        in_specs=[SMEM_SPEC] * 4 + [VMEM_SPEC] * 12,
        out_specs=VMEM_SPEC,
        out_shape=pltpu.VMEM((2 * PAIRS, ROWS, LANES), jnp.bfloat16),
        scratch_shapes=[
            pltpu.VMEM((3, PLEN // 4, PREF_GRP * LANES), jnp.bfloat16),
            pltpu.VMEM((3, PREF_GRP * LANES, PLEN // 4), jnp.bfloat16),
            pltpu.VMEM((2, ROWS, LANES), jnp.bfloat16),
            pltpu.VMEM((2, LANES, ROWS), jnp.bfloat16),
        ],
        compiler_params=pltpu.CompilerParams(vmem_limit_bytes=VMEM_LIMIT),
        cost_estimate=COST,
        name="attend_rest",
    )(*place, rel_bias.T, *on_chip(got, prev, after_it, far, *made[:3], made[4], *part, ready))


def finish_kernel(away, side_ref, att_ref, w_ref, tok_ref, gain_ref, in_one, in_two, out_one, out_two, *rest):
    at = (1 - side_ref[0] if away else side_ref[0]) * PAIRS
    attended = jnp.concatenate([att_ref[at + j] for j in range(PAIRS)], axis=1)
    hidden = (tok_ref[...].astype(jnp.float32) + dot(attended, w_ref[...])).astype(jnp.bfloat16)
    normed = norm_rows(hidden, gain_ref[...])
    got = None if away else hidden.astype(jnp.float32)
    for in_ref, out_w_ref in ((in_one, out_one), (in_two, out_two)):
        units = lax.dot_general(
            normed, in_ref[...], (((1,), (1,)), ((), ())), preferred_element_type=jnp.float32
        )
        part = dot(jnp.maximum(units, 0.0).astype(jnp.bfloat16), out_w_ref[...])
        got = part if got is None else got + part
    rest[-1][...] = got.astype(rest[-1].dtype)


def finish(away, side, att, w_attn_out, tokens, gain, weights, *ready):
    return pl.pallas_call(
        functools.partial(finish_kernel, away),
        in_specs=[SMEM_SPEC] + [VMEM_SPEC] * (8 + len(ready)),
        out_specs=VMEM_SPEC,
        out_shape=pltpu.VMEM((ROWS, D), jnp.bfloat16 if away else jnp.float32),
        compiler_params=pltpu.CompilerParams(vmem_limit_bytes=VMEM_LIMIT),
        cost_estimate=COST,
        name="finish",
    )(side, *on_chip(att, w_attn_out, tokens, gain.reshape(1, D), *weights, *ready))


def total_kernel(*refs):
    out_ref = refs[-1]
    total = functools.reduce(jnp.add, [ref[...].astype(jnp.float32) for ref in refs[:-1]])
    out_ref[...] = total.astype(out_ref.dtype)


def total(dtype, *arrays, last=False):
    return pl.pallas_call(
        total_kernel,
        in_specs=[VMEM_SPEC] * len(arrays),
        out_specs=VMEM_SPEC,
        out_shape=(jax.ShapeDtypeStruct if last else pltpu.VMEM)(arrays[0].shape, dtype),
        compiler_params=pltpu.CompilerParams(vmem_limit_bytes=VMEM_LIMIT),
        cost_estimate=COST,
        name="total",
    )(*on_chip(*arrays))


def body(
    tokens,
    attn_gain,
    w_query,
    w_key,
    w_value,
    w_attn_out,
    rel_bias,
    prefix_cache,
    lengths,
    prefix_map,
    mlp_gain,
    w_in,
    w_out,
):
    count_x = lax.axis_size("x")
    plane = lax.axis_index("z") * 2 + lax.axis_index("ylo")
    place = tuple(
        at.astype(jnp.int32).reshape(1) for at in (lax.axis_index("x"), plane, lax.axis_index("yhi"))
    )
    other_in = lax.ppermute(w_in, "core", SWAP)
    other_out = lax.ppermute(w_out, "core", SWAP)
    blocks, made = project(
        place, tokens, attn_gain, prefix_cache, rel_bias, lengths, prefix_map, w_query, w_key, w_value
    )
    got = lax.all_to_all(blocks, PLANE, 0, 0, tiled=True)
    mirrored = ("yhi", "ylo")
    up, down, far, same = spread(got, tokens, other_in, other_out)
    by = lambda d: [(i, (i + d) % count_x) for i in range(count_x)]
    opposite = lax.ppermute(far, "x", by(2))
    prev = lax.ppermute(up, "x", by(1))
    later = lax.ppermute(down, "x", by(-1))
    far_tokens = lax.ppermute(same, mirrored, MIRROR)
    *part, other_out = attend_own(place, rel_bias, got, made, (other_out,))
    mixed = attend_rest(place, rel_bias, got, prev, later, opposite, made, part, far_tokens)
    weights = (w_in, other_in, w_out, other_out)
    att = lax.all_to_all(mixed, ("yhi",) + PLANE, 0, 0, tiled=True)

    far_sum = finish(True, place[2], att, w_attn_out, far_tokens, mlp_gain, weights)
    back = lax.ppermute(far_sum, mirrored, MIRROR)
    local = finish(False, place[2], att, w_attn_out, tokens, mlp_gain, weights, far_sum)
    return total(jnp.bfloat16, local, back, last=True)


def solution(mesh):
    split = Mesh(mesh.devices.reshape(2, 2, 4, 4, 2), AXES)
    grp, req = ("yhi", "core"), REQ
    return jax.shard_map(
        body,
        mesh=split,
        in_specs=(
            P(grp + req, None),
            P(),
            P(),
            P(),
            P(),
            P(),
            P(),
            P(grp, req, None),
            P(grp, None),
            P(grp, None),
            P(),
            P(grp, None),
            P(grp, None),
        ),
        out_specs=P(grp + req, None),
        check_vma=False,
    )
```

```python
import functools

import jax
import jax.numpy as jnp
from jax import lax
from jax.experimental import pallas as pl
from jax.experimental.pallas import tpu as pltpu
from jax.sharding import Mesh, PartitionSpec as P

D = 1024
H = 16
DK = 64
PLEN = 512
PREF_GRP = 2
ROWS = 128
PAIRS = 8
LANES = 128
FIRST = 640
SHARE = 16
SENT = 3 * ROWS + 2 * PREF_GRP * SHARE
QUARTER = PAIRS * 2 * PREF_GRP * SHARE

epsilon = 1e-06
far_marks = (12, 16, 23, 32, 46, 64, 91)
masked_score = -1e30
VMEM_LIMIT = 16 * 1024 * 1024
COST = pl.CostEstimate(flops=1000, transcendentals=0, bytes_accessed=1000)

AXES = ("yhi", "core", "x", "z", "ylo")
REQ = ("x", "z", "ylo")
PLANE = ("z", "ylo")
MIRROR = [(0, 3), (3, 0), (1, 2), (2, 1)]
SWAP = [(0, 1), (1, 0)]


def norm_rows(values_in, gain):
    widened = values_in.astype(jnp.float32)
    scale = lax.rsqrt(jnp.mean(widened * widened, axis=-1, keepdims=True) + epsilon)
    return (widened * scale * gain).astype(jnp.bfloat16)


def dot(a, b):
    return jnp.dot(a, b, preferred_element_type=jnp.float32)


def on_chip(*arrays):
    return tuple(pltpu.with_memory_space_constraint(a, pltpu.VMEM) for a in arrays)


def off_chip(*arrays):
    return tuple(pltpu.with_memory_space_constraint(a, pltpu.HBM) for a in arrays)


VMEM_SPEC = pl.BlockSpec(memory_space=pltpu.VMEM)
HBM_SPEC = pl.BlockSpec(memory_space=pltpu.HBM)
SMEM_SPEC = pl.BlockSpec(memory_space=pltpu.SMEM)


def bias_line(rel_ref, head, first_bucket):
    lane = lax.broadcasted_iota(jnp.int32, (8, LANES), 1)

    def of(bucket):
        return rel_ref[pl.ds(head, 1), first_bucket + bucket : first_bucket + bucket + 1]

    line = jnp.broadcast_to(of(0), (8, LANES))
    for bucket in range(1, 16):
        mark = bucket if bucket <= 8 else far_marks[bucket - 9]
        line = jnp.where(lane >= mark, of(bucket), line)
    return jnp.broadcast_to(line[0:1], (ROWS, LANES))


def write_tables(
    place_ref, rel_ref, len_ref, map_ref, near_ref, name_ref, asked_ref, line_ref, chosen_ref
):
    row = lax.broadcasted_iota(jnp.int32, (ROWS, LANES), 0)
    lane = lax.broadcasted_iota(jnp.int32, (ROWS, LANES), 1)
    for h in range(2):
        head = place_ref[1] * 2 + h
        before = bias_line(rel_ref, head, 0)
        after_it = bias_line(rel_ref, head, 16)

        def pick(line, distance):
            return jnp.take_along_axis(line, jnp.clip(distance, 0, LANES - 1), axis=1)

        cut = slice(h * ROWS, (h + 1) * ROWS)
        near_ref[0:ROWS, cut] = pick(before, lane + ROWS - row)
        near_ref[ROWS : 2 * ROWS, cut] = jnp.where(
            row > lane, pick(after_it, row - lane), pick(before, lane - row)
        )
        near_ref[2 * ROWS : 3 * ROWS, cut] = pick(after_it, row + ROWS - lane)
        line_ref[h] = before[:8]

    requests = len_ref.shape[1]
    down_it = lax.broadcasted_iota(jnp.int32, (requests, requests), 0)
    along = lax.broadcasted_iota(jnp.int32, (requests, requests), 1)
    length = jnp.broadcast_to(len_ref[...], (requests, requests)).astype(jnp.float32)
    prefix = jnp.broadcast_to(map_ref[...], (requests, requests)).astype(jnp.float32)

    def column(keep, values):
        return jnp.sum(jnp.where(keep, values, 0.0), axis=1, keepdims=True)

    starts = column(along < down_it, length)
    ends = column(along <= down_it, length)
    prefixes = column(along == down_it, prefix)
    number = lax.broadcasted_iota(jnp.int32, (requests, LANES), 0).astype(jnp.float32) + 1.0
    first = place_ref[0] * (PAIRS * ROWS) - ROWS
    for b in range(PAIRS + 2):
        ids = lax.broadcasted_iota(jnp.int32, (requests, LANES), 1) + (first + b * ROWS)
        ids = ids.astype(jnp.float32)
        member = (ids >= starts) & (ids < ends)
        request = jnp.sum(jnp.where(member, number, 0.0), axis=0, keepdims=True) - 1.0
        offset = ids[0:1] - jnp.sum(jnp.where(member, starts, 0.0), axis=0, keepdims=True)
        chosen = jnp.sum(jnp.where(member, prefixes, 0.0), axis=0, keepdims=True)
        facts = jnp.concatenate([request, offset, chosen] + [request] * 5, axis=0)
        name_ref[b] = jnp.broadcast_to(jnp.transpose(facts)[:, 0:1], (ROWS, LANES)).astype(jnp.bfloat16)
        if 0 < b < PAIRS + 1:
            step = b - 1
            asked_ref[step] = facts
            chosen_ref[step] = jnp.broadcast_to(chosen, (ROWS, LANES)).astype(jnp.bfloat16)


def project_kernel(
    x_ref, pair_ref, side_ref, tok_hbm, gain_hbm, cache_hbm, rel_hbm, len_hbm, map_hbm, wq_hbm, wk_hbm, wv_hbm,
    out_ref, near_ref, name_ref, asked_ref, line_ref, chosen_ref,
    tok, gain, cache, rel, lengths, prefix_map, held, arrived, landed,
):
    place_ref = (x_ref[0], pair_ref[0], side_ref[0])
    first = [
        pltpu.make_async_copy(source, target, landed.at[i])
        for i, (source, target) in enumerate(
            (
                (tok_hbm, tok), (gain_hbm, gain), (cache_hbm, cache),
                (rel_hbm, rel), (len_hbm, lengths), (map_hbm, prefix_map),
            )
        )
    ]
    copies = [
        pltpu.make_async_copy(w_hbm, held.at[kind], arrived.at[kind])
        for kind, w_hbm in enumerate((wq_hbm, wk_hbm, wv_hbm))
    ]
    for copy in first + copies:
        copy.start()
    for copy in first:
        copy.wait()
    normed = norm_rows(tok[...], gain[...])
    for part in range(PAIRS):
        for kind in range(2):
            for p in range(PREF_GRP):
                at = 3 * ROWS + (kind * PREF_GRP + p) * SHARE
                cut = slice(kind * D + part * LANES, kind * D + (part + 1) * LANES)
                out_ref[part, at : at + SHARE] = cache[p, :, cut]
    write_tables(
        place_ref, rel, lengths, prefix_map, near_ref, name_ref, asked_ref, line_ref, chosen_ref
    )
    for kind, copy in enumerate(copies):
        copy.wait()
        got = dot(normed, held[kind]).astype(jnp.bfloat16)
        for to in range(PAIRS):
            out_ref[to, kind * ROWS : (kind + 1) * ROWS] = got[:, to * LANES : (to + 1) * LANES]


def project(place, tokens, gain, prefix_cache, rel_bias, lengths, prefix_map, w_query, w_key, w_value):
    small = (tokens, gain.reshape(1, D), prefix_cache, rel_bias.T, lengths, prefix_map)
    out_shape = (
        pltpu.VMEM((PAIRS, SENT, LANES), jnp.bfloat16),
        pltpu.VMEM((3 * ROWS, 2 * ROWS), jnp.float32),
        pltpu.VMEM((PAIRS + 2, ROWS, LANES), jnp.bfloat16),
        pltpu.VMEM((PAIRS, 8, ROWS), jnp.float32),
        pltpu.VMEM((2, 8, LANES), jnp.float32),
        pltpu.VMEM((PAIRS, ROWS, ROWS), jnp.bfloat16),
    )
    blocks, *made = pl.pallas_call(
        project_kernel,
        in_specs=[SMEM_SPEC] * 3 + [HBM_SPEC] * 9,
        out_specs=(VMEM_SPEC,) * 6,
        out_shape=out_shape,
        scratch_shapes=[pltpu.VMEM(value.shape, value.dtype) for value in small]
        + [
            pltpu.VMEM((3, D, D), jnp.bfloat16),
            pltpu.SemaphoreType.DMA((3,)),
            pltpu.SemaphoreType.DMA((6,)),
        ],
        compiler_params=pltpu.CompilerParams(vmem_limit_bytes=VMEM_LIMIT),
        cost_estimate=COST,
        name="project",
    )(*place, *off_chip(*small, w_query, w_key, w_value))
    return blocks, made


def spread_kernel(got_ref, tok_ref, *rest):
    up_ref, down_ref, far_ref, same_ref = rest[-4:]
    for source in range(PAIRS):
        rows = slice(source * 4 * SHARE, (source + 1) * 4 * SHARE)
        held = got_ref[source, 3 * ROWS :]
        up_ref[rows] = held
        down_ref[rows] = held
        far_ref[rows] = held
    up_ref[QUARTER:] = got_ref[PAIRS - 1, ROWS : 3 * ROWS]
    down_ref[QUARTER:] = got_ref[0, ROWS : 3 * ROWS]
    same_ref[...] = tok_ref[...]


def spread(got, tokens, on, off):
    shape = pltpu.VMEM((QUARTER + 2 * ROWS, LANES), jnp.bfloat16)
    return pl.pallas_call(
        spread_kernel,
        in_specs=[VMEM_SPEC] * 3 + [HBM_SPEC],
        out_specs=(VMEM_SPEC,) * 4,
        out_shape=(
            shape,
            shape,
            pltpu.VMEM((QUARTER, LANES), jnp.bfloat16),
            pltpu.VMEM((ROWS, D), jnp.bfloat16),
        ),
        compiler_params=pltpu.CompilerParams(vmem_limit_bytes=VMEM_LIMIT),
        cost_estimate=COST,
        name="spread",
    )(*on_chip(got, tokens, on), *off_chip(off))


def queries(got_ref, chosen_ref, step):
    query = jnp.transpose(got_ref[step, 0:ROWS])
    zero = jnp.zeros((DK, ROWS), jnp.bfloat16)
    stacked = jnp.concatenate(
        [jnp.concatenate([query[:DK], zero], axis=0), jnp.concatenate([zero, query[DK:]], axis=0)], axis=1
    )
    chosen = jnp.concatenate([chosen_ref[step], chosen_ref[step]], axis=1)
    return stacked, jnp.concatenate([stacked * (1 - chosen), stacked * chosen], axis=0)


def masked(scores, name_ref, block, asked_ref, step, bias):
    mine = name_ref[block].astype(jnp.float32) == asked_ref[step, 0:1]
    mine = jnp.concatenate([mine, mine], axis=1)
    return jnp.where(mine, scores + bias, masked_score)


def far_bias(place_ref, rel_ref):
    lane = lax.broadcasted_iota(jnp.int32, (1, 2 * ROWS), 1)
    head = place_ref[1] * 2
    return jnp.where(lane < ROWS, rel_ref[head, 15], rel_ref[head + 1, 15])


def own_head(values):
    return jnp.concatenate([values[:DK, :ROWS], values[DK:, ROWS:]], axis=0)


def by_feature(line):
    return jnp.concatenate(
        [jnp.broadcast_to(line[:, :ROWS], (DK, ROWS)), jnp.broadcast_to(line[:, ROWS:], (DK, ROWS))], axis=0
    )


def select(asked_ref, step, far_out):
    second = jnp.broadcast_to(asked_ref[step, 2:3], (LANES, ROWS)) > 0.5
    return jnp.where(second, own_head(far_out[LANES:]), own_head(far_out[:LANES]))


def quarter_of(rows_at, keys_ref, values_ref):
    for p in range(PREF_GRP):
        pieces = [
            jnp.concatenate(
                [rows_at(source, (kind * PREF_GRP + p) * SHARE) for source in range(PAIRS)], axis=0
            )
            for kind in range(2)
        ]
        keys_ref[:, p * LANES : (p + 1) * LANES] = pieces[0]
        values_ref[p * LANES : (p + 1) * LANES, :] = jnp.transpose(pieces[1])


def start_copies(pairs, landed):
    copies = [pltpu.make_async_copy(a, b, landed.at[i]) for i, (a, b) in enumerate(pairs)]
    for copy in copies:
        copy.start()
    return copies


def own_kernel(
    x_ref, pair_ref, side_ref, rel_ref, got_ref, near_ref, name_ref, asked_ref, line_ref, chosen_ref, w1_hbm,
    stat_ref, acc_ref, tail_ref, split_ref, w1_ref, keys, values, kwin, vwin, landed,
):
    place_ref = (x_ref[0], pair_ref[0], side_ref[0])
    copies = start_copies(((w1_hbm, w1_ref),), landed)
    for b in (0, PAIRS + 1):
        kwin[b] = jnp.zeros((ROWS, LANES), jnp.bfloat16)
        vwin[b] = jnp.zeros((LANES, ROWS), jnp.bfloat16)
    for b in range(PAIRS):
        kwin[b + 1] = got_ref[b, ROWS : 2 * ROWS]
        vwin[b + 1] = jnp.transpose(got_ref[b, 2 * ROWS : 3 * ROWS])
    quarter_of(lambda s, at: got_ref[s, 3 * ROWS + at : 3 * ROWS + at + SHARE], keys, values)
    is_last = place_ref[0] == 3
    full = far_bias(place_ref, rel_ref)

    row = lax.broadcasted_iota(jnp.int32, (ROWS, LANES), 0)
    lines = [jnp.broadcast_to(line_ref[h, 0:1], (ROWS, LANES)) for h in range(2)]

    def one(step, _):
        offset = jnp.broadcast_to(asked_ref[step, 1:2], (ROWS, LANES)).astype(jnp.int32)
        at = jnp.minimum(ROWS - row + offset, LANES - 1)
        tail = jnp.concatenate([jnp.take_along_axis(line, at, axis=1) for line in lines], axis=1)
        tail_ref[step] = tail
        stacked, split = queries(got_ref, chosen_ref, step)
        split_ref[step] = split
        parts = [dot(keys[...], split) + jnp.where(is_last, tail, full)]
        near_scores = dot(kwin[pl.ds(step, 3)].reshape(3 * ROWS, LANES), stacked)
        for b in range(3):
            at_edge = (step + b == 0) | (step + b == PAIRS + 1)
            cut = slice(b * ROWS, (b + 1) * ROWS)
            bias = near_ref[cut] + jnp.where(at_edge, masked_score, 0.0)
            parts.append(masked(near_scores[cut], name_ref, step + b, asked_ref, step, bias))
        top = jnp.max(functools.reduce(jnp.maximum, parts), axis=0, keepdims=True)
        terms = [jnp.exp(part - top) for part in parts]
        row_sum = jnp.sum(functools.reduce(jnp.add, terms), axis=0, keepdims=True)
        weights = [t.astype(jnp.bfloat16) for t in terms]
        near_values = jnp.concatenate([vwin[step + b] for b in range(3)], axis=1)
        near_out = dot(near_values, jnp.concatenate(weights[1:], axis=0))
        acc_ref[step] = select(asked_ref, step, dot(values[...], weights[0])) + own_head(near_out)
        stat_ref[step, 0:1] = top
        stat_ref[step, 1:2] = row_sum
        return 0

    lax.fori_loop(0, PAIRS, one, 0, unroll=4)
    for copy in copies:
        copy.wait()


def attend_own(place, rel_bias, got, made, later_weights):
    return pl.pallas_call(
        own_kernel,
        in_specs=[SMEM_SPEC] * 4 + [VMEM_SPEC] * 6 + [HBM_SPEC],
        out_specs=(VMEM_SPEC,) * 5,
        out_shape=(
            pltpu.VMEM((PAIRS, 8, 2 * ROWS), jnp.float32),
            pltpu.VMEM((PAIRS, LANES, ROWS), jnp.float32),
            pltpu.VMEM((PAIRS, ROWS, 2 * ROWS), jnp.float32),
            pltpu.VMEM((PAIRS, PREF_GRP * LANES, 2 * ROWS), jnp.bfloat16),
        )
        + tuple(pltpu.VMEM(w.shape, w.dtype) for w in later_weights),
        scratch_shapes=[
            pltpu.VMEM((PLEN // 4, PREF_GRP * LANES), jnp.bfloat16),
            pltpu.VMEM((PREF_GRP * LANES, PLEN // 4), jnp.bfloat16),
            pltpu.VMEM((PAIRS + 2, ROWS, LANES), jnp.bfloat16),
            pltpu.VMEM((PAIRS + 2, LANES, ROWS), jnp.bfloat16),
            pltpu.SemaphoreType.DMA((1,)),
        ],
        compiler_params=pltpu.CompilerParams(vmem_limit_bytes=VMEM_LIMIT),
        cost_estimate=COST,
        name="attend_own",
    )(*place, rel_bias.T, *on_chip(got, *made), *off_chip(*later_weights))


def rest_kernel(
    x_ref, pair_ref, side_ref, rel_ref, prev_ref, next_ref, far_ref, near_ref, name_ref, asked_ref,
    stat_ref, acc_ref, tail_ref, split_ref, _, out_ref, keys, values, kwin, vwin,
):
    place_ref = (x_ref[0], pair_ref[0], side_ref[0])
    turns = ((3, prev_ref), (1, next_ref), (2, far_ref))
    for i, (_, ref) in enumerate(turns):
        quarter_of(
            lambda s, at, ref=ref: ref[s * 4 * SHARE + at : s * 4 * SHARE + at + SHARE], keys.at[i], values.at[i]
        )
    for i, ref in enumerate((prev_ref, next_ref)):
        kwin[i] = ref[QUARTER : QUARTER + ROWS]
        vwin[i] = jnp.transpose(ref[QUARTER + ROWS :])
    is_last = [lax.rem(place_ref[0] + turn, 4) == 3 for turn, _ in turns]
    side = place_ref[2]
    full = far_bias(place_ref, rel_ref)

    def one(step, edge=None):
        split = split_ref[step]
        tail = tail_ref[step]
        scores = dot(keys[...].reshape(3 * PLEN // 4, PREF_GRP * LANES), split)
        parts = [
            scores[i * ROWS : (i + 1) * ROWS] + jnp.where(is_last[i], tail, full) for i in range(3)
        ]
        if edge is not None:
            bias = near_ref[edge * 2 * ROWS : (edge * 2 + 1) * ROWS]
            parts.append(
                masked(dot(kwin[edge], split[:LANES] + split[LANES:]), name_ref, edge * (PAIRS + 1), asked_ref, step, bias)
            )
        before = stat_ref[step, 0:1]
        top = jnp.max(functools.reduce(jnp.maximum, parts), axis=0, keepdims=True)
        top = jnp.maximum(top, before)
        shrink = jnp.exp(before - top)
        terms = [jnp.exp(part - top) for part in parts]
        row_sum = jnp.sum(functools.reduce(jnp.add, terms), axis=0, keepdims=True)
        row_sum = row_sum + stat_ref[step, 1:2] * shrink
        weights = [t.astype(jnp.bfloat16) for t in terms]
        far_values = jnp.concatenate([values[i] for i in range(3)], axis=1)
        far_out = dot(far_values, jnp.concatenate(weights[:3], axis=0))
        acc = acc_ref[step] * by_feature(shrink) + select(asked_ref, step, far_out)
        if edge is not None:
            acc = acc + own_head(dot(vwin[edge], weights[3]))
        done = jnp.transpose(acc * by_feature(1.0 / row_sum)).astype(jnp.bfloat16)
        out_ref[side * PAIRS + step] = done
        out_ref[(1 - side) * PAIRS + jnp.bitwise_xor(step, 1)] = done

    def middle(step, _):
        one(step)
        return 0

    one(jnp.int32(0), 0)
    lax.fori_loop(1, PAIRS - 1, middle, 0, unroll=3)
    one(jnp.int32(PAIRS - 1), 1)


def attend_rest(place, rel_bias, prev, after_it, far, made, part, ready):
    return pl.pallas_call(
        rest_kernel,
        in_specs=[SMEM_SPEC] * 4 + [VMEM_SPEC] * 11,
        out_specs=VMEM_SPEC,
        out_shape=pltpu.VMEM((2 * PAIRS, ROWS, LANES), jnp.bfloat16),
        scratch_shapes=[
            pltpu.VMEM((3, PLEN // 4, PREF_GRP * LANES), jnp.bfloat16),
            pltpu.VMEM((3, PREF_GRP * LANES, PLEN // 4), jnp.bfloat16),
            pltpu.VMEM((2, ROWS, LANES), jnp.bfloat16),
            pltpu.VMEM((2, LANES, ROWS), jnp.bfloat16),
        ],
        compiler_params=pltpu.CompilerParams(vmem_limit_bytes=VMEM_LIMIT),
        cost_estimate=COST,
        name="attend_rest",
    )(*place, rel_bias.T, *on_chip(prev, after_it, far, *made[:3], *part, ready))


def join(side, att_ref, w_ref, tok_ref):
    attended = jnp.concatenate([att_ref[side * PAIRS + j] for j in range(PAIRS)], axis=1)
    return (tok_ref[...].astype(jnp.float32) + dot(attended, w_ref[...])).astype(jnp.bfloat16)


def units_of(normed, in_ref):
    units = lax.dot_general(
        normed, in_ref[...], (((1,), (1,)), ((), ())), preferred_element_type=jnp.float32
    )
    return jnp.maximum(units, 0.0).astype(jnp.bfloat16)


def finish_kernel(side_ref, att_ref, w_ref, tok_ref, gain_ref, in_one, in_two, out_one, out_two, *rest):
    hidden = join(side_ref[0], att_ref, w_ref, tok_ref)
    normed = norm_rows(hidden, gain_ref[...])
    got = hidden.astype(jnp.float32)
    for in_ref, out_w_ref in ((in_one, out_one), (in_two, out_two)):
        got = got + dot(units_of(normed, in_ref), out_w_ref[...])
    rest[-1][...] = got


def finish(side, att, w_attn_out, tokens, gain, weights, *ready):
    return pl.pallas_call(
        finish_kernel,
        in_specs=[SMEM_SPEC] + [VMEM_SPEC] * (8 + len(ready)),
        out_specs=VMEM_SPEC,
        out_shape=pltpu.VMEM((ROWS, D), jnp.float32),
        compiler_params=pltpu.CompilerParams(vmem_limit_bytes=VMEM_LIMIT),
        cost_estimate=COST,
        name="finish",
    )(side, *on_chip(att, w_attn_out, tokens, gain.reshape(1, D), *weights, *ready))


def away_kernel(
    side_ref, att_ref, w_ref, tok_ref, gain_ref, in_one, in_two, out_one, out_two, half_ref, units_ref
):
    hidden = join(1 - side_ref[0], att_ref, w_ref, tok_ref)
    normed = norm_rows(hidden, gain_ref[...])
    units_ref[0] = units_of(normed, in_one)
    units_ref[1] = units_of(normed, in_two)
    got = dot(units_ref[0], out_one[:, :FIRST]) + dot(units_ref[1], out_two[:, :FIRST])
    half_ref[...] = got.astype(half_ref.dtype)


def away(side, att, w_attn_out, tokens, gain, weights):
    return pl.pallas_call(
        away_kernel,
        in_specs=[SMEM_SPEC] + [VMEM_SPEC] * 8,
        out_specs=(VMEM_SPEC,) * 2,
        out_shape=(pltpu.VMEM((ROWS, FIRST), jnp.bfloat16), pltpu.VMEM((2, ROWS, D), jnp.bfloat16)),
        compiler_params=pltpu.CompilerParams(vmem_limit_bytes=VMEM_LIMIT),
        cost_estimate=COST,
        name="away",
    )(side, *on_chip(att, w_attn_out, tokens, gain.reshape(1, D), *weights))


def remainder_kernel(units_ref, out_one, out_two, half_ref):
    got = dot(units_ref[0], out_one[:, FIRST:]) + dot(units_ref[1], out_two[:, FIRST:])
    half_ref[...] = got.astype(half_ref.dtype)


def remainder(units, out_one, out_two):
    return pl.pallas_call(
        remainder_kernel,
        in_specs=[VMEM_SPEC] * 3,
        out_specs=VMEM_SPEC,
        out_shape=pltpu.VMEM((ROWS, D - FIRST), jnp.bfloat16),
        compiler_params=pltpu.CompilerParams(vmem_limit_bytes=VMEM_LIMIT),
        cost_estimate=COST,
        name="remainder",
    )(*on_chip(units, out_one, out_two))


def total_kernel(home_ref, first_ref, second_ref, out_ref):
    for cut, ref in ((slice(0, FIRST), first_ref), (slice(FIRST, D), second_ref)):
        out_ref[:, cut] = (home_ref[:, cut] + ref[...].astype(jnp.float32)).astype(jnp.bfloat16)


def total(home, first, second):
    return pl.pallas_call(
        total_kernel,
        in_specs=[VMEM_SPEC] * 3,
        out_specs=VMEM_SPEC,
        out_shape=jax.ShapeDtypeStruct((ROWS, D), jnp.bfloat16),
        compiler_params=pltpu.CompilerParams(vmem_limit_bytes=VMEM_LIMIT),
        cost_estimate=COST,
        name="total",
    )(*on_chip(home, first, second))


def body(
    tokens,
    attn_gain,
    w_query,
    w_key,
    w_value,
    w_attn_out,
    rel_bias,
    prefix_cache,
    lengths,
    prefix_map,
    mlp_gain,
    w_in,
    w_out,
):
    count_x = lax.axis_size("x")
    plane = lax.axis_index("z") * 2 + lax.axis_index("ylo")
    place = tuple(
        at.astype(jnp.int32).reshape(1) for at in (lax.axis_index("x"), plane, lax.axis_index("yhi"))
    )
    other_in = lax.ppermute(w_in, "core", SWAP)
    other_out = lax.ppermute(w_out, "core", SWAP)
    blocks, made = project(
        place, tokens, attn_gain, prefix_cache, rel_bias, lengths, prefix_map, w_query, w_key, w_value
    )
    got = lax.all_to_all(blocks, PLANE, 0, 0, tiled=True)
    mirrored = ("yhi", "ylo")
    up, down, far, same = spread(got, tokens, other_in, other_out)
    by = lambda d: [(i, (i + d) % count_x) for i in range(count_x)]
    opposite = lax.ppermute(far, "x", by(2))
    prev = lax.ppermute(up, "x", by(1))
    later = lax.ppermute(down, "x", by(-1))
    far_tokens = lax.ppermute(same, mirrored, MIRROR)
    *part, other_out = attend_own(place, rel_bias, got, made, (other_out,))
    mixed = attend_rest(place, rel_bias, prev, later, opposite, made, part, far_tokens)
    weights = (w_in, other_in, w_out, other_out)
    att = lax.all_to_all(mixed, ("yhi",) + PLANE, 0, 0, tiled=True)

    first, units = away(place[2], att, w_attn_out, far_tokens, mlp_gain, weights)
    first_back = lax.ppermute(first, mirrored, MIRROR)
    second = remainder(units, *weights[2:])
    second_back = lax.ppermute(second, mirrored, MIRROR)
    local = finish(place[2], att, w_attn_out, tokens, mlp_gain, weights, second)
    return total(local, first_back, second_back)


def solution(mesh):
    split = Mesh(mesh.devices.reshape(2, 2, 4, 4, 2), AXES)
    grp, req = ("yhi", "core"), REQ
    return jax.shard_map(
        body,
        mesh=split,
        in_specs=(
            P(grp + req, None),
            P(),
            P(),
            P(),
            P(),
            P(),
            P(),
            P(grp, req, None),
            P(grp, None),
            P(grp, None),
            P(),
            P(grp, None),
            P(grp, None),
        ),
        out_specs=P(grp + req, None),
        check_vma=False,
    )
```

```python
import functools

import jax
import jax.numpy as jnp
from jax import lax
from jax.experimental import pallas as pl
from jax.experimental.pallas import tpu as pltpu
from jax.sharding import Mesh, PartitionSpec as P

D = 1024
H = 16
DK = 64
PLEN = 512
PREF_GRP = 2
ROWS = 128
PAIRS = 8
LANES = 128
FIRST = 640
SHARE = 16
SENT = 3 * ROWS + 2 * PREF_GRP * SHARE
QUARTER = PAIRS * 2 * PREF_GRP * SHARE

epsilon = 1e-06
far_marks = (12, 16, 23, 32, 46, 64, 91)
masked_score = -1e30
VMEM_LIMIT = 16 * 1024 * 1024
COST = pl.CostEstimate(flops=1000, transcendentals=0, bytes_accessed=1000)

AXES = ("yhi", "core", "x", "z", "ylo")
REQ = ("x", "z", "ylo")
PLANE = ("z", "ylo")
MIRROR = [(0, 3), (3, 0), (1, 2), (2, 1)]
SWAP = [(0, 1), (1, 0)]


def norm_rows(values_in, gain):
    widened = values_in.astype(jnp.float32)
    scale = lax.rsqrt(jnp.mean(widened * widened, axis=-1, keepdims=True) + epsilon)
    return (widened * scale * gain).astype(jnp.bfloat16)


def dot(a, b):
    return jnp.dot(a, b, preferred_element_type=jnp.float32)


def on_chip(*arrays):
    return tuple(pltpu.with_memory_space_constraint(a, pltpu.VMEM) for a in arrays)


def off_chip(*arrays):
    return tuple(pltpu.with_memory_space_constraint(a, pltpu.HBM) for a in arrays)


VMEM_SPEC = pl.BlockSpec(memory_space=pltpu.VMEM)
HBM_SPEC = pl.BlockSpec(memory_space=pltpu.HBM)
SMEM_SPEC = pl.BlockSpec(memory_space=pltpu.SMEM)


def bias_line(rel_ref, head, first_bucket):
    lane = lax.broadcasted_iota(jnp.int32, (8, LANES), 1)

    def of(bucket):
        return rel_ref[pl.ds(head, 1), first_bucket + bucket : first_bucket + bucket + 1]

    line = jnp.broadcast_to(of(0), (8, LANES))
    for bucket in range(1, 16):
        mark = bucket if bucket <= 8 else far_marks[bucket - 9]
        line = jnp.where(lane >= mark, of(bucket), line)
    return jnp.broadcast_to(line[0:1], (ROWS, LANES))


def write_tables(
    place_ref, rel_ref, len_ref, map_ref, near_ref, name_ref, asked_ref, line_ref, chosen_ref
):
    row = lax.broadcasted_iota(jnp.int32, (ROWS, LANES), 0)
    lane = lax.broadcasted_iota(jnp.int32, (ROWS, LANES), 1)
    for h in range(2):
        head = place_ref[1] * 2 + h
        before = bias_line(rel_ref, head, 0)
        after_it = bias_line(rel_ref, head, 16)

        def pick(line, distance):
            return jnp.take_along_axis(line, jnp.clip(distance, 0, LANES - 1), axis=1)

        cut = slice(h * ROWS, (h + 1) * ROWS)
        near_ref[0:ROWS, cut] = pick(before, lane + ROWS - row)
        near_ref[ROWS : 2 * ROWS, cut] = jnp.where(
            row > lane, pick(after_it, row - lane), pick(before, lane - row)
        )
        near_ref[2 * ROWS : 3 * ROWS, cut] = pick(after_it, row + ROWS - lane)
        line_ref[h] = before[:8]

    requests = len_ref.shape[1]
    down_it = lax.broadcasted_iota(jnp.int32, (requests, requests), 0)
    along = lax.broadcasted_iota(jnp.int32, (requests, requests), 1)
    length = jnp.broadcast_to(len_ref[...], (requests, requests)).astype(jnp.float32)
    prefix = jnp.broadcast_to(map_ref[...], (requests, requests)).astype(jnp.float32)

    def column(keep, values):
        return jnp.sum(jnp.where(keep, values, 0.0), axis=1, keepdims=True)

    starts = column(along < down_it, length)
    ends = column(along <= down_it, length)
    prefixes = column(along == down_it, prefix)
    number = lax.broadcasted_iota(jnp.int32, (requests, LANES), 0).astype(jnp.float32) + 1.0
    first = place_ref[0] * (PAIRS * ROWS) - ROWS
    for b in range(PAIRS + 2):
        ids = lax.broadcasted_iota(jnp.int32, (requests, LANES), 1) + (first + b * ROWS)
        ids = ids.astype(jnp.float32)
        member = (ids >= starts) & (ids < ends)
        request = jnp.sum(jnp.where(member, number, 0.0), axis=0, keepdims=True) - 1.0
        offset = ids[0:1] - jnp.sum(jnp.where(member, starts, 0.0), axis=0, keepdims=True)
        chosen = jnp.sum(jnp.where(member, prefixes, 0.0), axis=0, keepdims=True)
        facts = jnp.concatenate([request, offset, chosen] + [request] * 5, axis=0)
        name_ref[b] = jnp.broadcast_to(jnp.transpose(facts)[:, 0:1], (ROWS, LANES)).astype(jnp.bfloat16)
        if 0 < b < PAIRS + 1:
            step = b - 1
            asked_ref[step] = facts
            chosen_ref[step] = jnp.broadcast_to(chosen, (ROWS, LANES)).astype(jnp.bfloat16)


def project_kernel(
    x_ref, pair_ref, side_ref, tok_hbm, gain_hbm, cache_hbm, rel_hbm, len_hbm, map_hbm, wq_hbm, wk_hbm, wv_hbm,
    out_ref, near_ref, name_ref, asked_ref, line_ref, chosen_ref,
    tok, gain, cache, rel, lengths, prefix_map, held, arrived, landed,
):
    place_ref = (x_ref[0], pair_ref[0], side_ref[0])
    first = [
        pltpu.make_async_copy(source, target, landed.at[i])
        for i, (source, target) in enumerate(
            (
                (tok_hbm, tok), (gain_hbm, gain), (cache_hbm, cache),
                (rel_hbm, rel), (len_hbm, lengths), (map_hbm, prefix_map),
            )
        )
    ]
    copies = [
        pltpu.make_async_copy(w_hbm, held.at[kind], arrived.at[kind])
        for kind, w_hbm in enumerate((wq_hbm, wk_hbm, wv_hbm))
    ]
    for copy in first + copies:
        copy.start()
    for copy in first:
        copy.wait()
    normed = norm_rows(tok[...], gain[...])
    for part in range(PAIRS):
        for kind in range(2):
            for p in range(PREF_GRP):
                at = 3 * ROWS + (kind * PREF_GRP + p) * SHARE
                cut = slice(kind * D + part * LANES, kind * D + (part + 1) * LANES)
                out_ref[part, at : at + SHARE] = cache[p, :, cut]
    write_tables(
        place_ref, rel, lengths, prefix_map, near_ref, name_ref, asked_ref, line_ref, chosen_ref
    )
    for kind, copy in enumerate(copies):
        copy.wait()
        got = dot(normed, held[kind]).astype(jnp.bfloat16)
        for to in range(PAIRS):
            out_ref[to, kind * ROWS : (kind + 1) * ROWS] = got[:, to * LANES : (to + 1) * LANES]


def project(place, tokens, gain, prefix_cache, rel_bias, lengths, prefix_map, w_query, w_key, w_value):
    small = (tokens, gain.reshape(1, D), prefix_cache, rel_bias.T, lengths, prefix_map)
    out_shape = (
        pltpu.VMEM((PAIRS, SENT, LANES), jnp.bfloat16),
        pltpu.VMEM((3 * ROWS, 2 * ROWS), jnp.float32),
        pltpu.VMEM((PAIRS + 2, ROWS, LANES), jnp.bfloat16),
        pltpu.VMEM((PAIRS, 8, ROWS), jnp.float32),
        pltpu.VMEM((2, 8, LANES), jnp.float32),
        pltpu.VMEM((PAIRS, ROWS, ROWS), jnp.bfloat16),
    )
    blocks, *made = pl.pallas_call(
        project_kernel,
        in_specs=[SMEM_SPEC] * 3 + [HBM_SPEC] * 9,
        out_specs=(VMEM_SPEC,) * 6,
        out_shape=out_shape,
        scratch_shapes=[pltpu.VMEM(value.shape, value.dtype) for value in small]
        + [
            pltpu.VMEM((3, D, D), jnp.bfloat16),
            pltpu.SemaphoreType.DMA((3,)),
            pltpu.SemaphoreType.DMA((6,)),
        ],
        compiler_params=pltpu.CompilerParams(vmem_limit_bytes=VMEM_LIMIT),
        cost_estimate=COST,
        name="project",
    )(*place, *off_chip(*small, w_query, w_key, w_value))
    return blocks, made


def spread_kernel(got_ref, tok_ref, *rest):
    up_ref, down_ref, far_ref, same_ref = rest[-4:]
    for source in range(PAIRS):
        rows = slice(source * 4 * SHARE, (source + 1) * 4 * SHARE)
        held = got_ref[source, 3 * ROWS :]
        up_ref[rows] = held
        down_ref[rows] = held
        far_ref[rows] = held
    up_ref[QUARTER:] = got_ref[PAIRS - 1, ROWS : 3 * ROWS]
    down_ref[QUARTER:] = got_ref[0, ROWS : 3 * ROWS]
    same_ref[...] = tok_ref[...]


def spread(got, tokens, on, off):
    shape = pltpu.VMEM((QUARTER + 2 * ROWS, LANES), jnp.bfloat16)
    return pl.pallas_call(
        spread_kernel,
        in_specs=[VMEM_SPEC] * 3 + [HBM_SPEC],
        out_specs=(VMEM_SPEC,) * 4,
        out_shape=(
            shape,
            shape,
            pltpu.VMEM((QUARTER, LANES), jnp.bfloat16),
            pltpu.VMEM((ROWS, D), jnp.bfloat16),
        ),
        compiler_params=pltpu.CompilerParams(vmem_limit_bytes=VMEM_LIMIT),
        cost_estimate=COST,
        name="spread",
    )(*on_chip(got, tokens, on), *off_chip(off))


def queries(got_ref, chosen_ref, step):
    query = jnp.transpose(got_ref[step, 0:ROWS])
    zero = jnp.zeros((DK, ROWS), jnp.bfloat16)
    stacked = jnp.concatenate(
        [jnp.concatenate([query[:DK], zero], axis=0), jnp.concatenate([zero, query[DK:]], axis=0)], axis=1
    )
    chosen = jnp.concatenate([chosen_ref[step], chosen_ref[step]], axis=1)
    return stacked, jnp.concatenate([stacked * (1 - chosen), stacked * chosen], axis=0)


def masked(scores, name_ref, block, asked_ref, step, bias):
    mine = name_ref[block].astype(jnp.float32) == asked_ref[step, 0:1]
    mine = jnp.concatenate([mine, mine], axis=1)
    return jnp.where(mine, scores + bias, masked_score)


def far_bias(place_ref, rel_ref):
    lane = lax.broadcasted_iota(jnp.int32, (1, 2 * ROWS), 1)
    head = place_ref[1] * 2
    return jnp.where(lane < ROWS, rel_ref[head, 15], rel_ref[head + 1, 15])


def own_head(values):
    return jnp.concatenate([values[:DK, :ROWS], values[DK:, ROWS:]], axis=0)


def by_feature(line):
    return jnp.concatenate(
        [jnp.broadcast_to(line[:, :ROWS], (DK, ROWS)), jnp.broadcast_to(line[:, ROWS:], (DK, ROWS))], axis=0
    )


def select(asked_ref, step, far_out):
    second = jnp.broadcast_to(asked_ref[step, 2:3], (LANES, ROWS)) > 0.5
    return jnp.where(second, own_head(far_out[LANES:]), own_head(far_out[:LANES]))


def quarter_of(rows_at, keys_ref, values_ref):
    for p in range(PREF_GRP):
        pieces = [
            jnp.concatenate(
                [rows_at(source, (kind * PREF_GRP + p) * SHARE) for source in range(PAIRS)], axis=0
            )
            for kind in range(2)
        ]
        keys_ref[:, p * LANES : (p + 1) * LANES] = pieces[0]
        values_ref[p * LANES : (p + 1) * LANES, :] = jnp.transpose(pieces[1])


def start_copies(pairs, landed):
    copies = [pltpu.make_async_copy(a, b, landed.at[i]) for i, (a, b) in enumerate(pairs)]
    for copy in copies:
        copy.start()
    return copies


def own_kernel(
    x_ref, pair_ref, side_ref, rel_ref, got_ref, near_ref, name_ref, asked_ref, line_ref, chosen_ref, in_two, out_hbm, in_hbm,
    stat_ref, acc_ref, tail_ref, split_ref, out_two, turned_one, turned_two,
    keys, values, kwin, vwin, in_one, landed,
):
    place_ref = (x_ref[0], pair_ref[0], side_ref[0])
    copies = start_copies(((out_hbm, out_two), (in_hbm, in_one)), landed)
    for b in (0, PAIRS + 1):
        kwin[b] = jnp.zeros((ROWS, LANES), jnp.bfloat16)
        vwin[b] = jnp.zeros((LANES, ROWS), jnp.bfloat16)
    for b in range(PAIRS):
        kwin[b + 1] = got_ref[b, ROWS : 2 * ROWS]
        vwin[b + 1] = jnp.transpose(got_ref[b, 2 * ROWS : 3 * ROWS])
    quarter_of(lambda s, at: got_ref[s, 3 * ROWS + at : 3 * ROWS + at + SHARE], keys, values)
    is_last = place_ref[0] == 3
    full = far_bias(place_ref, rel_ref)

    row = lax.broadcasted_iota(jnp.int32, (ROWS, LANES), 0)
    lines = [jnp.broadcast_to(line_ref[h, 0:1], (ROWS, LANES)) for h in range(2)]

    def one(step, _):
        offset = jnp.broadcast_to(asked_ref[step, 1:2], (ROWS, LANES)).astype(jnp.int32)
        at = jnp.minimum(ROWS - row + offset, LANES - 1)
        tail = jnp.concatenate([jnp.take_along_axis(line, at, axis=1) for line in lines], axis=1)
        tail_ref[step] = tail
        stacked, split = queries(got_ref, chosen_ref, step)
        split_ref[step] = split
        parts = [dot(keys[...], split) + jnp.where(is_last, tail, full)]
        near_scores = dot(kwin[pl.ds(step, 3)].reshape(3 * ROWS, LANES), stacked)
        for b in range(3):
            at_edge = (step + b == 0) | (step + b == PAIRS + 1)
            cut = slice(b * ROWS, (b + 1) * ROWS)
            bias = near_ref[cut] + jnp.where(at_edge, masked_score, 0.0)
            parts.append(masked(near_scores[cut], name_ref, step + b, asked_ref, step, bias))
        top = jnp.max(functools.reduce(jnp.maximum, parts), axis=0, keepdims=True)
        terms = [jnp.exp(part - top) for part in parts]
        row_sum = jnp.sum(functools.reduce(jnp.add, terms), axis=0, keepdims=True)
        weights = [t.astype(jnp.bfloat16) for t in terms]
        near_values = jnp.concatenate([vwin[step + b] for b in range(3)], axis=1)
        near_out = dot(near_values, jnp.concatenate(weights[1:], axis=0))
        acc_ref[step] = select(asked_ref, step, dot(values[...], weights[0])) + own_head(near_out)
        stat_ref[step, 0:1] = top
        stat_ref[step, 1:2] = row_sum
        return 0

    lax.fori_loop(0, PAIRS, one, 0, unroll=4)
    for copy in copies:
        copy.wait()
    for source, target in ((in_two, turned_two), (in_one, turned_one)):
        for at in range(0, D, LANES):
            target[:, at : at + LANES] = jnp.transpose(source[at : at + LANES])


def attend_own(place, rel_bias, got, made, in_one, in_two, out_two):
    return pl.pallas_call(
        own_kernel,
        in_specs=[SMEM_SPEC] * 4 + [VMEM_SPEC] * 7 + [HBM_SPEC] * 2,
        out_specs=(VMEM_SPEC,) * 7,
        out_shape=(
            pltpu.VMEM((PAIRS, 8, 2 * ROWS), jnp.float32),
            pltpu.VMEM((PAIRS, LANES, ROWS), jnp.float32),
            pltpu.VMEM((PAIRS, ROWS, 2 * ROWS), jnp.float32),
            pltpu.VMEM((PAIRS, PREF_GRP * LANES, 2 * ROWS), jnp.bfloat16),
        )
        + (pltpu.VMEM((D, D), jnp.bfloat16),) * 3,
        scratch_shapes=[
            pltpu.VMEM((PLEN // 4, PREF_GRP * LANES), jnp.bfloat16),
            pltpu.VMEM((PREF_GRP * LANES, PLEN // 4), jnp.bfloat16),
            pltpu.VMEM((PAIRS + 2, ROWS, LANES), jnp.bfloat16),
            pltpu.VMEM((PAIRS + 2, LANES, ROWS), jnp.bfloat16),
            pltpu.VMEM((D, D), jnp.bfloat16),
            pltpu.SemaphoreType.DMA((2,)),
        ],
        compiler_params=pltpu.CompilerParams(vmem_limit_bytes=VMEM_LIMIT),
        cost_estimate=COST,
        name="attend_own",
    )(*place, rel_bias.T, *on_chip(got, *made, in_two), *off_chip(out_two, in_one))


def rest_kernel(
    x_ref, pair_ref, side_ref, rel_ref, prev_ref, next_ref, far_ref, near_ref, name_ref, asked_ref,
    stat_ref, acc_ref, tail_ref, split_ref, _, out_ref, keys, values, kwin, vwin,
):
    place_ref = (x_ref[0], pair_ref[0], side_ref[0])
    turns = ((3, prev_ref), (1, next_ref), (2, far_ref))
    for i, (_, ref) in enumerate(turns):
        quarter_of(
            lambda s, at, ref=ref: ref[s * 4 * SHARE + at : s * 4 * SHARE + at + SHARE], keys.at[i], values.at[i]
        )
    for i, ref in enumerate((prev_ref, next_ref)):
        kwin[i] = ref[QUARTER : QUARTER + ROWS]
        vwin[i] = jnp.transpose(ref[QUARTER + ROWS :])
    is_last = [lax.rem(place_ref[0] + turn, 4) == 3 for turn, _ in turns]
    side = place_ref[2]
    full = far_bias(place_ref, rel_ref)

    def one(step, edge=None):
        split = split_ref[step]
        tail = tail_ref[step]
        scores = dot(keys[...].reshape(3 * PLEN // 4, PREF_GRP * LANES), split)
        parts = [
            scores[i * ROWS : (i + 1) * ROWS] + jnp.where(is_last[i], tail, full) for i in range(3)
        ]
        if edge is not None:
            bias = near_ref[edge * 2 * ROWS : (edge * 2 + 1) * ROWS]
            parts.append(
                masked(dot(kwin[edge], split[:LANES] + split[LANES:]), name_ref, edge * (PAIRS + 1), asked_ref, step, bias)
            )
        before = stat_ref[step, 0:1]
        top = jnp.max(functools.reduce(jnp.maximum, parts), axis=0, keepdims=True)
        top = jnp.maximum(top, before)
        shrink = jnp.exp(before - top)
        terms = [jnp.exp(part - top) for part in parts]
        row_sum = jnp.sum(functools.reduce(jnp.add, terms), axis=0, keepdims=True)
        row_sum = row_sum + stat_ref[step, 1:2] * shrink
        weights = [t.astype(jnp.bfloat16) for t in terms]
        far_values = jnp.concatenate([values[i] for i in range(3)], axis=1)
        far_out = dot(far_values, jnp.concatenate(weights[:3], axis=0))
        acc = acc_ref[step] * by_feature(shrink) + select(asked_ref, step, far_out)
        if edge is not None:
            acc = acc + own_head(dot(vwin[edge], weights[3]))
        done = jnp.transpose(acc * by_feature(1.0 / row_sum)).astype(jnp.bfloat16)
        out_ref[side * PAIRS + step] = done
        out_ref[(1 - side) * PAIRS + jnp.bitwise_xor(step, 1)] = done

    def middle(step, _):
        one(step)
        return 0

    one(jnp.int32(0), 0)
    lax.fori_loop(1, PAIRS - 1, middle, 0, unroll=3)
    one(jnp.int32(PAIRS - 1), 1)


def attend_rest(place, rel_bias, prev, after_it, far, made, part, ready):
    return pl.pallas_call(
        rest_kernel,
        in_specs=[SMEM_SPEC] * 4 + [VMEM_SPEC] * 11,
        out_specs=VMEM_SPEC,
        out_shape=pltpu.VMEM((2 * PAIRS, ROWS, LANES), jnp.bfloat16),
        scratch_shapes=[
            pltpu.VMEM((3, PLEN // 4, PREF_GRP * LANES), jnp.bfloat16),
            pltpu.VMEM((3, PREF_GRP * LANES, PLEN // 4), jnp.bfloat16),
            pltpu.VMEM((2, ROWS, LANES), jnp.bfloat16),
            pltpu.VMEM((2, LANES, ROWS), jnp.bfloat16),
        ],
        compiler_params=pltpu.CompilerParams(vmem_limit_bytes=VMEM_LIMIT),
        cost_estimate=COST,
        name="attend_rest",
    )(*place, rel_bias.T, *on_chip(prev, after_it, far, *made[:3], *part, ready))


def join(side, att_ref, w_ref, tok_ref):
    attended = jnp.concatenate([att_ref[side * PAIRS + j] for j in range(PAIRS)], axis=1)
    return (tok_ref[...].astype(jnp.float32) + dot(attended, w_ref[...])).astype(jnp.bfloat16)


def units_of(normed, in_ref):
    return jnp.maximum(dot(normed, in_ref[...]), 0.0).astype(jnp.bfloat16)


def finish_kernel(side_ref, att_ref, w_ref, tok_ref, gain_ref, in_one, in_two, out_one, out_two, *rest):
    hidden = join(side_ref[0], att_ref, w_ref, tok_ref)
    normed = norm_rows(hidden, gain_ref[...])
    got = hidden.astype(jnp.float32)
    for in_ref, out_w_ref in ((in_one, out_one), (in_two, out_two)):
        got = got + dot(units_of(normed, in_ref), out_w_ref[...])
    rest[-1][...] = got


def finish(side, att, w_attn_out, tokens, gain, weights, *ready):
    return pl.pallas_call(
        finish_kernel,
        in_specs=[SMEM_SPEC] + [VMEM_SPEC] * (8 + len(ready)),
        out_specs=VMEM_SPEC,
        out_shape=pltpu.VMEM((ROWS, D), jnp.float32),
        compiler_params=pltpu.CompilerParams(vmem_limit_bytes=VMEM_LIMIT),
        cost_estimate=COST,
        name="finish",
    )(side, *on_chip(att, w_attn_out, tokens, gain.reshape(1, D), *weights, *ready))


def away_kernel(
    side_ref, att_ref, w_ref, tok_ref, gain_ref, in_one, in_two, out_one, out_two, half_ref, units_ref
):
    hidden = join(1 - side_ref[0], att_ref, w_ref, tok_ref)
    normed = norm_rows(hidden, gain_ref[...])
    units_ref[0] = units_of(normed, in_one)
    units_ref[1] = units_of(normed, in_two)
    got = dot(units_ref[0], out_one[:, :FIRST]) + dot(units_ref[1], out_two[:, :FIRST])
    half_ref[...] = got.astype(half_ref.dtype)


def away(side, att, w_attn_out, tokens, gain, weights):
    return pl.pallas_call(
        away_kernel,
        in_specs=[SMEM_SPEC] + [VMEM_SPEC] * 8,
        out_specs=(VMEM_SPEC,) * 2,
        out_shape=(pltpu.VMEM((ROWS, FIRST), jnp.bfloat16), pltpu.VMEM((2, ROWS, D), jnp.bfloat16)),
        compiler_params=pltpu.CompilerParams(vmem_limit_bytes=VMEM_LIMIT),
        cost_estimate=COST,
        name="away",
    )(side, *on_chip(att, w_attn_out, tokens, gain.reshape(1, D), *weights))


def remainder_kernel(units_ref, out_one, out_two, half_ref):
    got = dot(units_ref[0], out_one[:, FIRST:]) + dot(units_ref[1], out_two[:, FIRST:])
    half_ref[...] = got.astype(half_ref.dtype)


def remainder(units, out_one, out_two):
    return pl.pallas_call(
        remainder_kernel,
        in_specs=[VMEM_SPEC] * 3,
        out_specs=VMEM_SPEC,
        out_shape=pltpu.VMEM((ROWS, D - FIRST), jnp.bfloat16),
        compiler_params=pltpu.CompilerParams(vmem_limit_bytes=VMEM_LIMIT),
        cost_estimate=COST,
        name="remainder",
    )(*on_chip(units, out_one, out_two))


def total_kernel(home_ref, first_ref, second_ref, out_ref):
    for cut, ref in ((slice(0, FIRST), first_ref), (slice(FIRST, D), second_ref)):
        out_ref[:, cut] = (home_ref[:, cut] + ref[...].astype(jnp.float32)).astype(jnp.bfloat16)


def total(home, first, second):
    return pl.pallas_call(
        total_kernel,
        in_specs=[VMEM_SPEC] * 3,
        out_specs=VMEM_SPEC,
        out_shape=jax.ShapeDtypeStruct((ROWS, D), jnp.bfloat16),
        compiler_params=pltpu.CompilerParams(vmem_limit_bytes=VMEM_LIMIT),
        cost_estimate=COST,
        name="total",
    )(*on_chip(home, first, second))


def body(
    tokens,
    attn_gain,
    w_query,
    w_key,
    w_value,
    w_attn_out,
    rel_bias,
    prefix_cache,
    lengths,
    prefix_map,
    mlp_gain,
    w_in,
    w_out,
):
    count_x = lax.axis_size("x")
    plane = lax.axis_index("z") * 2 + lax.axis_index("ylo")
    place = tuple(
        at.astype(jnp.int32).reshape(1) for at in (lax.axis_index("x"), plane, lax.axis_index("yhi"))
    )
    other_in = lax.ppermute(w_in, "core", SWAP)
    other_out = lax.ppermute(w_out, "core", SWAP)
    blocks, made = project(
        place, tokens, attn_gain, prefix_cache, rel_bias, lengths, prefix_map, w_query, w_key, w_value
    )
    got = lax.all_to_all(blocks, PLANE, 0, 0, tiled=True)
    mirrored = ("yhi", "ylo")
    up, down, far, same = spread(got, tokens, other_in, other_out)
    by = lambda d: [(i, (i + d) % count_x) for i in range(count_x)]
    opposite = lax.ppermute(far, "x", by(2))
    prev = lax.ppermute(up, "x", by(1))
    later = lax.ppermute(down, "x", by(-1))
    far_tokens = lax.ppermute(same, mirrored, MIRROR)
    *part, other_out, turned, other_turned = attend_own(
        place, rel_bias, got, made, w_in, other_in, other_out
    )
    mixed = attend_rest(place, rel_bias, prev, later, opposite, made, part, far_tokens)
    weights = (turned, other_turned, w_out, other_out)
    att = lax.all_to_all(mixed, ("yhi",) + PLANE, 0, 0, tiled=True)

    first, units = away(place[2], att, w_attn_out, far_tokens, mlp_gain, weights)
    first_back = lax.ppermute(first, mirrored, MIRROR)
    second = remainder(units, *weights[2:])
    second_back = lax.ppermute(second, mirrored, MIRROR)
    local = finish(place[2], att, w_attn_out, tokens, mlp_gain, weights, second)
    return total(local, first_back, second_back)


def solution(mesh):
    split = Mesh(mesh.devices.reshape(2, 2, 4, 4, 2), AXES)
    grp, req = ("yhi", "core"), REQ
    return jax.shard_map(
        body,
        mesh=split,
        in_specs=(
            P(grp + req, None),
            P(),
            P(),
            P(),
            P(),
            P(),
            P(),
            P(grp, req, None),
            P(grp, None),
            P(grp, None),
            P(),
            P(grp, None),
            P(grp, None),
        ),
        out_specs=P(grp + req, None),
        check_vma=False,
    )
```

```python
import functools

import jax
import jax.numpy as jnp
from jax import lax
from jax.experimental import pallas as pl
from jax.experimental.pallas import tpu as pltpu
from jax.sharding import Mesh, PartitionSpec as P

D = 1024
H = 16
DK = 64
PLEN = 512
PREF_GRP = 2
ROWS = 128
PAIRS = 8
LANES = 128
FIRST = 640
SHARE = 16
SENT = 3 * ROWS + 2 * PREF_GRP * SHARE
QUARTER = PAIRS * 2 * PREF_GRP * SHARE

epsilon = 1e-06
far_marks = (12, 16, 23, 32, 46, 64, 91)
masked_score = -1e30
VMEM_LIMIT = 16 * 1024 * 1024
COST = pl.CostEstimate(flops=1000, transcendentals=0, bytes_accessed=1000)

AXES = ("yhi", "core", "x", "z", "ylo")
REQ = ("x", "z", "ylo")
PLANE = ("z", "ylo")
MIRROR = [(0, 3), (3, 0), (1, 2), (2, 1)]
SWAP = [(0, 1), (1, 0)]


def norm_rows(values_in, gain):
    widened = values_in.astype(jnp.float32)
    scale = lax.rsqrt(jnp.mean(widened * widened, axis=-1, keepdims=True) + epsilon)
    return (widened * scale * gain).astype(jnp.bfloat16)


def dot(a, b):
    return jnp.dot(a, b, preferred_element_type=jnp.float32)


def on_chip(*arrays):
    return tuple(pltpu.with_memory_space_constraint(a, pltpu.VMEM) for a in arrays)


def off_chip(*arrays):
    return tuple(pltpu.with_memory_space_constraint(a, pltpu.HBM) for a in arrays)


VMEM_SPEC = pl.BlockSpec(memory_space=pltpu.VMEM)
HBM_SPEC = pl.BlockSpec(memory_space=pltpu.HBM)
SMEM_SPEC = pl.BlockSpec(memory_space=pltpu.SMEM)


def bias_line(rel_ref, head, first_bucket):
    lane = lax.broadcasted_iota(jnp.int32, (8, LANES), 1)

    def of(bucket):
        return rel_ref[pl.ds(head, 1), first_bucket + bucket : first_bucket + bucket + 1]

    line = jnp.broadcast_to(of(0), (8, LANES))
    for bucket in range(1, 16):
        mark = bucket if bucket <= 8 else far_marks[bucket - 9]
        line = jnp.where(lane >= mark, of(bucket), line)
    return jnp.broadcast_to(line[0:1], (ROWS, LANES))


def write_tables(
    place_ref, rel_ref, len_ref, map_ref, near_ref, name_ref, asked_ref, line_ref, chosen_ref
):
    row = lax.broadcasted_iota(jnp.int32, (ROWS, LANES), 0)
    lane = lax.broadcasted_iota(jnp.int32, (ROWS, LANES), 1)
    for h in range(2):
        head = place_ref[1] * 2 + h
        before = bias_line(rel_ref, head, 0)
        after_it = bias_line(rel_ref, head, 16)

        def pick(line, distance):
            return jnp.take_along_axis(line, jnp.clip(distance, 0, LANES - 1), axis=1)

        cut = slice(h * ROWS, (h + 1) * ROWS)
        near_ref[0:ROWS, cut] = pick(before, lane + ROWS - row)
        near_ref[ROWS : 2 * ROWS, cut] = jnp.where(
            row > lane, pick(after_it, row - lane), pick(before, lane - row)
        )
        near_ref[2 * ROWS : 3 * ROWS, cut] = pick(after_it, row + ROWS - lane)
        line_ref[h] = before[:8]

    requests = len_ref.shape[1]
    down_it = lax.broadcasted_iota(jnp.int32, (requests, requests), 0)
    along = lax.broadcasted_iota(jnp.int32, (requests, requests), 1)
    length = jnp.broadcast_to(len_ref[...], (requests, requests)).astype(jnp.float32)
    prefix = jnp.broadcast_to(map_ref[...], (requests, requests)).astype(jnp.float32)

    def column(keep, values):
        return jnp.sum(jnp.where(keep, values, 0.0), axis=1, keepdims=True)

    starts = column(along < down_it, length)
    ends = column(along <= down_it, length)
    prefixes = column(along == down_it, prefix)
    number = lax.broadcasted_iota(jnp.int32, (requests, LANES), 0).astype(jnp.float32) + 1.0
    first = place_ref[0] * (PAIRS * ROWS) - ROWS
    for b in range(PAIRS + 2):
        ids = lax.broadcasted_iota(jnp.int32, (requests, LANES), 1) + (first + b * ROWS)
        ids = ids.astype(jnp.float32)
        member = (ids >= starts) & (ids < ends)
        request = jnp.sum(jnp.where(member, number, 0.0), axis=0, keepdims=True) - 1.0
        offset = ids[0:1] - jnp.sum(jnp.where(member, starts, 0.0), axis=0, keepdims=True)
        chosen = jnp.sum(jnp.where(member, prefixes, 0.0), axis=0, keepdims=True)
        facts = jnp.concatenate([request, offset, chosen] + [request] * 5, axis=0)
        name_ref[b] = jnp.broadcast_to(jnp.transpose(facts)[:, 0:1], (ROWS, LANES)).astype(jnp.bfloat16)
        if 0 < b < PAIRS + 1:
            step = b - 1
            asked_ref[step] = facts
            chosen_ref[step] = jnp.broadcast_to(chosen, (ROWS, LANES)).astype(jnp.bfloat16)


def project_kernel(
    x_ref, pair_ref, side_ref, tok_hbm, gain_hbm, cache_hbm, rel_hbm, len_hbm, map_hbm, wq_hbm, wk_hbm, wv_hbm,
    out_ref, near_ref, name_ref, asked_ref, line_ref, chosen_ref,
    tok, gain, cache, rel, lengths, prefix_map, held, arrived, landed,
):
    place_ref = (x_ref[0], pair_ref[0], side_ref[0])
    first = [
        pltpu.make_async_copy(source, target, landed.at[i])
        for i, (source, target) in enumerate(
            (
                (tok_hbm, tok), (gain_hbm, gain), (cache_hbm, cache),
                (rel_hbm, rel), (len_hbm, lengths), (map_hbm, prefix_map),
            )
        )
    ]
    copies = [
        pltpu.make_async_copy(w_hbm, held.at[kind], arrived.at[kind])
        for kind, w_hbm in enumerate((wq_hbm, wk_hbm, wv_hbm))
    ]
    for copy in first + copies:
        copy.start()
    for copy in first:
        copy.wait()
    normed = norm_rows(tok[...], gain[...])
    for part in range(PAIRS):
        for kind in range(2):
            for p in range(PREF_GRP):
                at = 3 * ROWS + (kind * PREF_GRP + p) * SHARE
                cut = slice(kind * D + part * LANES, kind * D + (part + 1) * LANES)
                out_ref[part, at : at + SHARE] = cache[p, :, cut]
    write_tables(
        place_ref, rel, lengths, prefix_map, near_ref, name_ref, asked_ref, line_ref, chosen_ref
    )
    for kind, copy in enumerate(copies):
        copy.wait()
        got = dot(normed, held[kind]).astype(jnp.bfloat16)
        for to in range(PAIRS):
            out_ref[to, kind * ROWS : (kind + 1) * ROWS] = got[:, to * LANES : (to + 1) * LANES]


def project(place, tokens, gain, prefix_cache, rel_bias, lengths, prefix_map, w_query, w_key, w_value):
    small = (tokens, gain.reshape(1, D), prefix_cache, rel_bias.T, lengths, prefix_map)
    out_shape = (
        pltpu.VMEM((PAIRS, SENT, LANES), jnp.bfloat16),
        pltpu.VMEM((3 * ROWS, 2 * ROWS), jnp.float32),
        pltpu.VMEM((PAIRS + 2, ROWS, LANES), jnp.bfloat16),
        pltpu.VMEM((PAIRS, 8, ROWS), jnp.float32),
        pltpu.VMEM((2, 8, LANES), jnp.float32),
        pltpu.VMEM((PAIRS, ROWS, ROWS), jnp.bfloat16),
    )
    blocks, *made = pl.pallas_call(
        project_kernel,
        in_specs=[SMEM_SPEC] * 3 + [HBM_SPEC] * 9,
        out_specs=(VMEM_SPEC,) * 6,
        out_shape=out_shape,
        scratch_shapes=[pltpu.VMEM(value.shape, value.dtype) for value in small]
        + [
            pltpu.VMEM((3, D, D), jnp.bfloat16),
            pltpu.SemaphoreType.DMA((3,)),
            pltpu.SemaphoreType.DMA((6,)),
        ],
        compiler_params=pltpu.CompilerParams(vmem_limit_bytes=VMEM_LIMIT),
        cost_estimate=COST,
        name="project",
    )(*place, *off_chip(*small, w_query, w_key, w_value))
    return blocks, made


def spread_kernel(got_ref, tok_ref, *rest):
    up_ref, down_ref, far_ref, same_ref = rest[-4:]
    for source in range(PAIRS):
        rows = slice(source * 4 * SHARE, (source + 1) * 4 * SHARE)
        held = got_ref[source, 3 * ROWS :]
        up_ref[rows] = held
        down_ref[rows] = held
        far_ref[rows] = held
    up_ref[QUARTER:] = got_ref[PAIRS - 1, ROWS : 3 * ROWS]
    down_ref[QUARTER:] = got_ref[0, ROWS : 3 * ROWS]
    same_ref[...] = tok_ref[...]


def spread(got, tokens, on, off):
    shape = pltpu.VMEM((QUARTER + 2 * ROWS, LANES), jnp.bfloat16)
    return pl.pallas_call(
        spread_kernel,
        in_specs=[VMEM_SPEC] * 3 + [HBM_SPEC],
        out_specs=(VMEM_SPEC,) * 4,
        out_shape=(
            shape,
            shape,
            pltpu.VMEM((QUARTER, LANES), jnp.bfloat16),
            pltpu.VMEM((ROWS, D), jnp.bfloat16),
        ),
        compiler_params=pltpu.CompilerParams(vmem_limit_bytes=VMEM_LIMIT),
        cost_estimate=COST,
        name="spread",
    )(*on_chip(got, tokens, on), *off_chip(off))


def queries(got_ref, chosen_ref, step):
    query = jnp.transpose(got_ref[step, 0:ROWS])
    zero = jnp.zeros((DK, ROWS), jnp.bfloat16)
    stacked = jnp.concatenate(
        [jnp.concatenate([query[:DK], zero], axis=0), jnp.concatenate([zero, query[DK:]], axis=0)], axis=1
    )
    chosen = jnp.concatenate([chosen_ref[step], chosen_ref[step]], axis=1)
    return stacked, jnp.concatenate([stacked * (1 - chosen), stacked * chosen], axis=0)


def masked(scores, name_ref, block, asked_ref, step, bias):
    mine = name_ref[block].astype(jnp.float32) == asked_ref[step, 0:1]
    mine = jnp.concatenate([mine, mine], axis=1)
    return jnp.where(mine, scores + bias, masked_score)


def far_bias(place_ref, rel_ref):
    lane = lax.broadcasted_iota(jnp.int32, (1, 2 * ROWS), 1)
    head = place_ref[1] * 2
    return jnp.where(lane < ROWS, rel_ref[head, 15], rel_ref[head + 1, 15])


def own_head(values):
    return jnp.concatenate([values[:DK, :ROWS], values[DK:, ROWS:]], axis=0)


def by_feature(line):
    return jnp.concatenate(
        [jnp.broadcast_to(line[:, :ROWS], (DK, ROWS)), jnp.broadcast_to(line[:, ROWS:], (DK, ROWS))], axis=0
    )


def select(asked_ref, step, far_out):
    second = jnp.broadcast_to(asked_ref[step, 2:3], (LANES, ROWS)) > 0.5
    return jnp.where(second, own_head(far_out[LANES:]), own_head(far_out[:LANES]))


def quarter_of(rows_at, keys_ref, values_ref):
    for p in range(PREF_GRP):
        pieces = [
            jnp.concatenate(
                [rows_at(source, (kind * PREF_GRP + p) * SHARE) for source in range(PAIRS)], axis=0
            )
            for kind in range(2)
        ]
        keys_ref[:, p * LANES : (p + 1) * LANES] = pieces[0]
        values_ref[p * LANES : (p + 1) * LANES, :] = jnp.transpose(pieces[1])


def start_copies(pairs, landed):
    copies = [pltpu.make_async_copy(a, b, landed.at[i]) for i, (a, b) in enumerate(pairs)]
    for copy in copies:
        copy.start()
    return copies


def own_kernel(
    x_ref, pair_ref, side_ref, rel_ref, got_ref, near_ref, name_ref, asked_ref, line_ref, chosen_ref, in_two, out_hbm, in_hbm,
    stat_ref, acc_ref, tail_ref, split_ref, out_two, turned_one, turned_two,
    keys, values, kwin, vwin, in_one, landed,
):
    place_ref = (x_ref[0], pair_ref[0], side_ref[0])
    copies = start_copies(((out_hbm, out_two), (in_hbm, in_one)), landed)
    for b in (0, PAIRS + 1):
        kwin[b] = jnp.zeros((ROWS, LANES), jnp.bfloat16)
        vwin[b] = jnp.zeros((LANES, ROWS), jnp.bfloat16)
    for b in range(PAIRS):
        kwin[b + 1] = got_ref[b, ROWS : 2 * ROWS]
        vwin[b + 1] = jnp.transpose(got_ref[b, 2 * ROWS : 3 * ROWS])
    quarter_of(lambda s, at: got_ref[s, 3 * ROWS + at : 3 * ROWS + at + SHARE], keys, values)
    is_last = place_ref[0] == 3
    full = far_bias(place_ref, rel_ref)

    row = lax.broadcasted_iota(jnp.int32, (ROWS, LANES), 0)
    lines = [jnp.broadcast_to(line_ref[h, 0:1], (ROWS, LANES)) for h in range(2)]

    def one(step, _):
        offset = jnp.broadcast_to(asked_ref[step, 1:2], (ROWS, LANES)).astype(jnp.int32)
        at = jnp.minimum(ROWS - row + offset, LANES - 1)
        tail = jnp.concatenate([jnp.take_along_axis(line, at, axis=1) for line in lines], axis=1)
        tail_ref[step] = tail
        stacked, split = queries(got_ref, chosen_ref, step)
        split_ref[step] = split
        parts = [dot(keys[...], split) + jnp.where(is_last, tail, full)]
        near_scores = dot(kwin[pl.ds(step, 3)].reshape(3 * ROWS, LANES), stacked)
        for b in range(3):
            at_edge = (step + b == 0) | (step + b == PAIRS + 1)
            cut = slice(b * ROWS, (b + 1) * ROWS)
            bias = near_ref[cut] + jnp.where(at_edge, masked_score, 0.0)
            parts.append(masked(near_scores[cut], name_ref, step + b, asked_ref, step, bias))
        top = jnp.max(functools.reduce(jnp.maximum, parts), axis=0, keepdims=True)
        terms = [jnp.exp(part - top) for part in parts]
        row_sum = jnp.sum(functools.reduce(jnp.add, terms), axis=0, keepdims=True)
        weights = [t.astype(jnp.bfloat16) for t in terms]
        near_values = jnp.concatenate([vwin[step + b] for b in range(3)], axis=1)
        near_out = dot(near_values, jnp.concatenate(weights[1:], axis=0))
        acc_ref[step] = select(asked_ref, step, dot(values[...], weights[0])) + own_head(near_out)
        stat_ref[step, 0:1] = top
        stat_ref[step, 1:2] = row_sum
        return 0

    lax.fori_loop(0, PAIRS, one, 0, unroll=PAIRS)
    for copy in copies:
        copy.wait()
    for source, target in ((in_two, turned_two), (in_one, turned_one)):
        for at in range(0, D, LANES):
            target[:, at : at + LANES] = jnp.transpose(source[at : at + LANES])


def attend_own(place, rel_bias, got, made, in_one, in_two, out_two):
    return pl.pallas_call(
        own_kernel,
        in_specs=[SMEM_SPEC] * 4 + [VMEM_SPEC] * 7 + [HBM_SPEC] * 2,
        out_specs=(VMEM_SPEC,) * 7,
        out_shape=(
            pltpu.VMEM((PAIRS, 8, 2 * ROWS), jnp.float32),
            pltpu.VMEM((PAIRS, LANES, ROWS), jnp.float32),
            pltpu.VMEM((PAIRS, ROWS, 2 * ROWS), jnp.float32),
            pltpu.VMEM((PAIRS, PREF_GRP * LANES, 2 * ROWS), jnp.bfloat16),
        )
        + (pltpu.VMEM((D, D), jnp.bfloat16),) * 3,
        scratch_shapes=[
            pltpu.VMEM((PLEN // 4, PREF_GRP * LANES), jnp.bfloat16),
            pltpu.VMEM((PREF_GRP * LANES, PLEN // 4), jnp.bfloat16),
            pltpu.VMEM((PAIRS + 2, ROWS, LANES), jnp.bfloat16),
            pltpu.VMEM((PAIRS + 2, LANES, ROWS), jnp.bfloat16),
            pltpu.VMEM((D, D), jnp.bfloat16),
            pltpu.SemaphoreType.DMA((2,)),
        ],
        compiler_params=pltpu.CompilerParams(vmem_limit_bytes=VMEM_LIMIT),
        cost_estimate=COST,
        name="attend_own",
    )(*place, rel_bias.T, *on_chip(got, *made, in_two), *off_chip(out_two, in_one))


def rest_kernel(
    x_ref, pair_ref, side_ref, rel_ref, prev_ref, next_ref, far_ref, near_ref, name_ref, asked_ref,
    stat_ref, acc_ref, tail_ref, split_ref, _, out_ref, keys, values, kwin, vwin,
):
    place_ref = (x_ref[0], pair_ref[0], side_ref[0])
    turns = ((3, prev_ref), (1, next_ref), (2, far_ref))
    for i, (_, ref) in enumerate(turns):
        quarter_of(
            lambda s, at, ref=ref: ref[s * 4 * SHARE + at : s * 4 * SHARE + at + SHARE], keys.at[i], values.at[i]
        )
    for i, ref in enumerate((prev_ref, next_ref)):
        kwin[i] = ref[QUARTER : QUARTER + ROWS]
        vwin[i] = jnp.transpose(ref[QUARTER + ROWS :])
    is_last = [lax.rem(place_ref[0] + turn, 4) == 3 for turn, _ in turns]
    side = place_ref[2]
    full = far_bias(place_ref, rel_ref)

    def one(step, edge=None):
        split = split_ref[step]
        tail = tail_ref[step]
        scores = dot(keys[...].reshape(3 * PLEN // 4, PREF_GRP * LANES), split)
        parts = [
            scores[i * ROWS : (i + 1) * ROWS] + jnp.where(is_last[i], tail, full) for i in range(3)
        ]
        if edge is not None:
            bias = near_ref[edge * 2 * ROWS : (edge * 2 + 1) * ROWS]
            parts.append(
                masked(dot(kwin[edge], split[:LANES] + split[LANES:]), name_ref, edge * (PAIRS + 1), asked_ref, step, bias)
            )
        before = stat_ref[step, 0:1]
        top = jnp.max(functools.reduce(jnp.maximum, parts), axis=0, keepdims=True)
        top = jnp.maximum(top, before)
        shrink = jnp.exp(before - top)
        terms = [jnp.exp(part - top) for part in parts]
        row_sum = jnp.sum(functools.reduce(jnp.add, terms), axis=0, keepdims=True)
        row_sum = row_sum + stat_ref[step, 1:2] * shrink
        weights = [t.astype(jnp.bfloat16) for t in terms]
        far_values = jnp.concatenate([values[i] for i in range(3)], axis=1)
        far_out = dot(far_values, jnp.concatenate(weights[:3], axis=0))
        acc = acc_ref[step] * by_feature(shrink) + select(asked_ref, step, far_out)
        if edge is not None:
            acc = acc + own_head(dot(vwin[edge], weights[3]))
        done = jnp.transpose(acc * by_feature(1.0 / row_sum)).astype(jnp.bfloat16)
        out_ref[side * PAIRS + step] = done
        out_ref[(1 - side) * PAIRS + jnp.bitwise_xor(step, 1)] = done

    def middle(step, _):
        one(step)
        return 0

    one(jnp.int32(0), 0)
    lax.fori_loop(1, PAIRS - 1, middle, 0, unroll=PAIRS - 2)
    one(jnp.int32(PAIRS - 1), 1)


def attend_rest(place, rel_bias, prev, after_it, far, made, part, ready):
    return pl.pallas_call(
        rest_kernel,
        in_specs=[SMEM_SPEC] * 4 + [VMEM_SPEC] * 11,
        out_specs=VMEM_SPEC,
        out_shape=pltpu.VMEM((2 * PAIRS, ROWS, LANES), jnp.bfloat16),
        scratch_shapes=[
            pltpu.VMEM((3, PLEN // 4, PREF_GRP * LANES), jnp.bfloat16),
            pltpu.VMEM((3, PREF_GRP * LANES, PLEN // 4), jnp.bfloat16),
            pltpu.VMEM((2, ROWS, LANES), jnp.bfloat16),
            pltpu.VMEM((2, LANES, ROWS), jnp.bfloat16),
        ],
        compiler_params=pltpu.CompilerParams(vmem_limit_bytes=VMEM_LIMIT),
        cost_estimate=COST,
        name="attend_rest",
    )(*place, rel_bias.T, *on_chip(prev, after_it, far, *made[:3], *part, ready))


def join(side, att_ref, w_ref, tok_ref):
    attended = jnp.concatenate([att_ref[side * PAIRS + j] for j in range(PAIRS)], axis=1)
    return (tok_ref[...].astype(jnp.float32) + dot(attended, w_ref[...])).astype(jnp.bfloat16)


def units_of(normed, in_ref):
    return jnp.maximum(dot(normed, in_ref[...]), 0.0).astype(jnp.bfloat16)


def finish_kernel(side_ref, att_ref, w_ref, tok_ref, gain_ref, in_one, in_two, out_one, out_two, *rest):
    hidden = join(side_ref[0], att_ref, w_ref, tok_ref)
    normed = norm_rows(hidden, gain_ref[...])
    got = hidden.astype(jnp.float32)
    for in_ref, out_w_ref in ((in_one, out_one), (in_two, out_two)):
        got = got + dot(units_of(normed, in_ref), out_w_ref[...])
    rest[-1][...] = got


def finish(side, att, w_attn_out, tokens, gain, weights, *ready):
    return pl.pallas_call(
        finish_kernel,
        in_specs=[SMEM_SPEC] + [VMEM_SPEC] * (8 + len(ready)),
        out_specs=VMEM_SPEC,
        out_shape=pltpu.VMEM((ROWS, D), jnp.float32),
        compiler_params=pltpu.CompilerParams(vmem_limit_bytes=VMEM_LIMIT),
        cost_estimate=COST,
        name="finish",
    )(side, *on_chip(att, w_attn_out, tokens, gain.reshape(1, D), *weights, *ready))


def away_kernel(
    side_ref, att_ref, w_ref, tok_ref, gain_ref, in_one, in_two, out_one, out_two, half_ref, units_ref
):
    hidden = join(1 - side_ref[0], att_ref, w_ref, tok_ref)
    normed = norm_rows(hidden, gain_ref[...])
    units_ref[0] = units_of(normed, in_one)
    units_ref[1] = units_of(normed, in_two)
    got = dot(units_ref[0], out_one[:, :FIRST]) + dot(units_ref[1], out_two[:, :FIRST])
    half_ref[...] = got.astype(half_ref.dtype)


def away(side, att, w_attn_out, tokens, gain, weights):
    return pl.pallas_call(
        away_kernel,
        in_specs=[SMEM_SPEC] + [VMEM_SPEC] * 8,
        out_specs=(VMEM_SPEC,) * 2,
        out_shape=(pltpu.VMEM((ROWS, FIRST), jnp.bfloat16), pltpu.VMEM((2, ROWS, D), jnp.bfloat16)),
        compiler_params=pltpu.CompilerParams(vmem_limit_bytes=VMEM_LIMIT),
        cost_estimate=COST,
        name="away",
    )(side, *on_chip(att, w_attn_out, tokens, gain.reshape(1, D), *weights))


def remainder_kernel(units_ref, out_one, out_two, half_ref):
    got = dot(units_ref[0], out_one[:, FIRST:]) + dot(units_ref[1], out_two[:, FIRST:])
    half_ref[...] = got.astype(half_ref.dtype)


def remainder(units, out_one, out_two):
    return pl.pallas_call(
        remainder_kernel,
        in_specs=[VMEM_SPEC] * 3,
        out_specs=VMEM_SPEC,
        out_shape=pltpu.VMEM((ROWS, D - FIRST), jnp.bfloat16),
        compiler_params=pltpu.CompilerParams(vmem_limit_bytes=VMEM_LIMIT),
        cost_estimate=COST,
        name="remainder",
    )(*on_chip(units, out_one, out_two))


def total_kernel(home_ref, first_ref, second_ref, out_ref):
    for cut, ref in ((slice(0, FIRST), first_ref), (slice(FIRST, D), second_ref)):
        out_ref[:, cut] = (home_ref[:, cut] + ref[...].astype(jnp.float32)).astype(jnp.bfloat16)


def total(home, first, second):
    return pl.pallas_call(
        total_kernel,
        in_specs=[VMEM_SPEC] * 3,
        out_specs=VMEM_SPEC,
        out_shape=jax.ShapeDtypeStruct((ROWS, D), jnp.bfloat16),
        compiler_params=pltpu.CompilerParams(vmem_limit_bytes=VMEM_LIMIT),
        cost_estimate=COST,
        name="total",
    )(*on_chip(home, first, second))


def body(
    tokens,
    attn_gain,
    w_query,
    w_key,
    w_value,
    w_attn_out,
    rel_bias,
    prefix_cache,
    lengths,
    prefix_map,
    mlp_gain,
    w_in,
    w_out,
):
    count_x = lax.axis_size("x")
    plane = lax.axis_index("z") * 2 + lax.axis_index("ylo")
    place = tuple(
        at.astype(jnp.int32).reshape(1) for at in (lax.axis_index("x"), plane, lax.axis_index("yhi"))
    )
    other_in = lax.ppermute(w_in, "core", SWAP)
    other_out = lax.ppermute(w_out, "core", SWAP)
    blocks, made = project(
        place, tokens, attn_gain, prefix_cache, rel_bias, lengths, prefix_map, w_query, w_key, w_value
    )
    got = lax.all_to_all(blocks, PLANE, 0, 0, tiled=True)
    mirrored = ("yhi", "ylo")
    up, down, far, same = spread(got, tokens, other_in, other_out)
    by = lambda d: [(i, (i + d) % count_x) for i in range(count_x)]
    opposite = lax.ppermute(far, "x", by(2))
    prev = lax.ppermute(up, "x", by(1))
    later = lax.ppermute(down, "x", by(-1))
    far_tokens = lax.ppermute(same, mirrored, MIRROR)
    *part, other_out, turned, other_turned = attend_own(
        place, rel_bias, got, made, w_in, other_in, other_out
    )
    mixed = attend_rest(place, rel_bias, prev, later, opposite, made, part, far_tokens)
    weights = (turned, other_turned, w_out, other_out)
    att = lax.all_to_all(mixed, ("yhi",) + PLANE, 0, 0, tiled=True)

    first, units = away(place[2], att, w_attn_out, far_tokens, mlp_gain, weights)
    first_back = lax.ppermute(first, mirrored, MIRROR)
    second = remainder(units, *weights[2:])
    second_back = lax.ppermute(second, mirrored, MIRROR)
    local = finish(place[2], att, w_attn_out, tokens, mlp_gain, weights, second)
    return total(local, first_back, second_back)


def solution(mesh):
    split = Mesh(mesh.devices.reshape(2, 2, 4, 4, 2), AXES)
    grp, req = ("yhi", "core"), REQ
    return jax.shard_map(
        body,
        mesh=split,
        in_specs=(
            P(grp + req, None),
            P(),
            P(),
            P(),
            P(),
            P(),
            P(),
            P(grp, req, None),
            P(grp, None),
            P(grp, None),
            P(),
            P(grp, None),
            P(grp, None),
        ),
        out_specs=P(grp + req, None),
        check_vma=False,
    )
```

```python
import functools

import jax
import jax.numpy as jnp
from jax import lax
from jax.experimental import pallas as pl
from jax.experimental.pallas import tpu as pltpu
from jax.sharding import Mesh, PartitionSpec as P

D = 1024
H = 16
DK = 64
PLEN = 512
PREF_GRP = 2
ROWS = 128
PAIRS = 8
LANES = 128
FIRST = 640
SHARE = 16
SENT = 3 * ROWS + 2 * PREF_GRP * SHARE
QUARTER = PAIRS * 2 * PREF_GRP * SHARE

epsilon = 1e-06
far_marks = (12, 16, 23, 32, 46, 64, 91)
masked_score = -1e30
VMEM_LIMIT = 16 * 1024 * 1024
COST = pl.CostEstimate(flops=1000, transcendentals=0, bytes_accessed=1000)

AXES = ("yhi", "core", "x", "z", "ylo")
REQ = ("x", "z", "ylo")
PLANE = ("z", "ylo")
MIRROR = [(0, 3), (3, 0), (1, 2), (2, 1)]
SWAP = [(0, 1), (1, 0)]


def norm_rows(values_in, gain):
    widened = values_in.astype(jnp.float32)
    scale = lax.rsqrt(jnp.mean(widened * widened, axis=-1, keepdims=True) + epsilon)
    return (widened * scale * gain).astype(jnp.bfloat16)


def dot(a, b):
    return jnp.dot(a, b, preferred_element_type=jnp.float32)


def on_chip(*arrays):
    return tuple(pltpu.with_memory_space_constraint(a, pltpu.VMEM) for a in arrays)


def off_chip(*arrays):
    return tuple(pltpu.with_memory_space_constraint(a, pltpu.HBM) for a in arrays)


VMEM_SPEC = pl.BlockSpec(memory_space=pltpu.VMEM)
HBM_SPEC = pl.BlockSpec(memory_space=pltpu.HBM)
SMEM_SPEC = pl.BlockSpec(memory_space=pltpu.SMEM)


def bias_line(rel_ref, head, first_bucket):
    lane = lax.broadcasted_iota(jnp.int32, (8, LANES), 1)

    def of(bucket):
        return rel_ref[pl.ds(head, 1), first_bucket + bucket : first_bucket + bucket + 1]

    line = jnp.broadcast_to(of(0), (8, LANES))
    for bucket in range(1, 16):
        mark = bucket if bucket <= 8 else far_marks[bucket - 9]
        line = jnp.where(lane >= mark, of(bucket), line)
    return jnp.broadcast_to(line[0:1], (ROWS, LANES))


def write_tables(
    place_ref, rel_ref, len_ref, map_ref, near_ref, name_ref, asked_ref, line_ref, chosen_ref
):
    row = lax.broadcasted_iota(jnp.int32, (ROWS, LANES), 0)
    lane = lax.broadcasted_iota(jnp.int32, (ROWS, LANES), 1)
    for h in range(2):
        head = place_ref[1] * 2 + h
        before = bias_line(rel_ref, head, 0)
        after_it = bias_line(rel_ref, head, 16)

        def pick(line, distance):
            return jnp.take_along_axis(line, jnp.clip(distance, 0, LANES - 1), axis=1)

        cut = slice(h * ROWS, (h + 1) * ROWS)
        near_ref[0:ROWS, cut] = pick(before, lane + ROWS - row)
        near_ref[ROWS : 2 * ROWS, cut] = jnp.where(
            row > lane, pick(after_it, row - lane), pick(before, lane - row)
        )
        near_ref[2 * ROWS : 3 * ROWS, cut] = pick(after_it, row + ROWS - lane)
        line_ref[h] = before[:8]

    requests = len_ref.shape[1]
    down_it = lax.broadcasted_iota(jnp.int32, (requests, requests), 0)
    along = lax.broadcasted_iota(jnp.int32, (requests, requests), 1)
    length = jnp.broadcast_to(len_ref[...], (requests, requests)).astype(jnp.float32)
    prefix = jnp.broadcast_to(map_ref[...], (requests, requests)).astype(jnp.float32)

    def column(keep, values):
        return jnp.sum(jnp.where(keep, values, 0.0), axis=1, keepdims=True)

    starts = column(along < down_it, length)
    ends = column(along <= down_it, length)
    prefixes = column(along == down_it, prefix)
    number = lax.broadcasted_iota(jnp.int32, (requests, LANES), 0).astype(jnp.float32) + 1.0
    first = place_ref[0] * (PAIRS * ROWS) - ROWS
    for b in range(PAIRS + 2):
        ids = lax.broadcasted_iota(jnp.int32, (requests, LANES), 1) + (first + b * ROWS)
        ids = ids.astype(jnp.float32)
        member = (ids >= starts) & (ids < ends)
        request = jnp.sum(jnp.where(member, number, 0.0), axis=0, keepdims=True) - 1.0
        offset = ids[0:1] - jnp.sum(jnp.where(member, starts, 0.0), axis=0, keepdims=True)
        chosen = jnp.sum(jnp.where(member, prefixes, 0.0), axis=0, keepdims=True)
        facts = jnp.concatenate([request, offset, chosen] + [request] * 5, axis=0)
        name_ref[b] = jnp.broadcast_to(jnp.transpose(facts)[:, 0:1], (ROWS, LANES)).astype(jnp.bfloat16)
        if 0 < b < PAIRS + 1:
            step = b - 1
            asked_ref[step] = facts
            chosen_ref[step] = jnp.broadcast_to(chosen, (ROWS, LANES)).astype(jnp.bfloat16)


def project_kernel(
    x_ref, pair_ref, side_ref, tok_hbm, gain_hbm, cache_hbm, rel_hbm, len_hbm, map_hbm, wq_hbm, wk_hbm, wv_hbm,
    out_ref, near_ref, name_ref, asked_ref, line_ref, chosen_ref,
    tok, gain, cache, rel, lengths, prefix_map, held, arrived, landed,
):
    place_ref = (x_ref[0], pair_ref[0], side_ref[0])
    first = [
        pltpu.make_async_copy(source, target, landed.at[i])
        for i, (source, target) in enumerate(
            (
                (tok_hbm, tok), (gain_hbm, gain), (cache_hbm, cache),
                (rel_hbm, rel), (len_hbm, lengths), (map_hbm, prefix_map),
            )
        )
    ]
    copies = [
        pltpu.make_async_copy(w_hbm, held.at[kind], arrived.at[kind])
        for kind, w_hbm in enumerate((wq_hbm, wk_hbm, wv_hbm))
    ]
    for copy in first + copies:
        copy.start()
    for copy in first:
        copy.wait()
    normed = norm_rows(tok[...], gain[...])
    for part in range(PAIRS):
        for kind in range(2):
            for p in range(PREF_GRP):
                at = 3 * ROWS + (kind * PREF_GRP + p) * SHARE
                cut = slice(kind * D + part * LANES, kind * D + (part + 1) * LANES)
                out_ref[part, at : at + SHARE] = cache[p, :, cut]
    write_tables(
        place_ref, rel, lengths, prefix_map, near_ref, name_ref, asked_ref, line_ref, chosen_ref
    )
    for kind, copy in enumerate(copies):
        copy.wait()
        got = dot(normed, held[kind]).astype(jnp.bfloat16)
        for to in range(PAIRS):
            out_ref[to, kind * ROWS : (kind + 1) * ROWS] = got[:, to * LANES : (to + 1) * LANES]


def project(place, tokens, gain, prefix_cache, rel_bias, lengths, prefix_map, w_query, w_key, w_value):
    small = (tokens, gain.reshape(1, D), prefix_cache, rel_bias.T, lengths, prefix_map)
    out_shape = (
        pltpu.VMEM((PAIRS, SENT, LANES), jnp.bfloat16),
        pltpu.VMEM((3 * ROWS, 2 * ROWS), jnp.float32),
        pltpu.VMEM((PAIRS + 2, ROWS, LANES), jnp.bfloat16),
        pltpu.VMEM((PAIRS, 8, ROWS), jnp.float32),
        pltpu.VMEM((2, 8, LANES), jnp.float32),
        pltpu.VMEM((PAIRS, ROWS, ROWS), jnp.bfloat16),
    )
    blocks, *made = pl.pallas_call(
        project_kernel,
        in_specs=[SMEM_SPEC] * 3 + [HBM_SPEC] * 9,
        out_specs=(VMEM_SPEC,) * 6,
        out_shape=out_shape,
        scratch_shapes=[pltpu.VMEM(value.shape, value.dtype) for value in small]
        + [
            pltpu.VMEM((3, D, D), jnp.bfloat16),
            pltpu.SemaphoreType.DMA((3,)),
            pltpu.SemaphoreType.DMA((6,)),
        ],
        compiler_params=pltpu.CompilerParams(vmem_limit_bytes=VMEM_LIMIT),
        cost_estimate=COST,
        name="project",
    )(*place, *off_chip(*small, w_query, w_key, w_value))
    return blocks, made


def spread_kernel(got_ref, tok_ref, *rest):
    up_ref, down_ref, far_ref, same_ref = rest[-4:]
    for source in range(PAIRS):
        rows = slice(source * 4 * SHARE, (source + 1) * 4 * SHARE)
        held = got_ref[source, 3 * ROWS :]
        up_ref[rows] = held
        down_ref[rows] = held
        far_ref[rows] = held
    up_ref[QUARTER:] = got_ref[PAIRS - 1, ROWS : 3 * ROWS]
    down_ref[QUARTER:] = got_ref[0, ROWS : 3 * ROWS]
    same_ref[...] = tok_ref[...]


def spread(got, tokens, on, off):
    shape = pltpu.VMEM((QUARTER + 2 * ROWS, LANES), jnp.bfloat16)
    return pl.pallas_call(
        spread_kernel,
        in_specs=[VMEM_SPEC] * 3 + [HBM_SPEC],
        out_specs=(VMEM_SPEC,) * 4,
        out_shape=(
            shape,
            shape,
            pltpu.VMEM((QUARTER, LANES), jnp.bfloat16),
            pltpu.VMEM((ROWS, D), jnp.bfloat16),
        ),
        compiler_params=pltpu.CompilerParams(vmem_limit_bytes=VMEM_LIMIT),
        cost_estimate=COST,
        name="spread",
    )(*on_chip(got, tokens, on), *off_chip(off))


def queries(got_ref, chosen_ref, step):
    query = jnp.transpose(got_ref[step, 0:ROWS])
    zero = jnp.zeros((DK, ROWS), jnp.bfloat16)
    stacked = jnp.concatenate(
        [jnp.concatenate([query[:DK], zero], axis=0), jnp.concatenate([zero, query[DK:]], axis=0)], axis=1
    )
    chosen = jnp.concatenate([chosen_ref[step], chosen_ref[step]], axis=1)
    return stacked, jnp.concatenate([stacked * (1 - chosen), stacked * chosen], axis=0)


def masked(scores, name_ref, block, asked_ref, step, bias):
    mine = name_ref[block].astype(jnp.float32) == asked_ref[step, 0:1]
    mine = jnp.concatenate([mine, mine], axis=1)
    return jnp.where(mine, scores + bias, masked_score)


def far_bias(place_ref, rel_ref):
    lane = lax.broadcasted_iota(jnp.int32, (1, 2 * ROWS), 1)
    head = place_ref[1] * 2
    return jnp.where(lane < ROWS, rel_ref[head, 15], rel_ref[head + 1, 15])


def own_head(values):
    return jnp.concatenate([values[:DK, :ROWS], values[DK:, ROWS:]], axis=0)


def by_feature(line):
    return jnp.concatenate(
        [jnp.broadcast_to(line[:, :ROWS], (DK, ROWS)), jnp.broadcast_to(line[:, ROWS:], (DK, ROWS))], axis=0
    )


def select(asked_ref, step, far_out):
    second = jnp.broadcast_to(asked_ref[step, 2:3], (LANES, ROWS)) > 0.5
    return jnp.where(second, own_head(far_out[LANES:]), own_head(far_out[:LANES]))


def quarter_of(rows_at, keys_ref, values_ref):
    for p in range(PREF_GRP):
        pieces = [
            jnp.concatenate(
                [rows_at(source, (kind * PREF_GRP + p) * SHARE) for source in range(PAIRS)], axis=0
            )
            for kind in range(2)
        ]
        keys_ref[:, p * LANES : (p + 1) * LANES] = pieces[0]
        values_ref[p * LANES : (p + 1) * LANES, :] = jnp.transpose(pieces[1])


def start_copies(pairs, landed):
    copies = [pltpu.make_async_copy(a, b, landed.at[i]) for i, (a, b) in enumerate(pairs)]
    for copy in copies:
        copy.start()
    return copies


def own_kernel(
    x_ref, pair_ref, side_ref, rel_ref, got_ref, near_ref, name_ref, asked_ref, line_ref, chosen_ref, in_two, out_hbm, in_hbm,
    stat_ref, acc_ref, tail_ref, split_ref, out_two, turned_one, turned_two,
    keys, values, kwin, vwin, in_one, landed,
):
    place_ref = (x_ref[0], pair_ref[0], side_ref[0])
    copies = start_copies(((out_hbm, out_two), (in_hbm, in_one)), landed)
    for b in (0, PAIRS + 1):
        kwin[b] = jnp.zeros((ROWS, LANES), jnp.bfloat16)
        vwin[b] = jnp.zeros((LANES, ROWS), jnp.bfloat16)
    for b in range(PAIRS):
        kwin[b + 1] = got_ref[b, ROWS : 2 * ROWS]
        vwin[b + 1] = jnp.transpose(got_ref[b, 2 * ROWS : 3 * ROWS])
    quarter_of(lambda s, at: got_ref[s, 3 * ROWS + at : 3 * ROWS + at + SHARE], keys, values)
    is_last = place_ref[0] == 3
    full = far_bias(place_ref, rel_ref)

    row = lax.broadcasted_iota(jnp.int32, (ROWS, LANES), 0)
    lines = [jnp.broadcast_to(line_ref[h, 0:1], (ROWS, LANES)) for h in range(2)]

    def one(step, _):
        offset = jnp.broadcast_to(asked_ref[step, 1:2], (ROWS, LANES)).astype(jnp.int32)
        at = jnp.minimum(ROWS - row + offset, LANES - 1)
        tail = jnp.concatenate([jnp.take_along_axis(line, at, axis=1) for line in lines], axis=1)
        tail_ref[step] = tail
        stacked, split = queries(got_ref, chosen_ref, step)
        split_ref[step] = split
        parts = [dot(keys[...], split) + jnp.where(is_last, tail, full)]
        near_scores = dot(kwin[pl.ds(step, 3)].reshape(3 * ROWS, LANES), stacked)
        for b in range(3):
            at_edge = (step + b == 0) | (step + b == PAIRS + 1)
            cut = slice(b * ROWS, (b + 1) * ROWS)
            bias = near_ref[cut] + jnp.where(at_edge, masked_score, 0.0)
            parts.append(masked(near_scores[cut], name_ref, step + b, asked_ref, step, bias))
        top = jnp.max(functools.reduce(jnp.maximum, parts), axis=0, keepdims=True)
        terms = [jnp.exp(part - top) for part in parts]
        row_sum = jnp.sum(functools.reduce(jnp.add, terms), axis=0, keepdims=True)
        weights = [t.astype(jnp.bfloat16) for t in terms]
        near_values = jnp.concatenate([vwin[step + b] for b in range(3)], axis=1)
        near_out = dot(near_values, jnp.concatenate(weights[1:], axis=0))
        acc_ref[step] = select(asked_ref, step, dot(values[...], weights[0])) + own_head(near_out)
        stat_ref[step, 0:1] = top
        stat_ref[step, 1:2] = row_sum
        return 0

    lax.fori_loop(0, PAIRS, one, 0, unroll=4)
    for copy in copies:
        copy.wait()
    for source, target in ((in_two, turned_two), (in_one, turned_one)):
        for at in range(0, D, LANES):
            target[:, at : at + LANES] = jnp.transpose(source[at : at + LANES])


def attend_own(place, rel_bias, got, made, in_one, in_two, out_two):
    return pl.pallas_call(
        own_kernel,
        in_specs=[SMEM_SPEC] * 4 + [VMEM_SPEC] * 7 + [HBM_SPEC] * 2,
        out_specs=(VMEM_SPEC,) * 7,
        out_shape=(
            pltpu.VMEM((PAIRS, 8, 2 * ROWS), jnp.float32),
            pltpu.VMEM((PAIRS, LANES, ROWS), jnp.float32),
            pltpu.VMEM((PAIRS, ROWS, 2 * ROWS), jnp.float32),
            pltpu.VMEM((PAIRS, PREF_GRP * LANES, 2 * ROWS), jnp.bfloat16),
        )
        + (pltpu.VMEM((D, D), jnp.bfloat16),) * 3,
        scratch_shapes=[
            pltpu.VMEM((PLEN // 4, PREF_GRP * LANES), jnp.bfloat16),
            pltpu.VMEM((PREF_GRP * LANES, PLEN // 4), jnp.bfloat16),
            pltpu.VMEM((PAIRS + 2, ROWS, LANES), jnp.bfloat16),
            pltpu.VMEM((PAIRS + 2, LANES, ROWS), jnp.bfloat16),
            pltpu.VMEM((D, D), jnp.bfloat16),
            pltpu.SemaphoreType.DMA((2,)),
        ],
        compiler_params=pltpu.CompilerParams(vmem_limit_bytes=VMEM_LIMIT),
        cost_estimate=COST,
        name="attend_own",
    )(*place, rel_bias.T, *on_chip(got, *made, in_two), *off_chip(out_two, in_one))


def rest_kernel(
    x_ref, pair_ref, side_ref, rel_ref, prev_ref, next_ref, far_ref, near_ref, name_ref, asked_ref,
    stat_ref, acc_ref, tail_ref, split_ref, _, out_ref, keys, values, kwin, vwin,
):
    place_ref = (x_ref[0], pair_ref[0], side_ref[0])
    turns = ((3, prev_ref), (1, next_ref), (2, far_ref))
    for i, (_, ref) in enumerate(turns):
        quarter_of(
            lambda s, at, ref=ref: ref[s * 4 * SHARE + at : s * 4 * SHARE + at + SHARE], keys.at[i], values.at[i]
        )
    for i, ref in enumerate((prev_ref, next_ref)):
        kwin[i] = ref[QUARTER : QUARTER + ROWS]
        vwin[i] = jnp.transpose(ref[QUARTER + ROWS :])
    is_last = [lax.rem(place_ref[0] + turn, 4) == 3 for turn, _ in turns]
    side = place_ref[2]
    full = far_bias(place_ref, rel_ref)

    def one(step, edge=None):
        split = split_ref[step]
        tail = tail_ref[step]
        scores = dot(keys[...].reshape(3 * PLEN // 4, PREF_GRP * LANES), split)
        parts = [
            scores[i * ROWS : (i + 1) * ROWS] + jnp.where(is_last[i], tail, full) for i in range(3)
        ]
        if edge is not None:
            bias = near_ref[edge * 2 * ROWS : (edge * 2 + 1) * ROWS]
            parts.append(
                masked(dot(kwin[edge], split[:LANES] + split[LANES:]), name_ref, edge * (PAIRS + 1), asked_ref, step, bias)
            )
        before = stat_ref[step, 0:1]
        top = jnp.max(functools.reduce(jnp.maximum, parts), axis=0, keepdims=True)
        top = jnp.maximum(top, before)
        shrink = jnp.exp(before - top)
        terms = [jnp.exp(part - top) for part in parts]
        row_sum = jnp.sum(functools.reduce(jnp.add, terms), axis=0, keepdims=True)
        row_sum = row_sum + stat_ref[step, 1:2] * shrink
        weights = [t.astype(jnp.bfloat16) for t in terms]
        far_values = jnp.concatenate([values[i] for i in range(3)], axis=1)
        far_out = dot(far_values, jnp.concatenate(weights[:3], axis=0))
        acc = acc_ref[step] * by_feature(shrink) + select(asked_ref, step, far_out)
        if edge is not None:
            acc = acc + own_head(dot(vwin[edge], weights[3]))
        done = jnp.transpose(acc * by_feature(1.0 / row_sum)).astype(jnp.bfloat16)
        out_ref[side * PAIRS + step] = done
        out_ref[(1 - side) * PAIRS + jnp.bitwise_xor(step, 1)] = done

    def middle(step, _):
        one(step)
        return 0

    one(jnp.int32(0), 0)
    lax.fori_loop(1, PAIRS - 1, middle, 0, unroll=PAIRS - 2)
    one(jnp.int32(PAIRS - 1), 1)


def attend_rest(place, rel_bias, prev, after_it, far, made, part, ready):
    return pl.pallas_call(
        rest_kernel,
        in_specs=[SMEM_SPEC] * 4 + [VMEM_SPEC] * 11,
        out_specs=VMEM_SPEC,
        out_shape=pltpu.VMEM((2 * PAIRS, ROWS, LANES), jnp.bfloat16),
        scratch_shapes=[
            pltpu.VMEM((3, PLEN // 4, PREF_GRP * LANES), jnp.bfloat16),
            pltpu.VMEM((3, PREF_GRP * LANES, PLEN // 4), jnp.bfloat16),
            pltpu.VMEM((2, ROWS, LANES), jnp.bfloat16),
            pltpu.VMEM((2, LANES, ROWS), jnp.bfloat16),
        ],
        compiler_params=pltpu.CompilerParams(vmem_limit_bytes=VMEM_LIMIT),
        cost_estimate=COST,
        name="attend_rest",
    )(*place, rel_bias.T, *on_chip(prev, after_it, far, *made[:3], *part, ready))


def join(side, att_ref, w_ref, tok_ref):
    attended = jnp.concatenate([att_ref[side * PAIRS + j] for j in range(PAIRS)], axis=1)
    return (tok_ref[...].astype(jnp.float32) + dot(attended, w_ref[...])).astype(jnp.bfloat16)


def units_of(normed, in_ref):
    return jnp.maximum(dot(normed, in_ref[...]), 0.0).astype(jnp.bfloat16)


def finish_kernel(side_ref, att_ref, w_ref, tok_ref, gain_ref, in_one, in_two, out_one, out_two, *rest):
    hidden = join(side_ref[0], att_ref, w_ref, tok_ref)
    normed = norm_rows(hidden, gain_ref[...])
    got = hidden.astype(jnp.float32)
    for in_ref, out_w_ref in ((in_one, out_one), (in_two, out_two)):
        got = got + dot(units_of(normed, in_ref), out_w_ref[...])
    rest[-1][...] = got


def finish(side, att, w_attn_out, tokens, gain, weights, *ready):
    return pl.pallas_call(
        finish_kernel,
        in_specs=[SMEM_SPEC] + [VMEM_SPEC] * (8 + len(ready)),
        out_specs=VMEM_SPEC,
        out_shape=pltpu.VMEM((ROWS, D), jnp.float32),
        compiler_params=pltpu.CompilerParams(vmem_limit_bytes=VMEM_LIMIT),
        cost_estimate=COST,
        name="finish",
    )(side, *on_chip(att, w_attn_out, tokens, gain.reshape(1, D), *weights, *ready))


def away_kernel(
    side_ref, att_ref, w_ref, tok_ref, gain_ref, in_one, in_two, out_one, out_two, half_ref, units_ref
):
    hidden = join(1 - side_ref[0], att_ref, w_ref, tok_ref)
    normed = norm_rows(hidden, gain_ref[...])
    units_ref[0] = units_of(normed, in_one)
    units_ref[1] = units_of(normed, in_two)
    got = dot(units_ref[0], out_one[:, :FIRST]) + dot(units_ref[1], out_two[:, :FIRST])
    half_ref[...] = got.astype(half_ref.dtype)


def away(side, att, w_attn_out, tokens, gain, weights):
    return pl.pallas_call(
        away_kernel,
        in_specs=[SMEM_SPEC] + [VMEM_SPEC] * 8,
        out_specs=(VMEM_SPEC,) * 2,
        out_shape=(pltpu.VMEM((ROWS, FIRST), jnp.bfloat16), pltpu.VMEM((2, ROWS, D), jnp.bfloat16)),
        compiler_params=pltpu.CompilerParams(vmem_limit_bytes=VMEM_LIMIT),
        cost_estimate=COST,
        name="away",
    )(side, *on_chip(att, w_attn_out, tokens, gain.reshape(1, D), *weights))


def remainder_kernel(units_ref, out_one, out_two, half_ref):
    got = dot(units_ref[0], out_one[:, FIRST:]) + dot(units_ref[1], out_two[:, FIRST:])
    half_ref[...] = got.astype(half_ref.dtype)


def remainder(units, out_one, out_two):
    return pl.pallas_call(
        remainder_kernel,
        in_specs=[VMEM_SPEC] * 3,
        out_specs=VMEM_SPEC,
        out_shape=pltpu.VMEM((ROWS, D - FIRST), jnp.bfloat16),
        compiler_params=pltpu.CompilerParams(vmem_limit_bytes=VMEM_LIMIT),
        cost_estimate=COST,
        name="remainder",
    )(*on_chip(units, out_one, out_two))


def total_kernel(home_ref, first_ref, second_ref, out_ref):
    for cut, ref in ((slice(0, FIRST), first_ref), (slice(FIRST, D), second_ref)):
        out_ref[:, cut] = (home_ref[:, cut] + ref[...].astype(jnp.float32)).astype(jnp.bfloat16)


def total(home, first, second):
    return pl.pallas_call(
        total_kernel,
        in_specs=[VMEM_SPEC] * 3,
        out_specs=VMEM_SPEC,
        out_shape=jax.ShapeDtypeStruct((ROWS, D), jnp.bfloat16),
        compiler_params=pltpu.CompilerParams(vmem_limit_bytes=VMEM_LIMIT),
        cost_estimate=COST,
        name="total",
    )(*on_chip(home, first, second))


def body(
    tokens,
    attn_gain,
    w_query,
    w_key,
    w_value,
    w_attn_out,
    rel_bias,
    prefix_cache,
    lengths,
    prefix_map,
    mlp_gain,
    w_in,
    w_out,
):
    count_x = lax.axis_size("x")
    plane = lax.axis_index("z") * 2 + lax.axis_index("ylo")
    place = tuple(
        at.astype(jnp.int32).reshape(1) for at in (lax.axis_index("x"), plane, lax.axis_index("yhi"))
    )
    other_in = lax.ppermute(w_in, "core", SWAP)
    other_out = lax.ppermute(w_out, "core", SWAP)
    blocks, made = project(
        place, tokens, attn_gain, prefix_cache, rel_bias, lengths, prefix_map, w_query, w_key, w_value
    )
    got = lax.all_to_all(blocks, PLANE, 0, 0, tiled=True)
    mirrored = ("yhi", "ylo")
    up, down, far, same = spread(got, tokens, other_in, other_out)
    by = lambda d: [(i, (i + d) % count_x) for i in range(count_x)]
    opposite = lax.ppermute(far, "x", by(2))
    prev = lax.ppermute(up, "x", by(1))
    later = lax.ppermute(down, "x", by(-1))
    far_tokens = lax.ppermute(same, mirrored, MIRROR)
    *part, other_out, turned, other_turned = attend_own(
        place, rel_bias, got, made, w_in, other_in, other_out
    )
    mixed = attend_rest(place, rel_bias, prev, later, opposite, made, part, far_tokens)
    weights = (turned, other_turned, w_out, other_out)
    att = lax.all_to_all(mixed, ("yhi",) + PLANE, 0, 0, tiled=True)

    first, units = away(place[2], att, w_attn_out, far_tokens, mlp_gain, weights)
    first_back = lax.ppermute(first, mirrored, MIRROR)
    second = remainder(units, *weights[2:])
    second_back = lax.ppermute(second, mirrored, MIRROR)
    local = finish(place[2], att, w_attn_out, tokens, mlp_gain, weights, second)
    return total(local, first_back, second_back)


def solution(mesh):
    split = Mesh(mesh.devices.reshape(2, 2, 4, 4, 2), AXES)
    grp, req = ("yhi", "core"), REQ
    return jax.shard_map(
        body,
        mesh=split,
        in_specs=(
            P(grp + req, None),
            P(),
            P(),
            P(),
            P(),
            P(),
            P(),
            P(grp, req, None),
            P(grp, None),
            P(grp, None),
            P(),
            P(grp, None),
            P(grp, None),
        ),
        out_specs=P(grp + req, None),
        check_vma=False,
    )
```

```python
import functools

import jax
import jax.numpy as jnp
from jax import lax
from jax.experimental import pallas as pl
from jax.experimental.pallas import tpu as pltpu
from jax.sharding import Mesh, PartitionSpec as P

D = 1024
H = 16
DK = 64
PLEN = 512
PREF_GRP = 2
ROWS = 128
PAIRS = 8
LANES = 128
FIRST = 640
SHARE = 16
SENT = 3 * ROWS + 2 * PREF_GRP * SHARE
QUARTER = PAIRS * 2 * PREF_GRP * SHARE

epsilon = 1e-06
far_marks = (12, 16, 23, 32, 46, 64, 91)
masked_score = -1e30
VMEM_LIMIT = 16 * 1024 * 1024
COST = pl.CostEstimate(flops=1000, transcendentals=0, bytes_accessed=1000)

AXES = ("yhi", "core", "x", "z", "ylo")
REQ = ("x", "z", "ylo")
PLANE = ("z", "ylo")
MIRROR = [(0, 3), (3, 0), (1, 2), (2, 1)]
SWAP = [(0, 1), (1, 0)]


def norm_rows(values_in, gain):
    widened = values_in.astype(jnp.float32)
    scale = lax.rsqrt(jnp.mean(widened * widened, axis=-1, keepdims=True) + epsilon)
    return (widened * scale * gain).astype(jnp.bfloat16)


def dot(a, b):
    return jnp.dot(a, b, preferred_element_type=jnp.float32)


def on_chip(*arrays):
    return tuple(pltpu.with_memory_space_constraint(a, pltpu.VMEM) for a in arrays)


def off_chip(*arrays):
    return tuple(pltpu.with_memory_space_constraint(a, pltpu.HBM) for a in arrays)


VMEM_SPEC = pl.BlockSpec(memory_space=pltpu.VMEM)
HBM_SPEC = pl.BlockSpec(memory_space=pltpu.HBM)
SMEM_SPEC = pl.BlockSpec(memory_space=pltpu.SMEM)


def bias_line(rel_ref, head, first_bucket):
    lane = lax.broadcasted_iota(jnp.int32, (8, LANES), 1)

    def of(bucket):
        return rel_ref[pl.ds(head, 1), first_bucket + bucket : first_bucket + bucket + 1]

    line = jnp.broadcast_to(of(0), (8, LANES))
    for bucket in range(1, 16):
        mark = bucket if bucket <= 8 else far_marks[bucket - 9]
        line = jnp.where(lane >= mark, of(bucket), line)
    return jnp.broadcast_to(line[0:1], (ROWS, LANES))


def write_tables(
    place_ref, rel_ref, len_ref, map_ref, near_ref, name_ref, asked_ref, line_ref, chosen_ref
):
    row = lax.broadcasted_iota(jnp.int32, (ROWS, LANES), 0)
    lane = lax.broadcasted_iota(jnp.int32, (ROWS, LANES), 1)
    for h in range(2):
        head = place_ref[1] * 2 + h
        before = bias_line(rel_ref, head, 0)
        after_it = bias_line(rel_ref, head, 16)

        def pick(line, distance):
            return jnp.take_along_axis(line, jnp.clip(distance, 0, LANES - 1), axis=1)

        cut = slice(h * ROWS, (h + 1) * ROWS)
        near_ref[0:ROWS, cut] = pick(before, lane + ROWS - row)
        near_ref[ROWS : 2 * ROWS, cut] = jnp.where(
            row > lane, pick(after_it, row - lane), pick(before, lane - row)
        )
        near_ref[2 * ROWS : 3 * ROWS, cut] = pick(after_it, row + ROWS - lane)
        line_ref[h] = before[:8]

    requests = len_ref.shape[1]
    down_it = lax.broadcasted_iota(jnp.int32, (requests, requests), 0)
    along = lax.broadcasted_iota(jnp.int32, (requests, requests), 1)
    length = jnp.broadcast_to(len_ref[...], (requests, requests)).astype(jnp.float32)
    prefix = jnp.broadcast_to(map_ref[...], (requests, requests)).astype(jnp.float32)

    def column(keep, values):
        return jnp.sum(jnp.where(keep, values, 0.0), axis=1, keepdims=True)

    starts = column(along < down_it, length)
    ends = column(along <= down_it, length)
    prefixes = column(along == down_it, prefix)
    number = lax.broadcasted_iota(jnp.int32, (requests, LANES), 0).astype(jnp.float32) + 1.0
    first = place_ref[0] * (PAIRS * ROWS) - ROWS
    for b in range(PAIRS + 2):
        ids = lax.broadcasted_iota(jnp.int32, (requests, LANES), 1) + (first + b * ROWS)
        ids = ids.astype(jnp.float32)
        member = (ids >= starts) & (ids < ends)
        request = jnp.sum(jnp.where(member, number, 0.0), axis=0, keepdims=True) - 1.0
        offset = ids[0:1] - jnp.sum(jnp.where(member, starts, 0.0), axis=0, keepdims=True)
        chosen = jnp.sum(jnp.where(member, prefixes, 0.0), axis=0, keepdims=True)
        facts = jnp.concatenate([request, offset, chosen] + [request] * 5, axis=0)
        name_ref[b] = jnp.broadcast_to(jnp.transpose(facts)[:, 0:1], (ROWS, LANES)).astype(jnp.bfloat16)
        if 0 < b < PAIRS + 1:
            step = b - 1
            asked_ref[step] = facts
            chosen_ref[step] = jnp.broadcast_to(chosen, (ROWS, LANES)).astype(jnp.bfloat16)


def project_kernel(
    x_ref, pair_ref, side_ref, tok_hbm, gain_hbm, cache_hbm, rel_hbm, len_hbm, map_hbm, wq_hbm, wk_hbm, wv_hbm,
    out_ref, near_ref, name_ref, asked_ref, line_ref, chosen_ref,
    tok, gain, cache, rel, lengths, prefix_map, held, arrived, landed,
):
    place_ref = (x_ref[0], pair_ref[0], side_ref[0])
    first = [
        pltpu.make_async_copy(source, target, landed.at[i])
        for i, (source, target) in enumerate(
            (
                (tok_hbm, tok), (gain_hbm, gain), (cache_hbm, cache),
                (rel_hbm, rel), (len_hbm, lengths), (map_hbm, prefix_map),
            )
        )
    ]
    copies = [
        pltpu.make_async_copy(w_hbm, held.at[kind], arrived.at[kind])
        for kind, w_hbm in enumerate((wq_hbm, wk_hbm, wv_hbm))
    ]
    for copy in first + copies:
        copy.start()
    for copy in first:
        copy.wait()
    normed = norm_rows(tok[...], gain[...])
    for part in range(PAIRS):
        for kind in range(2):
            for p in range(PREF_GRP):
                at = 3 * ROWS + (kind * PREF_GRP + p) * SHARE
                cut = slice(kind * D + part * LANES, kind * D + (part + 1) * LANES)
                out_ref[part, at : at + SHARE] = cache[p, :, cut]
    write_tables(
        place_ref, rel, lengths, prefix_map, near_ref, name_ref, asked_ref, line_ref, chosen_ref
    )
    for kind, copy in enumerate(copies):
        copy.wait()
        got = dot(normed, held[kind]).astype(jnp.bfloat16)
        for to in range(PAIRS):
            out_ref[to, kind * ROWS : (kind + 1) * ROWS] = got[:, to * LANES : (to + 1) * LANES]


def project(place, tokens, gain, prefix_cache, rel_bias, lengths, prefix_map, w_query, w_key, w_value):
    small = (tokens, gain.reshape(1, D), prefix_cache, rel_bias.T, lengths, prefix_map)
    out_shape = (
        pltpu.VMEM((PAIRS, SENT, LANES), jnp.bfloat16),
        pltpu.VMEM((3 * ROWS, 2 * ROWS), jnp.float32),
        pltpu.VMEM((PAIRS + 2, ROWS, LANES), jnp.bfloat16),
        pltpu.VMEM((PAIRS, 8, ROWS), jnp.float32),
        pltpu.VMEM((2, 8, LANES), jnp.float32),
        pltpu.VMEM((PAIRS, ROWS, ROWS), jnp.bfloat16),
    )
    blocks, *made = pl.pallas_call(
        project_kernel,
        in_specs=[SMEM_SPEC] * 3 + [HBM_SPEC] * 9,
        out_specs=(VMEM_SPEC,) * 6,
        out_shape=out_shape,
        scratch_shapes=[pltpu.VMEM(value.shape, value.dtype) for value in small]
        + [
            pltpu.VMEM((3, D, D), jnp.bfloat16),
            pltpu.SemaphoreType.DMA((3,)),
            pltpu.SemaphoreType.DMA((6,)),
        ],
        compiler_params=pltpu.CompilerParams(vmem_limit_bytes=VMEM_LIMIT),
        cost_estimate=COST,
        name="project",
    )(*place, *off_chip(*small, w_query, w_key, w_value))
    return blocks, made


def spread_kernel(got_ref, tok_ref, *rest):
    up_ref, down_ref, far_ref, same_ref = rest[-4:]
    for source in range(PAIRS):
        rows = slice(source * 4 * SHARE, (source + 1) * 4 * SHARE)
        held = got_ref[source, 3 * ROWS :]
        up_ref[rows] = held
        down_ref[rows] = held
        far_ref[rows] = held
    up_ref[QUARTER:] = got_ref[PAIRS - 1, ROWS : 3 * ROWS]
    down_ref[QUARTER:] = got_ref[0, ROWS : 3 * ROWS]
    same_ref[...] = tok_ref[...]


def spread(got, tokens, on, off):
    shape = pltpu.VMEM((QUARTER + 2 * ROWS, LANES), jnp.bfloat16)
    return pl.pallas_call(
        spread_kernel,
        in_specs=[VMEM_SPEC] * 3 + [HBM_SPEC],
        out_specs=(VMEM_SPEC,) * 4,
        out_shape=(
            shape,
            shape,
            pltpu.VMEM((QUARTER, LANES), jnp.bfloat16),
            pltpu.VMEM((ROWS, D), jnp.bfloat16),
        ),
        compiler_params=pltpu.CompilerParams(vmem_limit_bytes=VMEM_LIMIT),
        cost_estimate=COST,
        name="spread",
    )(*on_chip(got, tokens, on), *off_chip(off))


def queries(got_ref, chosen_ref, step):
    query = jnp.transpose(got_ref[step, 0:ROWS])
    zero = jnp.zeros((DK, ROWS), jnp.bfloat16)
    stacked = jnp.concatenate(
        [jnp.concatenate([query[:DK], zero], axis=0), jnp.concatenate([zero, query[DK:]], axis=0)], axis=1
    )
    chosen = jnp.concatenate([chosen_ref[step], chosen_ref[step]], axis=1)
    return stacked, jnp.concatenate([stacked * (1 - chosen), stacked * chosen], axis=0)


def masked(scores, name_ref, block, asked_ref, step, bias):
    mine = name_ref[block].astype(jnp.float32) == asked_ref[step, 0:1]
    mine = jnp.concatenate([mine, mine], axis=1)
    return jnp.where(mine, scores + bias, masked_score)


def far_bias(place_ref, rel_ref):
    lane = lax.broadcasted_iota(jnp.int32, (1, 2 * ROWS), 1)
    head = place_ref[1] * 2
    return jnp.where(lane < ROWS, rel_ref[head, 15], rel_ref[head + 1, 15])


def own_head(values):
    return jnp.concatenate([values[:DK, :ROWS], values[DK:, ROWS:]], axis=0)


def by_feature(line):
    return jnp.concatenate(
        [jnp.broadcast_to(line[:, :ROWS], (DK, ROWS)), jnp.broadcast_to(line[:, ROWS:], (DK, ROWS))], axis=0
    )


def select(asked_ref, step, far_out):
    second = jnp.broadcast_to(asked_ref[step, 2:3], (LANES, ROWS)) > 0.5
    return jnp.where(second, own_head(far_out[LANES:]), own_head(far_out[:LANES]))


def quarter_of(rows_at, keys_ref, values_ref):
    for p in range(PREF_GRP):
        pieces = [
            jnp.concatenate(
                [rows_at(source, (kind * PREF_GRP + p) * SHARE) for source in range(PAIRS)], axis=0
            )
            for kind in range(2)
        ]
        keys_ref[:, p * LANES : (p + 1) * LANES] = pieces[0]
        values_ref[p * LANES : (p + 1) * LANES, :] = jnp.transpose(pieces[1])


def start_copies(pairs, landed):
    copies = [pltpu.make_async_copy(a, b, landed.at[i]) for i, (a, b) in enumerate(pairs)]
    for copy in copies:
        copy.start()
    return copies


def own_kernel(
    x_ref, pair_ref, side_ref, rel_ref, got_ref, near_ref, name_ref, asked_ref, line_ref, chosen_ref, in_two, out_hbm, in_hbm,
    stat_ref, acc_ref, tail_ref, split_ref, out_two, turned_one, turned_two,
    keys, values, kwin, vwin, in_one, landed,
):
    place_ref = (x_ref[0], pair_ref[0], side_ref[0])
    copies = start_copies(((out_hbm, out_two), (in_hbm, in_one)), landed)
    for b in (0, PAIRS + 1):
        kwin[b] = jnp.zeros((ROWS, LANES), jnp.bfloat16)
        vwin[b] = jnp.zeros((LANES, ROWS), jnp.bfloat16)
    for b in range(PAIRS):
        kwin[b + 1] = got_ref[b, ROWS : 2 * ROWS]
        vwin[b + 1] = jnp.transpose(got_ref[b, 2 * ROWS : 3 * ROWS])
    quarter_of(lambda s, at: got_ref[s, 3 * ROWS + at : 3 * ROWS + at + SHARE], keys, values)
    is_last = place_ref[0] == 3
    full = far_bias(place_ref, rel_ref)

    row = lax.broadcasted_iota(jnp.int32, (ROWS, LANES), 0)
    lines = [jnp.broadcast_to(line_ref[h, 0:1], (ROWS, LANES)) for h in range(2)]

    def one(step, _):
        offset = jnp.broadcast_to(asked_ref[step, 1:2], (ROWS, LANES)).astype(jnp.int32)
        at = jnp.minimum(ROWS - row + offset, LANES - 1)
        tail = jnp.concatenate([jnp.take_along_axis(line, at, axis=1) for line in lines], axis=1)
        tail_ref[step] = tail
        stacked, split = queries(got_ref, chosen_ref, step)
        split_ref[step] = split
        parts = [dot(keys[...], split) + jnp.where(is_last, tail, full)]
        near_scores = dot(kwin[pl.ds(step, 3)].reshape(3 * ROWS, LANES), stacked)
        for b in range(3):
            at_edge = (step + b == 0) | (step + b == PAIRS + 1)
            cut = slice(b * ROWS, (b + 1) * ROWS)
            bias = near_ref[cut] + jnp.where(at_edge, masked_score, 0.0)
            parts.append(masked(near_scores[cut], name_ref, step + b, asked_ref, step, bias))
        top = jnp.max(functools.reduce(jnp.maximum, parts), axis=0, keepdims=True)
        terms = [jnp.exp(part - top) for part in parts]
        row_sum = jnp.sum(functools.reduce(jnp.add, terms), axis=0, keepdims=True)
        weights = [t.astype(jnp.bfloat16) for t in terms]
        near_values = jnp.concatenate([vwin[step + b] for b in range(3)], axis=1)
        near_out = dot(near_values, jnp.concatenate(weights[1:], axis=0))
        acc_ref[step] = select(asked_ref, step, dot(values[...], weights[0])) + own_head(near_out)
        stat_ref[step, 0:1] = top
        stat_ref[step, 1:2] = row_sum
        strip = pl.ds(pl.multiple_of(step * LANES, LANES), LANES)
        turned_two[:, strip] = jnp.transpose(in_two[strip])
        return 0

    lax.fori_loop(0, PAIRS, one, 0, unroll=4)
    for copy in copies:
        copy.wait()
    for at in range(0, D, LANES):
        turned_one[:, at : at + LANES] = jnp.transpose(in_one[at : at + LANES])


def attend_own(place, rel_bias, got, made, in_one, in_two, out_two):
    return pl.pallas_call(
        own_kernel,
        in_specs=[SMEM_SPEC] * 4 + [VMEM_SPEC] * 7 + [HBM_SPEC] * 2,
        out_specs=(VMEM_SPEC,) * 7,
        out_shape=(
            pltpu.VMEM((PAIRS, 8, 2 * ROWS), jnp.float32),
            pltpu.VMEM((PAIRS, LANES, ROWS), jnp.float32),
            pltpu.VMEM((PAIRS, ROWS, 2 * ROWS), jnp.float32),
            pltpu.VMEM((PAIRS, PREF_GRP * LANES, 2 * ROWS), jnp.bfloat16),
        )
        + (pltpu.VMEM((D, D), jnp.bfloat16),) * 3,
        scratch_shapes=[
            pltpu.VMEM((PLEN // 4, PREF_GRP * LANES), jnp.bfloat16),
            pltpu.VMEM((PREF_GRP * LANES, PLEN // 4), jnp.bfloat16),
            pltpu.VMEM((PAIRS + 2, ROWS, LANES), jnp.bfloat16),
            pltpu.VMEM((PAIRS + 2, LANES, ROWS), jnp.bfloat16),
            pltpu.VMEM((D, D), jnp.bfloat16),
            pltpu.SemaphoreType.DMA((2,)),
        ],
        compiler_params=pltpu.CompilerParams(vmem_limit_bytes=VMEM_LIMIT),
        cost_estimate=COST,
        name="attend_own",
    )(*place, rel_bias.T, *on_chip(got, *made, in_two), *off_chip(out_two, in_one))


def rest_kernel(
    x_ref, pair_ref, side_ref, rel_ref, prev_ref, next_ref, far_ref, near_ref, name_ref, asked_ref,
    stat_ref, acc_ref, tail_ref, split_ref, _, out_ref, keys, values, kwin, vwin,
):
    place_ref = (x_ref[0], pair_ref[0], side_ref[0])
    turns = ((3, prev_ref), (1, next_ref), (2, far_ref))
    for i, (_, ref) in enumerate(turns):
        quarter_of(
            lambda s, at, ref=ref: ref[s * 4 * SHARE + at : s * 4 * SHARE + at + SHARE], keys.at[i], values.at[i]
        )
    for i, ref in enumerate((prev_ref, next_ref)):
        kwin[i] = ref[QUARTER : QUARTER + ROWS]
        vwin[i] = jnp.transpose(ref[QUARTER + ROWS :])
    is_last = [lax.rem(place_ref[0] + turn, 4) == 3 for turn, _ in turns]
    side = place_ref[2]
    full = far_bias(place_ref, rel_ref)

    def one(step, edge=None):
        split = split_ref[step]
        tail = tail_ref[step]
        scores = dot(keys[...].reshape(3 * PLEN // 4, PREF_GRP * LANES), split)
        parts = [
            scores[i * ROWS : (i + 1) * ROWS] + jnp.where(is_last[i], tail, full) for i in range(3)
        ]
        if edge is not None:
            bias = near_ref[edge * 2 * ROWS : (edge * 2 + 1) * ROWS]
            parts.append(
                masked(dot(kwin[edge], split[:LANES] + split[LANES:]), name_ref, edge * (PAIRS + 1), asked_ref, step, bias)
            )
        before = stat_ref[step, 0:1]
        top = jnp.max(functools.reduce(jnp.maximum, parts), axis=0, keepdims=True)
        top = jnp.maximum(top, before)
        shrink = jnp.exp(before - top)
        terms = [jnp.exp(part - top) for part in parts]
        row_sum = jnp.sum(functools.reduce(jnp.add, terms), axis=0, keepdims=True)
        row_sum = row_sum + stat_ref[step, 1:2] * shrink
        weights = [t.astype(jnp.bfloat16) for t in terms]
        far_values = jnp.concatenate([values[i] for i in range(3)], axis=1)
        far_out = dot(far_values, jnp.concatenate(weights[:3], axis=0))
        acc = acc_ref[step] * by_feature(shrink) + select(asked_ref, step, far_out)
        if edge is not None:
            acc = acc + own_head(dot(vwin[edge], weights[3]))
        done = jnp.transpose(acc * by_feature(1.0 / row_sum)).astype(jnp.bfloat16)
        out_ref[side * PAIRS + step] = done
        out_ref[(1 - side) * PAIRS + jnp.bitwise_xor(step, 1)] = done

    def middle(step, _):
        one(step)
        return 0

    one(jnp.int32(0), 0)
    lax.fori_loop(1, PAIRS - 1, middle, 0, unroll=PAIRS - 2)
    one(jnp.int32(PAIRS - 1), 1)


def attend_rest(place, rel_bias, prev, after_it, far, made, part, ready):
    return pl.pallas_call(
        rest_kernel,
        in_specs=[SMEM_SPEC] * 4 + [VMEM_SPEC] * 11,
        out_specs=VMEM_SPEC,
        out_shape=pltpu.VMEM((2 * PAIRS, ROWS, LANES), jnp.bfloat16),
        scratch_shapes=[
            pltpu.VMEM((3, PLEN // 4, PREF_GRP * LANES), jnp.bfloat16),
            pltpu.VMEM((3, PREF_GRP * LANES, PLEN // 4), jnp.bfloat16),
            pltpu.VMEM((2, ROWS, LANES), jnp.bfloat16),
            pltpu.VMEM((2, LANES, ROWS), jnp.bfloat16),
        ],
        compiler_params=pltpu.CompilerParams(vmem_limit_bytes=VMEM_LIMIT),
        cost_estimate=COST,
        name="attend_rest",
    )(*place, rel_bias.T, *on_chip(prev, after_it, far, *made[:3], *part, ready))


def join(side, att_ref, w_ref, tok_ref):
    attended = jnp.concatenate([att_ref[side * PAIRS + j] for j in range(PAIRS)], axis=1)
    return (tok_ref[...].astype(jnp.float32) + dot(attended, w_ref[...])).astype(jnp.bfloat16)


def units_of(normed, in_ref):
    return jnp.maximum(dot(normed, in_ref[...]), 0.0).astype(jnp.bfloat16)


def finish_kernel(side_ref, att_ref, w_ref, tok_ref, gain_ref, in_one, in_two, out_one, out_two, *rest):
    hidden = join(side_ref[0], att_ref, w_ref, tok_ref)
    normed = norm_rows(hidden, gain_ref[...])
    got = hidden.astype(jnp.float32)
    for in_ref, out_w_ref in ((in_one, out_one), (in_two, out_two)):
        got = got + dot(units_of(normed, in_ref), out_w_ref[...])
    rest[-1][...] = got


def finish(side, att, w_attn_out, tokens, gain, weights, *ready):
    return pl.pallas_call(
        finish_kernel,
        in_specs=[SMEM_SPEC] + [VMEM_SPEC] * (8 + len(ready)),
        out_specs=VMEM_SPEC,
        out_shape=pltpu.VMEM((ROWS, D), jnp.float32),
        compiler_params=pltpu.CompilerParams(vmem_limit_bytes=VMEM_LIMIT),
        cost_estimate=COST,
        name="finish",
    )(side, *on_chip(att, w_attn_out, tokens, gain.reshape(1, D), *weights, *ready))


def away_kernel(
    side_ref, att_ref, w_ref, tok_ref, gain_ref, in_one, in_two, out_one, out_two, half_ref, units_ref
):
    hidden = join(1 - side_ref[0], att_ref, w_ref, tok_ref)
    normed = norm_rows(hidden, gain_ref[...])
    units_ref[0] = units_of(normed, in_one)
    units_ref[1] = units_of(normed, in_two)
    got = dot(units_ref[0], out_one[:, :FIRST]) + dot(units_ref[1], out_two[:, :FIRST])
    half_ref[...] = got.astype(half_ref.dtype)


def away(side, att, w_attn_out, tokens, gain, weights):
    return pl.pallas_call(
        away_kernel,
        in_specs=[SMEM_SPEC] + [VMEM_SPEC] * 8,
        out_specs=(VMEM_SPEC,) * 2,
        out_shape=(pltpu.VMEM((ROWS, FIRST), jnp.bfloat16), pltpu.VMEM((2, ROWS, D), jnp.bfloat16)),
        compiler_params=pltpu.CompilerParams(vmem_limit_bytes=VMEM_LIMIT),
        cost_estimate=COST,
        name="away",
    )(side, *on_chip(att, w_attn_out, tokens, gain.reshape(1, D), *weights))


def remainder_kernel(units_ref, out_one, out_two, half_ref):
    got = dot(units_ref[0], out_one[:, FIRST:]) + dot(units_ref[1], out_two[:, FIRST:])
    half_ref[...] = got.astype(half_ref.dtype)


def remainder(units, out_one, out_two):
    return pl.pallas_call(
        remainder_kernel,
        in_specs=[VMEM_SPEC] * 3,
        out_specs=VMEM_SPEC,
        out_shape=pltpu.VMEM((ROWS, D - FIRST), jnp.bfloat16),
        compiler_params=pltpu.CompilerParams(vmem_limit_bytes=VMEM_LIMIT),
        cost_estimate=COST,
        name="remainder",
    )(*on_chip(units, out_one, out_two))


def total_kernel(home_ref, first_ref, second_ref, out_ref):
    for cut, ref in ((slice(0, FIRST), first_ref), (slice(FIRST, D), second_ref)):
        out_ref[:, cut] = (home_ref[:, cut] + ref[...].astype(jnp.float32)).astype(jnp.bfloat16)


def total(home, first, second):
    return pl.pallas_call(
        total_kernel,
        in_specs=[VMEM_SPEC] * 3,
        out_specs=VMEM_SPEC,
        out_shape=jax.ShapeDtypeStruct((ROWS, D), jnp.bfloat16),
        compiler_params=pltpu.CompilerParams(vmem_limit_bytes=VMEM_LIMIT),
        cost_estimate=COST,
        name="total",
    )(*on_chip(home, first, second))


def body(
    tokens,
    attn_gain,
    w_query,
    w_key,
    w_value,
    w_attn_out,
    rel_bias,
    prefix_cache,
    lengths,
    prefix_map,
    mlp_gain,
    w_in,
    w_out,
):
    count_x = lax.axis_size("x")
    plane = lax.axis_index("z") * 2 + lax.axis_index("ylo")
    place = tuple(
        at.astype(jnp.int32).reshape(1) for at in (lax.axis_index("x"), plane, lax.axis_index("yhi"))
    )
    other_in = lax.ppermute(w_in, "core", SWAP)
    other_out = lax.ppermute(w_out, "core", SWAP)
    blocks, made = project(
        place, tokens, attn_gain, prefix_cache, rel_bias, lengths, prefix_map, w_query, w_key, w_value
    )
    got = lax.all_to_all(blocks, PLANE, 0, 0, tiled=True)
    mirrored = ("yhi", "ylo")
    up, down, far, same = spread(got, tokens, other_in, other_out)
    by = lambda d: [(i, (i + d) % count_x) for i in range(count_x)]
    opposite = lax.ppermute(far, "x", by(2))
    prev = lax.ppermute(up, "x", by(1))
    later = lax.ppermute(down, "x", by(-1))
    far_tokens = lax.ppermute(same, mirrored, MIRROR)
    *part, other_out, turned, other_turned = attend_own(
        place, rel_bias, got, made, w_in, other_in, other_out
    )
    mixed = attend_rest(place, rel_bias, prev, later, opposite, made, part, far_tokens)
    weights = (turned, other_turned, w_out, other_out)
    att = lax.all_to_all(mixed, ("yhi",) + PLANE, 0, 0, tiled=True)

    first, units = away(place[2], att, w_attn_out, far_tokens, mlp_gain, weights)
    first_back = lax.ppermute(first, mirrored, MIRROR)
    second = remainder(units, *weights[2:])
    second_back = lax.ppermute(second, mirrored, MIRROR)
    local = finish(place[2], att, w_attn_out, tokens, mlp_gain, weights, second)
    return total(local, first_back, second_back)


def solution(mesh):
    split = Mesh(mesh.devices.reshape(2, 2, 4, 4, 2), AXES)
    grp, req = ("yhi", "core"), REQ
    return jax.shard_map(
        body,
        mesh=split,
        in_specs=(
            P(grp + req, None),
            P(),
            P(),
            P(),
            P(),
            P(),
            P(),
            P(grp, req, None),
            P(grp, None),
            P(grp, None),
            P(),
            P(grp, None),
            P(grp, None),
        ),
        out_specs=P(grp + req, None),
        check_vma=False,
    )
```
